32 devices in a mesh: groups: 2 (over x), mp: 16 (over z, y, core).
Axes of the slice: x: 2, y: 2, z: 4, core: 2. Of those that a mesh axis runs over, the one named last changes fastest.
Arguments:
- hidden_in: bfloat16 [1536, 2560], P(('groups', 'mp')), parts along dimension 0, may hold values from -6 to 6
- ln_gain: float32 [2560], replicated, may hold values from 0.1 to 1.9
- w_qkv: bfloat16 [3, 2560, 2048], P(None, None, 'mp'), may hold values from -2 to 2
- w_out: bfloat16 [2048, 2560], P('mp'), may hold values from -0.125 to 0.125
- residue_index: int32 [1536], P('groups'), parts along dimension 0, may hold values from 0 to 1343, as said below
- w_map: bfloat16 [32, 128], replicated, may hold values from -1 to 1, as said below
- relpos_table: float32 [65, 128], replicated, may hold values from -0.75 to 0.75
- w_side: bfloat16 [2, 2560, 128], replicated, may hold values from -0.009765625 to 0.009765625
- tri_gain: float32 [2, 128], replicated, may hold values from 0.1 to 1.9
- w_tri: bfloat16 [5, 128, 128], replicated, may hold values from -0.5 to 0.5
- w_tri_out: bfloat16 [128, 128], replicated, may hold values from -0.5 to 0.5
Outputs:
- hidden_out: bfloat16 [1536, 2560], P(('groups', 'mp')), parts along dimension 0
- pair_out: bfloat16 [1536, 768, 128], P(('groups', 'mp')), parts along dimension 0
The draws below stay inside these ranges and needn't reach their ends.
There are 2 independent parts, one for each index of `groups`. The reference program is written for one: setup_inputs(seed, part) draws one part's arguments, and reference() takes and returns one part's arrays. A program takes and returns all parts, laid end to end along the dimension named above; an argument that names none is the same for every part. Nothing has to cross between parts.
Inputs may be any that keep to these rules, and one draw needn't show every extreme that they name: `w_map`: each column sums to zero over the 32 heads before rounding to bfloat16. `residue_index`: strictly increasing from 0; consecutive entries differ by 1 or by 25, exactly 24 of them by 25.
All inputs are finite; a program needn't handle non-finite values.
Results may differ from the reference program's by a relative error of at most 0.011.
Values may be sent and summed in bfloat16 or wider, within the bound.
A program may use at most 192 MiB of HBM per device.

```python
import jax
import jax.numpy as jnp
from jax import lax

D = 2560
HEADS = 32
HD = 64
C = 128
BINS = 65
L = 768


def draw_w_qkv(key, part):
    width = HEADS * HD
    base = jnp.clip(jax.random.normal(key, (3, D, width), jnp.float32), -6.0, 6.0) * D ** (-0.5)
    factors = jnp.array([1.25, 1.25, 1.0], jnp.float32)
    stacked = base * factors[:, None, None]
    return jnp.clip(stacked, -2.0, 2.0).astype(jnp.bfloat16)


def draw_w_map(key, part):
    basis = jnp.clip(jax.random.normal(key, (HEADS, C), jnp.float32), -4.0, 4.0)
    shifted = jnp.roll(basis, 1, axis=0)
    return ((basis - shifted) * 0.05).astype(jnp.bfloat16)


def draw_residue_index(key, part):
    jump_count = L // 32
    order = jax.random.permutation(key, L - 1)
    places = order[:jump_count] + 1
    flags = jnp.zeros((L,), jnp.int32).at[places].set(1)
    increments = jnp.where(flags == 1, 25, 1)
    increments = jnp.where(jnp.arange(L) == 0, 0, increments)
    return jnp.cumsum(increments).astype(jnp.int32)


def level_of(stream_key, shape, pieces, least, largest):
    def one(position, parts):
        draws = jax.random.uniform(jax.random.fold_in(jax.random.fold_in(stream_key, 6), position), (parts,), jnp.float32, least / len(pieces), largest / len(pieces))
        return jnp.repeat(jnp.exp(draws), shape[position] // parts).reshape((-1,) + (1,) * (len(shape) - position - 1))

    gain = one(*pieces[0])
    for cut in pieces[1:]:
        gain = gain * one(*cut)
    return gain


def scatter_about(rng, dims, scale, most, split=(), kind=jnp.bfloat16):
    result = jax.random.normal(rng, dims, jnp.float32) * scale
    if len(split) > 0:
        result = level_of(rng, dims, split, -0.22, 0.18) * result
    return jnp.clip(result, min=-most, max=most).astype(kind)


def setup_inputs(seed: int = 0, part: int = 0) -> dict:
    seeds = jax.random.split(jax.random.key(seed), 12)
    own_keys = jax.random.split(jax.random.fold_in(seeds[11], part), 12)
    hidden_in = scatter_about(own_keys[0], (L, D), 1.0, 6.0, ((0, 16),))
    ln_gain = jnp.clip(1.0 + 0.18 * jax.random.normal(seeds[1], (D,), jnp.float32), 0.1, 1.9)
    w_qkv = draw_w_qkv(jax.random.fold_in(seeds[11], 71), part)
    w_out = scatter_about(seeds[3], (HEADS * HD, D), (HEADS * HD) ** -0.5, 0.125, ((0, 16),))
    residue_index = draw_residue_index(jax.random.fold_in(jax.random.fold_in(seeds[11], part), 71), part)
    w_map = draw_w_map(jax.random.fold_in(seeds[11], 71), part)
    relpos_table = scatter_about(seeds[6], (BINS, C), 0.12, 0.75, (), jnp.float32)
    w_side = scatter_about(seeds[7], (2, D, C), (128 * D) ** -0.5, 0.009765625)
    tri_gain = jnp.clip(1.0 + 0.18 * jax.random.normal(seeds[8], (2, C), jnp.float32), 0.1, 1.9)
    w_tri = scatter_about(seeds[9], (5, C, C), C ** -0.5, 0.5)
    w_tri_out = scatter_about(seeds[10], (C, C), C ** -0.5, 0.5)
    return dict(hidden_in=hidden_in, ln_gain=ln_gain, w_qkv=w_qkv, w_out=w_out, residue_index=residue_index, w_map=w_map, relpos_table=relpos_table, w_side=w_side, tri_gain=tri_gain, w_tri=w_tri, w_tri_out=w_tri_out)


def layer_norm(tensor, gain_vec, norm_axis):
    center = lax.optimization_barrier(jnp.mean(tensor, axis=norm_axis, keepdims=True))
    centered = tensor - center
    variance = lax.optimization_barrier(jnp.mean(centered * centered, axis=norm_axis, keepdims=True))
    return centered * lax.rsqrt(variance + 1e-05) * gain_vec

def rotary_tables(length, width):
    inv_freq = 1.0 / 10000.0 ** (jnp.arange(0, width, 2, dtype=jnp.float32) / width)
    angles = jnp.arange(length, dtype=jnp.float32)[:, None] * inv_freq[None, :]
    angles = jnp.concatenate([angles, angles], axis=-1)
    return (jnp.cos(angles)[:, None, :], jnp.sin(angles)[:, None, :])

def rotate(tensor, cos_table, sin_table):
    middle = tensor.shape[-1] // 2
    turned = jnp.concatenate([-tensor[..., middle:], tensor[..., :middle]], axis=-1)
    return tensor * cos_table + turned * sin_table

def gated_edge(pair_normed, w_value, w_gate):
    value_part = jnp.einsum('ijc,cd->dij', pair_normed.astype(jnp.float32), w_value.astype(jnp.float32))
    gate_part = jnp.einsum('ijc,cd->dij', pair_normed.astype(jnp.float32), w_gate.astype(jnp.float32))
    return (jax.nn.sigmoid(gate_part) * value_part).astype(jnp.bfloat16)

def reference(hidden_in, ln_gain, w_qkv, w_out, residue_index, w_map, relpos_table, w_side, tri_gain, w_tri, w_tri_out):
    length = hidden_in.shape[0]
    normed = layer_norm(hidden_in.astype(jnp.float32), ln_gain, -1).astype(jnp.bfloat16)
    projected = jnp.einsum('rd,tdh->trh', normed.astype(jnp.float32), w_qkv.astype(jnp.float32))
    projected = projected.reshape(3, length, HEADS, HD)
    cos_table, sin_table = rotary_tables(length, HD)
    queries = rotate(projected[0] * HD ** (-0.5), cos_table, sin_table).astype(jnp.bfloat16)
    key_rows = rotate(projected[1], cos_table, sin_table).astype(jnp.bfloat16)
    value_rows = projected[2].astype(jnp.bfloat16)
    scores = jnp.einsum('qhd,khd->hqk', queries.astype(jnp.float32), key_rows.astype(jnp.float32))
    attn_probs = jax.nn.softmax(scores, axis=-1).astype(jnp.bfloat16)
    attended = jnp.einsum('hqk,khd->qhd', attn_probs.astype(jnp.float32), value_rows.astype(jnp.float32))
    attended = attended.astype(jnp.bfloat16).reshape(length, HEADS * HD)
    hidden_out = (hidden_in.astype(jnp.float32) + jnp.dot(attended, w_out, preferred_element_type=jnp.float32)).astype(jnp.bfloat16)
    pair_sum = length * jnp.einsum('hij,hc->ijc', attn_probs.astype(jnp.float32), w_map.astype(jnp.float32))
    reach = (BINS - 1) // 2
    rel_bins = jnp.clip(residue_index[None, :] - residue_index[:, None], -reach, reach) + reach
    pair_sum = pair_sum + relpos_table[rel_bins.astype(jnp.int32)]
    left_terms = jnp.dot(hidden_out, w_side[0], preferred_element_type=jnp.float32).astype(jnp.bfloat16)
    right_terms = jnp.dot(hidden_out, w_side[1], preferred_element_type=jnp.float32).astype(jnp.bfloat16)
    pair_sum = pair_sum + left_terms[:, None, :].astype(jnp.float32) + right_terms[None, :, :].astype(jnp.float32)
    pair_normed = layer_norm(pair_sum, tri_gain[0], -1).astype(jnp.bfloat16)
    left_edge = gated_edge(pair_normed, w_tri[0], w_tri[1])
    right_edge = gated_edge(pair_normed, w_tri[2], w_tri[3])
    out_gate = jax.nn.sigmoid(jnp.einsum('ijc,cd->ijd', pair_normed.astype(jnp.float32), w_tri[4].astype(jnp.float32)))
    products = jnp.einsum('cik,cjk->cij', left_edge.astype(jnp.float32), right_edge.astype(jnp.float32)).astype(jnp.bfloat16)
    prod_normed = layer_norm(products.astype(jnp.float32), tri_gain[1][:, None, None], 0).astype(jnp.bfloat16)
    projected_out = jnp.einsum('cij,cd->ijd', prod_normed.astype(jnp.float32), w_tri_out.astype(jnp.float32))
    pair_out = (pair_sum + out_gate * projected_out).astype(jnp.bfloat16)
    return (hidden_out, pair_out)
```

```python
import functools

import jax
import jax.numpy as jnp
from jax import lax
from jax.experimental import pallas as pl
from jax.experimental.pallas import tpu as pltpu
from jax.sharding import PartitionSpec as P

HD = 64
BINS = 65
BIN_ROWS = 80
LANES = 128
CHUNKS = 3
PAD = 8
VMEM_BYTES = 60 * 1024 * 1024
MESH = pl.DeviceIdType.MESH
EXACT = lax.Precision.HIGHEST


def layer_norm(tensor, gain_vec, norm_axis):
    center = jnp.mean(tensor, axis=norm_axis, keepdims=True)
    centered = tensor - center
    variance = jnp.mean(centered * centered, axis=norm_axis, keepdims=True)
    return centered * lax.rsqrt(variance + 1e-05) * gain_vec


def rotary_tables(length, width):
    inv_freq = 1.0 / 10000.0 ** (jnp.arange(0, width, 2, dtype=jnp.float32) / width)
    angles = jnp.arange(length, dtype=jnp.float32)[:, None] * inv_freq[None, :]
    angles = jnp.concatenate([angles, angles], axis=-1)
    return (jnp.cos(angles)[:, None, :], jnp.sin(angles)[:, None, :])


def rotate(tensor, cos_table, sin_table):
    middle = tensor.shape[-1] // 2
    turned = jnp.concatenate([-tensor[..., middle:], tensor[..., :middle]], axis=-1)
    return tensor * cos_table + turned * sin_table


def two_terms(value):
    high = lax.reduce_precision(value, 8, 7)
    return high.astype(jnp.bfloat16), (value - high).astype(jnp.bfloat16)


def maps_kernel(q_ref, k_ref, out_ref, scratch):
    heads, rows, _ = q_ref.shape
    blocks = scratch.shape[0]

    def one_head(h, carry):
        scores = jnp.dot(q_ref[h], k_ref[h], preferred_element_type=jnp.float32)
        top = jnp.max(scores, axis=-1, keepdims=True)
        powers = jnp.exp(scores - top)
        probs = powers / jnp.sum(powers, axis=-1, keepdims=True)
        start = pl.multiple_of(h * (rows + PAD), 8)
        for n in range(blocks):
            scratch[n, pl.ds(start, rows), :] = probs[:, n * LANES : (n + 1) * LANES]
        return carry

    lax.fori_loop(0, heads, one_head, 0, unroll=8)

    def one_row(j, carry):
        for n in range(blocks):
            rows_of = scratch[n, pl.ds(j, heads, stride=rows + PAD), :]
            out_ref[j, :, n * LANES : (n + 1) * LANES] = rows_of.astype(jnp.bfloat16)
        return carry

    lax.fori_loop(0, rows, one_row, 0, unroll=8)


def attention_maps(queries, keys, block):
    heads, rows, width = queries.shape
    length = keys.shape[2]
    return pl.pallas_call(
        maps_kernel,
        out_shape=jax.ShapeDtypeStruct((rows, heads, length), jnp.bfloat16),
        grid=(rows // block,),
        in_specs=[
            pl.BlockSpec((heads, block, width), lambda b: (0, b, 0)),
            pl.BlockSpec((heads, width, length), lambda b: (0, 0, 0)),
        ],
        out_specs=pl.BlockSpec((block, heads, length), lambda b: (b, 0, 0)),
        scratch_shapes=[pltpu.VMEM((length // LANES, heads * (block + PAD), LANES), jnp.float32)],
        compiler_params=pltpu.CompilerParams(vmem_limit_bytes=VMEM_BYTES),
        cost_estimate=pl.CostEstimate(
            flops=2 * heads * rows * length * width * 4,
            bytes_accessed=2 * heads * rows * length,
            transcendentals=heads * rows * length,
        ),
        name="attention_maps",
    )(queries, keys)


def sides_kernel(count, part_ref, own_ref, out_ref, landed, mine, send_a, recv_a, send_b, recv_b):
    me = lax.axis_index("mp")

    def each(step):
        def run(d, carry):
            step(d)
            return carry

        lax.fori_loop(1, count, run, 0)

    barrier = pltpu.get_barrier_semaphore()
    each(
        lambda d: pl.semaphore_signal(
            barrier, inc=1, device_id={"mp": lax.rem(me + d, count)}, device_id_type=MESH
        )
    )
    pl.semaphore_wait(barrier, count - 1)

    def scatter(d):
        target = lax.rem(me + d, count)
        return pltpu.make_async_remote_copy(
            src_ref=part_ref.at[target],
            dst_ref=landed.at[d],
            send_sem=send_a.at[d],
            recv_sem=recv_a.at[d],
            device_id={"mp": target},
            device_id_type=MESH,
        )

    def spread(d):
        return pltpu.make_async_remote_copy(
            src_ref=mine,
            dst_ref=out_ref.at[me],
            send_sem=send_b.at[d],
            recv_sem=recv_b.at[d],
            device_id={"mp": lax.rem(me + d, count)},
            device_id_type=MESH,
        )

    each(lambda d: scatter(d).start())

    def add(d, total):
        scatter(d).wait_recv()
        return total + landed[d].astype(jnp.float32)

    total = lax.fori_loop(1, count, add, own_ref[...] + part_ref[me].astype(jnp.float32))
    mine[...] = total.astype(jnp.bfloat16)
    out_ref[me] = total.astype(jnp.bfloat16)
    each(lambda d: spread(d).start())
    each(lambda d: spread(d).wait_recv())
    each(lambda d: scatter(d).wait_send())
    each(lambda d: spread(d).wait_send())


def exchange_sides(parts, own):
    count, rows, width = parts.shape
    sems = pltpu.SemaphoreType.DMA((count,))
    return pl.pallas_call(
        functools.partial(sides_kernel, count),
        out_shape=jax.ShapeDtypeStruct(parts.shape, jnp.bfloat16),
        in_specs=[pl.BlockSpec(memory_space=pltpu.VMEM)] * 2,
        out_specs=pl.BlockSpec(memory_space=pltpu.VMEM),
        scratch_shapes=[
            pltpu.VMEM(parts.shape, jnp.bfloat16),
            pltpu.VMEM((rows, width), jnp.bfloat16),
            sems,
            sems,
            sems,
            sems,
        ],
        compiler_params=pltpu.CompilerParams(collective_id=0, has_side_effects=True),
        cost_estimate=pl.CostEstimate(
            flops=count * rows * width, bytes_accessed=4 * count * rows * width, transcendentals=0
        ),
        name="exchange_sides",
    )(parts, own)


def places_of(rows, width):
    places = lax.broadcasted_iota(jnp.int32, (rows, width), 0)
    return places.astype(jnp.float32).astype(jnp.bfloat16)


def hot_rows(places, index):
    index = index.astype(jnp.float32).astype(jnp.bfloat16)
    return jnp.where(places == index, jnp.ones((), jnp.bfloat16), jnp.zeros((), jnp.bfloat16))


def edges_kernel(
    own, row_index, maps_ref, left_ref, fold_ref, mix_ref, low_ref, right_ref, cols_ref, *rest
):
    scratch, full_ref = rest[-2], rest[-1]
    block, heads, length = maps_ref.shape
    channels = right_ref.shape[0]
    eye_rows = mix_ref.shape[1] - channels - heads - BIN_ROWS
    pitch = channels + 1
    width = 2 * LANES
    reach = (BINS - 1) // 2
    first = pl.program_id(0) * block

    lefts = jnp.concatenate(
        [left_ref[...], jnp.zeros((LANES - block, channels), jnp.bfloat16)], axis=0
    )
    folded = lax.dot_general(
        fold_ref[...], lefts, (((1,), (1,)), ((), ())), preferred_element_type=jnp.float32
    )
    full_ref[:, :LANES] = (folded + mix_ref[:, :LANES].astype(jnp.float32)).astype(jnp.bfloat16)
    full_ref[:, LANES:] = mix_ref[:, LANES:]

    def one_row(j, carry):
        here = row_index[first + j]
        eye = hot_rows(places_of(eye_rows, width), jnp.broadcast_to(j, (1, width)))
        for n in range(length // width):
            cols = slice(n * width, (n + 1) * width)
            bins = jnp.clip(cols_ref[:, cols] - here, -reach, reach) + reach
            hot = hot_rows(places_of(BIN_ROWS, width), bins)
            probs = maps_ref[j, :, cols]
            terms = jnp.concatenate([eye, probs, hot, right_ref[:, cols]], axis=0)
            mixed = jnp.dot(full_ref[...], terms, preferred_element_type=jnp.float32)
            centered = mixed[:channels]
            if own:
                pair = centered + jnp.dot(
                    low_ref[...],
                    jnp.concatenate([eye, probs, hot], axis=0),
                    preferred_element_type=jnp.float32,
                )
                rest[2][j, :, cols] = pair
                centered = pair - jnp.sum(pair, axis=0, keepdims=True) * (1.0 / channels)
            variance = jnp.sum(centered * centered, axis=0, keepdims=True) * (1.0 / channels)
            scale = lax.rsqrt(variance + 1e-05)
            value = mixed[channels : 2 * channels] * scale
            edge = value + value * jnp.tanh(mixed[2 * channels : 3 * channels] * scale)
            start = j * pitch
            for m in range(width // LANES):
                scratch[n * (width // LANES) + m, pl.ds(start, channels), :] = edge[
                    :, m * LANES : (m + 1) * LANES
                ]
            if own:
                gate = 0.5 + 0.5 * jnp.tanh(mixed[3 * channels :] * scale)
                rest[3][j, :, cols] = gate.astype(jnp.bfloat16)
        return carry

    lax.fori_loop(0, block, one_row, 0, unroll=min(16, block))
    half = channels // 2

    def one_channel(c, carry):
        for n in range(length // LANES):
            for side in range(2):
                rows_of = scratch[n, pl.ds(c + side * half, block, stride=pitch), :]
                rest[side][c, :, n * LANES : (n + 1) * LANES] = rows_of.astype(jnp.bfloat16)
        return carry

    lax.fori_loop(0, half, one_channel, 0, unroll=16)


def edges(own, row_index, maps, left, fold, mix, low, right, cols, block, skip=0, rows=None):
    _, heads, length = maps.shape
    rows = maps.shape[0] if rows is None else rows
    channels = right.shape[0]
    half = channels // 2
    out_shape = [jax.ShapeDtypeStruct((half, rows, length), jnp.bfloat16)] * 2
    out_specs = [pl.BlockSpec((half, block, length), lambda b, s: (0, b, 0))] * 2
    if own:
        out_shape += [
            jax.ShapeDtypeStruct((rows, channels, length), jnp.float32),
            jax.ShapeDtypeStruct((rows, channels, length), jnp.bfloat16),
        ]
        out_specs += [pl.BlockSpec((block, channels, length), lambda b, s: (b, 0, 0))] * 2
    first = skip // block
    whole = [pl.BlockSpec(a.shape, lambda b, s: (0, 0)) for a in (fold, mix, low, right, cols)]
    return pl.pallas_call(
        functools.partial(edges_kernel, own),
        out_shape=out_shape,
        grid_spec=pltpu.PrefetchScalarGridSpec(
            num_scalar_prefetch=1,
            grid=(rows // block,),
            in_specs=[
                pl.BlockSpec((block, heads, length), lambda b, s: (b + first, 0, 0)),
                pl.BlockSpec((block, channels), lambda b, s: (b, 0)),
            ]
            + whole,
            out_specs=out_specs,
            scratch_shapes=[
                pltpu.VMEM((length // LANES, block * (channels + 1) + 7, LANES), jnp.float32),
                pltpu.VMEM(mix.shape, jnp.bfloat16),
            ],
        ),
        compiler_params=pltpu.CompilerParams(vmem_limit_bytes=VMEM_BYTES),
        cost_estimate=pl.CostEstimate(
            flops=2 * rows * length * channels * 800,
            bytes_accessed=2 * rows * length * channels,
            transcendentals=rows * length * channels,
        ),
        name="own_edges" if own else "right_edges",
    )(row_index, maps, left, fold, mix, low, right, cols)


def products_kernel(keep_ref, arrive_ref, *refs):
    parts, (mine_ref, theirs_ref) = refs[:-2], refs[-2:]
    count, rows, _ = keep_ref.shape
    for c in range(count):
        lefts = jnp.concatenate([keep_ref[c], arrive_ref[c]], axis=0)
        for p, part in enumerate(parts):
            out = lax.dot_general(
                lefts, part[c], (((1,), (1,)), ((), ())), preferred_element_type=jnp.float32
            ).astype(jnp.bfloat16)
            mine_ref[p, c] = out[:rows]
            theirs_ref[p, c] = out[rows:]


def edge_products(keep, arrive, parts):
    half, rows, length = keep.shape
    each = parts[0].shape[1]
    count = 8 if half % 8 == 0 else 1
    out = jax.ShapeDtypeStruct((len(parts), half, rows, each), jnp.bfloat16)
    return pl.pallas_call(
        products_kernel,
        out_shape=[out] * 2,
        grid=(half // count,),
        in_specs=[pl.BlockSpec((count, rows, length), lambda b: (b, 0, 0))] * 2
        + [pl.BlockSpec((count, each, length), lambda b: (b, 0, 0))] * len(parts),
        out_specs=[pl.BlockSpec((len(parts), count, rows, each), lambda b: (0, b, 0, 0))] * 2,
        compiler_params=pltpu.CompilerParams(vmem_limit_bytes=VMEM_BYTES),
        cost_estimate=pl.CostEstimate(
            flops=4 * half * rows * len(parts) * each * length,
            bytes_accessed=2 * half * len(parts) * each * length,
            transcendentals=0,
        ),
        name="edge_products",
    )(keep, arrive, *parts)


def final_kernel(core, mine_ref, theirs_ref, pair_ref, gate_ref, gain_ref, w_ref, out_ref, scratch):
    half, block, width = mine_ref.shape[1:]
    for n, ref in enumerate((mine_ref, theirs_ref)):

        def one_channel(c, carry):
            start = pl.multiple_of(c * (block + PAD), 8)
            scratch[n, pl.ds(start, block), :] = ref[0, c].astype(jnp.float32)
            return carry

        lax.fori_loop(0, half, one_channel, 0, unroll=8)

    def one_row(i, carry):
        products = jnp.concatenate(
            [scratch[n, pl.ds(i, half, stride=block + PAD), :] for n in range(2)], axis=0
        )
        center = jnp.mean(products, axis=0, keepdims=True)
        centered = products - center
        variance = jnp.mean(centered * centered, axis=0, keepdims=True)
        normed = (centered * lax.rsqrt(variance + 1e-05) * gain_ref[...]).astype(jnp.bfloat16)
        projected = jnp.dot(w_ref[...], normed, preferred_element_type=jnp.float32)
        total = pair_ref[i] + gate_ref[i].astype(jnp.float32) * projected
        out_ref[i] = total.T.astype(jnp.bfloat16)
        return carry

    lax.fori_loop(0, block, one_row, 0, unroll=16)


def finish(core, mine, theirs, pair, gate, gain, weights, block):
    pieces, half, rows, width = mine.shape
    _, channels, length = pair.shape
    each = pieces // 2

    def column(u, core):
        side = u // each
        return (side + core[0] - 2 * side * core[0]) * each + u % each

    return pl.pallas_call(
        final_kernel,
        out_shape=jax.ShapeDtypeStruct((rows, length, channels), jnp.bfloat16),
        grid_spec=pltpu.PrefetchScalarGridSpec(
            num_scalar_prefetch=1,
            grid=(rows // block, pieces),
            in_specs=[
                pl.BlockSpec((1, half, block, width), lambda b, u, s: (u, 0, b, 0)),
                pl.BlockSpec(
                    (1, half, block, width), lambda b, u, s: ((u + each) % pieces, 0, b, 0)
                ),
                pl.BlockSpec((block, channels, width), lambda b, u, s: (b, 0, column(u, s))),
                pl.BlockSpec((block, channels, width), lambda b, u, s: (b, 0, column(u, s))),
                pl.BlockSpec(gain.shape, lambda b, u, s: (0, 0)),
                pl.BlockSpec(weights.shape, lambda b, u, s: (0, 0)),
            ],
            out_specs=pl.BlockSpec((block, width, channels), lambda b, u, s: (b, column(u, s), 0)),
            scratch_shapes=[pltpu.VMEM((2, half * (block + PAD), width), jnp.float32)],
        ),
        compiler_params=pltpu.CompilerParams(vmem_limit_bytes=VMEM_BYTES),
        name="finish",
    )(core, mine, theirs, pair, gate, gain, weights)


def per_device(
    hidden_in,
    ln_gain,
    w_qkv,
    w_out,
    residue_index,
    w_map,
    relpos_table,
    w_side,
    tri_gain,
    w_tri,
    w_tri_out,
):
    local_rows = hidden_in.shape[0]
    devices_mp = lax.axis_size("mp")
    me = lax.axis_index("mp")
    core = lax.rem(me, 2)
    length = local_rows * devices_mp
    local_heads = w_qkv.shape[2] // HD
    heads, channels = w_map.shape
    swap = [(d, d ^ 1) for d in range(devices_mp)]
    normed = layer_norm(hidden_in.astype(jnp.float32), ln_gain, -1).astype(jnp.bfloat16)
    projected = jnp.einsum(
        "rd,tdh->trh",
        lax.all_gather(normed, "mp", axis=0, tiled=True),
        w_qkv,
        preferred_element_type=jnp.float32,
    )
    projected = projected.reshape(3, length, local_heads, HD)
    cos_table, sin_table = rotary_tables(length, HD)
    queries = rotate(projected[0] * HD ** (-0.5), cos_table, sin_table).astype(jnp.bfloat16)
    key_rows = rotate(projected[1], cos_table, sin_table).astype(jnp.bfloat16)
    value_rows = projected[2].astype(jnp.bfloat16)
    both = jnp.stack([queries.reshape(length, -1).T, key_rows.reshape(length, -1).T])
    gathered = lax.all_gather(both, "mp", axis=1, tiled=True)

    scores = jnp.einsum("qhd,khd->hqk", queries, key_rows, preferred_element_type=jnp.float32)
    attn_probs = jax.nn.softmax(scores, axis=-1).astype(jnp.bfloat16)
    attended = jnp.einsum(
        "hqk,khd->qhd", attn_probs, value_rows, preferred_element_type=jnp.float32
    )
    attended = attended.astype(jnp.bfloat16).reshape(length, local_heads * HD)
    side_parts = jnp.einsum(
        "rh,hsc->rsc",
        attended,
        jnp.einsum("hd,sdc->hsc", w_out, w_side, preferred_element_type=jnp.float32).astype(
            jnp.bfloat16
        ),
        preferred_element_type=jnp.float32,
    ).astype(jnp.bfloat16)
    own_sides = jnp.einsum("rd,sdc->rsc", hidden_in, w_side, preferred_element_type=jnp.float32)
    all_sides = exchange_sides(
        side_parts.reshape(devices_mp, local_rows, 2 * channels),
        own_sides.reshape(local_rows, 2 * channels),
    )
    partial, all_sides, gathered = lax.optimization_barrier(
        (
            jnp.dot(attended, w_out, preferred_element_type=jnp.float32).astype(jnp.bfloat16),
            all_sides,
            gathered,
        )
    )
    all_keys = gathered[1].reshape(heads, HD, length)
    all_queries = gathered[0].reshape(heads, HD, length).transpose(0, 2, 1)
    mixed = lax.psum_scatter(partial, "mp", scatter_dimension=0, tiled=True)

    half_rows = length // 2
    row_start = me * local_rows
    half_start = core * half_rows
    own_maps = attention_maps(
        lax.dynamic_slice_in_dim(all_queries, row_start, local_rows, 1), all_keys, local_rows
    )
    map_block = 64 if half_rows % 64 == 0 else local_rows
    half_maps = attention_maps(
        lax.dynamic_slice_in_dim(all_queries, half_start, half_rows, 1), all_keys, map_block
    )

    all_sides = all_sides.reshape(length, 2 * channels)
    left_rows = all_sides[:, :channels]
    right = all_sides[:, channels:].T

    map_high, map_low = two_terms(w_map.astype(jnp.float32) * length)
    bin_high, bin_low = two_terms(relpos_table)
    bin_pad = ((0, BIN_ROWS - relpos_table.shape[0]), (0, 0))
    map_full = w_map.astype(jnp.float32) * length
    turn = -core * (channels // 2)
    halved = 0.5 * w_tri.astype(jnp.float32) * tri_gain[0][None, :, None]
    identity = jnp.eye(channels, dtype=jnp.float32)
    center = identity - 1.0 / channels

    def gated(p, shift):
        return jnp.dot(jnp.roll(halved[p].T, shift, axis=0), center, precision=EXACT)

    def mixing(fold, block):
        eye_rows = -(-block // 16) * 16
        parts = [
            jnp.zeros((eye_rows, channels), jnp.float32),
            map_full,
            jnp.pad(relpos_table, bin_pad),
            identity,
        ]
        mix = jnp.dot(fold, jnp.concatenate(parts, axis=0).T, precision=EXACT)
        return fold.astype(jnp.bfloat16), mix

    def low_terms(block):
        eye_rows = -(-block // 16) * 16
        parts = [jnp.zeros((eye_rows, channels), jnp.bfloat16), map_low, jnp.pad(bin_low, bin_pad)]
        return jnp.concatenate(parts, axis=0).T

    cols = residue_index[None, :]

    block = 16 if local_rows % 16 == 0 else local_rows
    half_left = lax.dynamic_slice_in_dim(left_rows, half_start, half_rows, 0)
    half_index = lax.dynamic_slice_in_dim(residue_index, half_start, half_rows, 0)
    each = half_rows // CHUNKS
    r_block = 16 if each % 16 == 0 else each
    right_fold, right_mix = mixing(
        jnp.concatenate([center, gated(2, turn), gated(3, turn)], axis=0), r_block
    )
    right_mix = right_mix.astype(jnp.bfloat16)
    left_fold, left_mix = mixing(
        jnp.concatenate([identity, gated(0, turn), gated(1, turn), gated(4, 0)], axis=0), block
    )
    left_mix = lax.reduce_precision(left_mix, 8, 7).astype(jnp.bfloat16)
    own_low = low_terms(block)
    right_low = low_terms(r_block)
    kept, arriving = [], []
    for n in range(CHUNKS):
        part = slice(n * each, (n + 1) * each)
        keep, send = edges(
            False,
            half_index[part],
            half_maps,
            half_left[part],
            right_fold,
            right_mix,
            right_low,
            right,
            cols,
            r_block,
            n * each,
            each,
        )
        kept.append(keep)
        arriving.append(lax.ppermute(send, "mp", swap))
    left_keep, left_send, pair, gate = edges(
        True,
        lax.dynamic_slice_in_dim(residue_index, row_start, local_rows, 0),
        own_maps,
        lax.dynamic_slice_in_dim(left_rows, row_start, local_rows, 0),
        left_fold,
        left_mix,
        own_low,
        right,
        cols,
        block,
    )
    left_arrive = lax.ppermute(left_send, "mp", swap)
    mine_kept, theirs_kept = edge_products(left_keep, left_arrive, kept)
    theirs_kept = lax.ppermute(theirs_kept, "mp", swap)
    mine_other, theirs_other = edge_products(left_keep, left_arrive, arriving)
    theirs_other = lax.ppermute(theirs_other, "mp", swap)
    pair_out = finish(
        core[None],
        jnp.concatenate([mine_kept, mine_other]),
        jnp.concatenate([theirs_kept, theirs_other]),
        pair,
        gate,
        jnp.broadcast_to(jnp.roll(tri_gain[1], turn)[:, None], (channels, each)),
        jnp.roll(w_tri_out, turn, axis=0).T,
        block,
    )
    hidden_out = (hidden_in.astype(jnp.float32) + mixed.astype(jnp.float32)).astype(jnp.bfloat16)
    return (hidden_out, pair_out)


def solution(mesh):
    placed = (
        P(("groups", "mp"), None),
        P(),
        P(None, None, "mp"),
        P("mp", None),
        P("groups"),
        P(),
        P(),
        P(),
        P(),
        P(),
        P(),
    )
    return jax.shard_map(
        per_device,
        mesh=mesh,
        in_specs=placed,
        out_specs=(P(("groups", "mp"), None), P(("groups", "mp"), None, None)),
        check_vma=False,
    )
```

```python
import functools

import jax
import jax.numpy as jnp
from jax import lax
from jax.experimental import pallas as pl
from jax.experimental.pallas import tpu as pltpu
from jax.sharding import PartitionSpec as P

HD = 64
BINS = 65
BIN_ROWS = 80
LANES = 128
CHUNKS = 3
VMEM_BYTES = 60 * 1024 * 1024
MESH = pl.DeviceIdType.MESH
EXACT = lax.Precision.HIGHEST


def layer_norm(tensor, gain_vec, norm_axis):
    center = jnp.mean(tensor, axis=norm_axis, keepdims=True)
    centered = tensor - center
    variance = jnp.mean(centered * centered, axis=norm_axis, keepdims=True)
    return centered * lax.rsqrt(variance + 1e-05) * gain_vec


def rotary_tables(length, width):
    inv_freq = 1.0 / 10000.0 ** (jnp.arange(0, width, 2, dtype=jnp.float32) / width)
    angles = jnp.arange(length, dtype=jnp.float32)[:, None] * inv_freq[None, :]
    angles = jnp.concatenate([angles, angles], axis=-1)
    return (jnp.cos(angles)[:, None, :], jnp.sin(angles)[:, None, :])


def rotate(tensor, cos_table, sin_table):
    middle = tensor.shape[-1] // 2
    turned = jnp.concatenate([-tensor[..., middle:], tensor[..., :middle]], axis=-1)
    return tensor * cos_table + turned * sin_table


def two_terms(value):
    high = lax.reduce_precision(value, 8, 7)
    return high.astype(jnp.bfloat16), (value - high).astype(jnp.bfloat16)


def maps_kernel(q_ref, k_ref, out_ref, scratch):
    heads, rows, _ = q_ref.shape
    blocks = scratch.shape[0]

    def one_head(h, carry):
        scores = jnp.dot(q_ref[h], k_ref[h], preferred_element_type=jnp.float32)
        top = jnp.max(scores, axis=-1, keepdims=True)
        powers = jnp.exp(scores - top)
        probs = powers / jnp.sum(powers, axis=-1, keepdims=True)
        for n in range(blocks):
            scratch[n, pl.ds(h * (rows + 1), rows), :] = probs[:, n * LANES : (n + 1) * LANES]
        return carry

    lax.fori_loop(0, heads, one_head, 0, unroll=8)

    def one_row(j, carry):
        for n in range(blocks):
            rows_of = scratch[n, pl.ds(j, heads, stride=rows + 1), :]
            out_ref[j, :, n * LANES : (n + 1) * LANES] = rows_of.astype(jnp.bfloat16)
        return carry

    lax.fori_loop(0, rows, one_row, 0, unroll=8)


def attention_maps(queries, keys, block):
    heads, rows, width = queries.shape
    length = keys.shape[2]
    return pl.pallas_call(
        maps_kernel,
        out_shape=jax.ShapeDtypeStruct((rows, heads, length), jnp.bfloat16),
        grid=(rows // block,),
        in_specs=[
            pl.BlockSpec((heads, block, width), lambda b: (0, b, 0)),
            pl.BlockSpec((heads, width, length), lambda b: (0, 0, 0)),
        ],
        out_specs=pl.BlockSpec((block, heads, length), lambda b: (b, 0, 0)),
        scratch_shapes=[pltpu.VMEM((length // LANES, heads * (block + 1) + 7, LANES), jnp.float32)],
        compiler_params=pltpu.CompilerParams(vmem_limit_bytes=VMEM_BYTES),
        cost_estimate=pl.CostEstimate(
            flops=2 * heads * rows * length * width * 4,
            bytes_accessed=2 * heads * rows * length,
            transcendentals=heads * rows * length,
        ),
        name="attention_maps",
    )(queries, keys)


def sides_kernel(
    count, part_ref, own_ref, att_ref, out_ref, rows_ref, landed, mine, *sems
):
    send_a, recv_a, send_b, recv_b, send_c, recv_c = sems
    me = lax.axis_index("mp")

    def each(step):
        def run(d, carry):
            step(d)
            return carry

        lax.fori_loop(1, count, run, 0)

    barrier = pltpu.get_barrier_semaphore()
    each(
        lambda d: pl.semaphore_signal(
            barrier, inc=1, device_id={"mp": lax.rem(me + d, count)}, device_id_type=MESH
        )
    )
    pl.semaphore_wait(barrier, count - 1)

    def scatter(d):
        target = lax.rem(me + d, count)
        return pltpu.make_async_remote_copy(
            src_ref=part_ref.at[target],
            dst_ref=landed.at[d],
            send_sem=send_a.at[d],
            recv_sem=recv_a.at[d],
            device_id={"mp": target},
            device_id_type=MESH,
        )

    def carry_rows(d):
        target = lax.rem(me + d, count)
        return pltpu.make_async_remote_copy(
            src_ref=att_ref.at[target],
            dst_ref=rows_ref.at[me],
            send_sem=send_c.at[d],
            recv_sem=recv_c.at[d],
            device_id={"mp": target},
            device_id_type=MESH,
        )

    def spread(d):
        return pltpu.make_async_remote_copy(
            src_ref=mine,
            dst_ref=out_ref.at[me],
            send_sem=send_b.at[d],
            recv_sem=recv_b.at[d],
            device_id={"mp": lax.rem(me + d, count)},
            device_id_type=MESH,
        )

    each(lambda d: scatter(d).start())

    def add(d, total):
        scatter(d).wait_recv()
        return total + landed[d].astype(jnp.float32)

    total = lax.fori_loop(1, count, add, own_ref[...] + part_ref[me].astype(jnp.float32))
    mine[...] = total.astype(jnp.bfloat16)
    out_ref[me] = total.astype(jnp.bfloat16)
    each(lambda d: spread(d).start())
    rows_ref[me] = att_ref[me]
    each(lambda d: carry_rows(d).start())
    each(lambda d: spread(d).wait_recv())
    each(lambda d: carry_rows(d).wait_recv())
    each(lambda d: scatter(d).wait_send())
    each(lambda d: spread(d).wait_send())
    each(lambda d: carry_rows(d).wait_send())


def exchange_sides(parts, own, attended):
    count, rows, width = parts.shape
    sems = pltpu.SemaphoreType.DMA((count,))
    return pl.pallas_call(
        functools.partial(sides_kernel, count),
        out_shape=[jax.ShapeDtypeStruct(a.shape, jnp.bfloat16) for a in (parts, attended)],
        in_specs=[pl.BlockSpec(memory_space=pltpu.VMEM)] * 3,
        out_specs=[pl.BlockSpec(memory_space=pltpu.VMEM)] * 2,
        scratch_shapes=[
            pltpu.VMEM(parts.shape, jnp.bfloat16),
            pltpu.VMEM((rows, width), jnp.bfloat16),
        ]
        + [sems] * 6,
        compiler_params=pltpu.CompilerParams(collective_id=0, has_side_effects=True),
        cost_estimate=pl.CostEstimate(
            flops=count * rows * width, bytes_accessed=4 * count * rows * width, transcendentals=0
        ),
        name="exchange_sides",
    )(parts, own, attended)


def places_of(rows, width):
    places = lax.broadcasted_iota(jnp.int32, (rows, width), 0)
    return places.astype(jnp.float32).astype(jnp.bfloat16)


def hot_rows(places, index):
    index = index.astype(jnp.float32).astype(jnp.bfloat16)
    return jnp.where(places == index, jnp.ones((), jnp.bfloat16), jnp.zeros((), jnp.bfloat16))


def edges_kernel(
    own, row_index, maps_ref, left_ref, fold_ref, mix_ref, low_ref, right_ref, cols_ref, *rest
):
    scratch, full_ref = rest[-2], rest[-1]
    block, heads, length = maps_ref.shape
    channels = right_ref.shape[0]
    eye_rows = mix_ref.shape[1] - channels - heads - BIN_ROWS
    pitch = channels + 1
    width = 2 * LANES
    reach = (BINS - 1) // 2
    first = pl.program_id(0) * block

    lefts = jnp.concatenate(
        [left_ref[...], jnp.zeros((LANES - block, channels), jnp.bfloat16)], axis=0
    )
    folded = lax.dot_general(
        fold_ref[...], lefts, (((1,), (1,)), ((), ())), preferred_element_type=jnp.float32
    )
    full_ref[:, :LANES] = (folded + mix_ref[:, :LANES].astype(jnp.float32)).astype(jnp.bfloat16)
    full_ref[:, LANES:] = mix_ref[:, LANES:]

    def one_row(j, carry):
        here = row_index[first + j]
        eye = hot_rows(places_of(eye_rows, width), jnp.broadcast_to(j, (1, width)))
        for n in range(length // width):
            cols = slice(n * width, (n + 1) * width)
            bins = jnp.clip(cols_ref[:, cols] - here, -reach, reach) + reach
            hot = hot_rows(places_of(BIN_ROWS, width), bins)
            probs = maps_ref[j, :, cols]
            terms = jnp.concatenate([eye, probs, hot, right_ref[:, cols]], axis=0)
            mixed = jnp.dot(
                full_ref[: 3 * channels], terms, preferred_element_type=jnp.float32
            )
            centered = mixed[:channels]
            if own:
                pair = centered + jnp.dot(
                    low_ref[...],
                    jnp.concatenate([eye, probs, hot], axis=0),
                    preferred_element_type=jnp.float32,
                )
                rest[2][j, :, cols] = pair.astype(jnp.bfloat16)
                centered = pair - jnp.sum(pair, axis=0, keepdims=True) * (1.0 / channels)
            variance = jnp.sum(centered * centered, axis=0, keepdims=True) * (1.0 / channels)
            scale = lax.rsqrt(variance + 1e-05)
            value = mixed[channels : 2 * channels] * scale
            edge = value + value * jnp.tanh(mixed[2 * channels : 3 * channels] * scale)
            start = j * pitch
            for m in range(width // LANES):
                scratch[n * (width // LANES) + m, pl.ds(start, channels), :] = edge[
                    :, m * LANES : (m + 1) * LANES
                ]
            if own:
                gated = jnp.dot(
                    full_ref[3 * channels :], terms, preferred_element_type=jnp.float32
                )
                gate = 0.5 + 0.5 * jnp.tanh(gated * scale)
                rest[3][j, :, cols] = gate.astype(jnp.bfloat16)
        return carry

    lax.fori_loop(0, block, one_row, 0, unroll=min(16, block))
    half = channels // 2

    def one_channel(c, carry):
        for n in range(length // LANES):
            for side in range(2):
                rows_of = scratch[n, pl.ds(c + side * half, block, stride=pitch), :]
                rest[side][c, :, n * LANES : (n + 1) * LANES] = rows_of.astype(jnp.bfloat16)
        return carry

    lax.fori_loop(0, half, one_channel, 0, unroll=16)


def edges(own, row_index, maps, left, fold, mix, low, right, cols, block, skip=0, rows=None):
    _, heads, length = maps.shape
    rows = maps.shape[0] if rows is None else rows
    channels = right.shape[0]
    half = channels // 2
    out_shape = [jax.ShapeDtypeStruct((half, rows, length), jnp.bfloat16)] * 2
    out_specs = [pl.BlockSpec((half, block, length), lambda b, s: (0, b, 0))] * 2
    if own:
        out_shape += [jax.ShapeDtypeStruct((rows, channels, length), jnp.bfloat16)] * 2
        out_specs += [pl.BlockSpec((block, channels, length), lambda b, s: (b, 0, 0))] * 2
    first = skip // block
    whole = [pl.BlockSpec(a.shape, lambda b, s: (0, 0)) for a in (fold, mix, low, right, cols)]
    return pl.pallas_call(
        functools.partial(edges_kernel, own),
        out_shape=out_shape,
        grid_spec=pltpu.PrefetchScalarGridSpec(
            num_scalar_prefetch=1,
            grid=(rows // block,),
            in_specs=[
                pl.BlockSpec((block, heads, length), lambda b, s: (b + first, 0, 0)),
                pl.BlockSpec((block, channels), lambda b, s: (b, 0)),
            ]
            + whole,
            out_specs=out_specs,
            scratch_shapes=[
                pltpu.VMEM((length // LANES, block * (channels + 1) + 7, LANES), jnp.float32),
                pltpu.VMEM(mix.shape, jnp.bfloat16),
            ],
        ),
        compiler_params=pltpu.CompilerParams(vmem_limit_bytes=VMEM_BYTES),
        cost_estimate=pl.CostEstimate(
            flops=2 * rows * length * channels * 800,
            bytes_accessed=2 * rows * length * channels,
            transcendentals=rows * length * channels,
        ),
        name="own_edges" if own else "right_edges",
    )(row_index, maps, left, fold, mix, low, right, cols)


def products_kernel(keep_ref, arrive_ref, *refs):
    parts, (mine_ref, theirs_ref) = refs[:-2], refs[-2:]
    count, rows, _ = keep_ref.shape
    for c in range(count):
        lefts = jnp.concatenate([keep_ref[c], arrive_ref[c]], axis=0)
        for p, part in enumerate(parts):
            out = lax.dot_general(
                lefts, part[c], (((1,), (1,)), ((), ())), preferred_element_type=jnp.float32
            ).astype(jnp.bfloat16)
            mine_ref[p, c] = out[:rows]
            theirs_ref[p, c] = out[rows:]


def edge_products(keep, arrive, parts):
    half, rows, length = keep.shape
    each = parts[0].shape[1]
    count = 4 if half % 4 == 0 else 1
    out = jax.ShapeDtypeStruct((len(parts), half, rows, each), jnp.bfloat16)
    return pl.pallas_call(
        products_kernel,
        out_shape=[out] * 2,
        grid=(half // count,),
        in_specs=[pl.BlockSpec((count, rows, length), lambda b: (b, 0, 0))] * 2
        + [pl.BlockSpec((count, each, length), lambda b: (b, 0, 0))] * len(parts),
        out_specs=[pl.BlockSpec((len(parts), count, rows, each), lambda b: (0, b, 0, 0))] * 2,
        compiler_params=pltpu.CompilerParams(vmem_limit_bytes=VMEM_BYTES),
        cost_estimate=pl.CostEstimate(
            flops=4 * half * rows * len(parts) * each * length,
            bytes_accessed=2 * half * len(parts) * each * length,
            transcendentals=0,
        ),
        name="edge_products",
    )(keep, arrive, *parts)


def final_kernel(core, mine_ref, theirs_ref, pair_ref, gate_ref, gain_ref, w_ref, out_ref, scratch):
    half, block, width = mine_ref.shape[1:]
    for n, ref in enumerate((mine_ref, theirs_ref)):

        def one_channel(c, carry):
            scratch[n, pl.ds(c * (block + 1), block), :] = ref[0, c].astype(jnp.float32)
            return carry

        lax.fori_loop(0, half, one_channel, 0, unroll=8)

    def one_row(i, carry):
        products = jnp.concatenate(
            [scratch[n, pl.ds(i, half, stride=block + 1), :] for n in range(2)], axis=0
        )
        center = jnp.mean(products, axis=0, keepdims=True)
        centered = products - center
        variance = jnp.mean(centered * centered, axis=0, keepdims=True)
        normed = (centered * lax.rsqrt(variance + 1e-05) * gain_ref[...]).astype(jnp.bfloat16)
        projected = jnp.dot(w_ref[...], normed, preferred_element_type=jnp.float32)
        total = pair_ref[i].astype(jnp.float32) + gate_ref[i].astype(jnp.float32) * projected
        out_ref[i] = total.T.astype(jnp.bfloat16)
        return carry

    lax.fori_loop(0, block, one_row, 0, unroll=16)


def finish(core, mine, theirs, pair, gate, gain, weights, block):
    pieces, half, rows, width = mine.shape
    _, channels, length = pair.shape
    each = pieces // 2

    def column(u, core):
        side = u // each
        return (side + core[0] - 2 * side * core[0]) * each + u % each

    return pl.pallas_call(
        final_kernel,
        out_shape=jax.ShapeDtypeStruct((rows, length, channels), jnp.bfloat16),
        grid_spec=pltpu.PrefetchScalarGridSpec(
            num_scalar_prefetch=1,
            grid=(rows // block, pieces),
            in_specs=[
                pl.BlockSpec((1, half, block, width), lambda b, u, s: (u, 0, b, 0)),
                pl.BlockSpec(
                    (1, half, block, width), lambda b, u, s: ((u + each) % pieces, 0, b, 0)
                ),
                pl.BlockSpec((block, channels, width), lambda b, u, s: (b, 0, column(u, s))),
                pl.BlockSpec((block, channels, width), lambda b, u, s: (b, 0, column(u, s))),
                pl.BlockSpec(gain.shape, lambda b, u, s: (0, 0)),
                pl.BlockSpec(weights.shape, lambda b, u, s: (0, 0)),
            ],
            out_specs=pl.BlockSpec((block, width, channels), lambda b, u, s: (b, column(u, s), 0)),
            scratch_shapes=[pltpu.VMEM((2, half * (block + 1) + 7, width), jnp.float32)],
        ),
        compiler_params=pltpu.CompilerParams(vmem_limit_bytes=VMEM_BYTES),
        name="finish",
    )(core, mine, theirs, pair, gate, gain, weights)


def per_device(
    hidden_in,
    ln_gain,
    w_qkv,
    w_out,
    residue_index,
    w_map,
    relpos_table,
    w_side,
    tri_gain,
    w_tri,
    w_tri_out,
):
    local_rows = hidden_in.shape[0]
    devices_mp = lax.axis_size("mp")
    me = lax.axis_index("mp")
    core = lax.rem(me, 2)
    length = local_rows * devices_mp
    local_heads = w_qkv.shape[2] // HD
    heads, channels = w_map.shape
    swap = [(d, d ^ 1) for d in range(devices_mp)]
    normed = layer_norm(hidden_in.astype(jnp.float32), ln_gain, -1).astype(jnp.bfloat16)
    projected = jnp.einsum(
        "rd,tdh->trh",
        lax.all_gather(normed, "mp", axis=0, tiled=True),
        w_qkv,
        preferred_element_type=jnp.float32,
    )
    projected = projected.reshape(3, length, local_heads, HD)
    cos_table, sin_table = rotary_tables(length, HD)
    queries = rotate(projected[0] * HD ** (-0.5), cos_table, sin_table).astype(jnp.bfloat16)
    key_rows = rotate(projected[1], cos_table, sin_table).astype(jnp.bfloat16)
    value_rows = projected[2].astype(jnp.bfloat16)
    both = jnp.stack([queries.reshape(length, -1).T, key_rows.reshape(length, -1).T])
    gathered = lax.all_gather(both, "mp", axis=1, tiled=True)

    scores = jnp.einsum("qhd,khd->hqk", queries, key_rows, preferred_element_type=jnp.float32)
    attn_probs = jax.nn.softmax(scores, axis=-1).astype(jnp.bfloat16)
    attended = jnp.einsum(
        "hqk,khd->qhd", attn_probs, value_rows, preferred_element_type=jnp.float32
    )
    attended = attended.astype(jnp.bfloat16).reshape(length, local_heads * HD)
    side_parts = jnp.einsum(
        "rh,hsc->rsc",
        attended,
        jnp.einsum("hd,sdc->hsc", w_out, w_side, preferred_element_type=jnp.float32).astype(
            jnp.bfloat16
        ),
        preferred_element_type=jnp.float32,
    ).astype(jnp.bfloat16)
    own_sides = jnp.einsum("rd,sdc->rsc", hidden_in, w_side, preferred_element_type=jnp.float32)
    all_sides, att_rows = exchange_sides(
        side_parts.reshape(devices_mp, local_rows, 2 * channels),
        own_sides.reshape(local_rows, 2 * channels),
        attended.reshape(devices_mp, local_rows, local_heads * HD),
    )
    out_part, all_sides, att_rows, gathered = lax.optimization_barrier(
        (w_out, all_sides, att_rows, gathered)
    )
    full_out = lax.all_gather(out_part, "mp", axis=0)
    all_keys = gathered[1].reshape(heads, HD, length)
    all_queries = gathered[0].reshape(heads, HD, length).transpose(0, 2, 1)

    half_rows = length // 2
    row_start = me * local_rows
    half_start = core * half_rows
    own_maps = attention_maps(
        lax.dynamic_slice_in_dim(all_queries, row_start, local_rows, 1), all_keys, local_rows
    )
    map_block = 64 if half_rows % 64 == 0 else local_rows
    half_maps = attention_maps(
        lax.dynamic_slice_in_dim(all_queries, half_start, half_rows, 1), all_keys, map_block
    )

    all_sides = all_sides.reshape(length, 2 * channels)
    left_rows = all_sides[:, :channels]
    right = all_sides[:, channels:].T

    map_high, map_low = two_terms(w_map.astype(jnp.float32) * length)
    bin_high, bin_low = two_terms(relpos_table)
    bin_pad = ((0, BIN_ROWS - relpos_table.shape[0]), (0, 0))
    map_full = w_map.astype(jnp.float32) * length
    turn = -core * (channels // 2)
    halved = 0.5 * w_tri.astype(jnp.float32) * tri_gain[0][None, :, None]
    identity = jnp.eye(channels, dtype=jnp.float32)
    center = identity - 1.0 / channels

    def gated(p, shift):
        return jnp.dot(jnp.roll(halved[p].T, shift, axis=0), center, precision=EXACT)

    def mixing(fold, block):
        eye_rows = -(-block // 16) * 16
        parts = [
            jnp.zeros((eye_rows, channels), jnp.float32),
            map_full,
            jnp.pad(relpos_table, bin_pad),
            identity,
        ]
        mix = jnp.dot(fold, jnp.concatenate(parts, axis=0).T, precision=EXACT)
        return fold.astype(jnp.bfloat16), mix

    def low_terms(block):
        eye_rows = -(-block // 16) * 16
        parts = [jnp.zeros((eye_rows, channels), jnp.bfloat16), map_low, jnp.pad(bin_low, bin_pad)]
        return jnp.concatenate(parts, axis=0).T

    cols = residue_index[None, :]

    block = 16 if local_rows % 16 == 0 else local_rows
    half_left = lax.dynamic_slice_in_dim(left_rows, half_start, half_rows, 0)
    half_index = lax.dynamic_slice_in_dim(residue_index, half_start, half_rows, 0)
    each = half_rows // CHUNKS
    r_block = 16 if each % 16 == 0 else each
    right_fold, right_mix = mixing(
        jnp.concatenate([center, gated(2, turn), gated(3, turn)], axis=0), r_block
    )
    right_mix = right_mix.astype(jnp.bfloat16)
    left_fold, left_mix = mixing(
        jnp.concatenate([identity, gated(0, turn), gated(1, turn), gated(4, 0)], axis=0), block
    )
    left_mix = lax.reduce_precision(left_mix, 8, 7).astype(jnp.bfloat16)
    own_low = low_terms(block)
    right_low = low_terms(r_block)
    kept, arriving = [], []
    for n in range(CHUNKS):
        part = slice(n * each, (n + 1) * each)
        keep, send = edges(
            False,
            half_index[part],
            half_maps,
            half_left[part],
            right_fold,
            right_mix,
            right_low,
            right,
            cols,
            r_block,
            n * each,
            each,
        )
        kept.append(keep)
        arriving.append(lax.ppermute(send, "mp", swap))
    left_keep, left_send, pair, gate = edges(
        True,
        lax.dynamic_slice_in_dim(residue_index, row_start, local_rows, 0),
        own_maps,
        lax.dynamic_slice_in_dim(left_rows, row_start, local_rows, 0),
        left_fold,
        left_mix,
        own_low,
        right,
        cols,
        block,
    )
    left_arrive = lax.ppermute(left_send, "mp", swap)
    mine, theirs = edge_products(left_keep, left_arrive, kept + arriving)
    theirs = lax.ppermute(theirs, "mp", swap)
    pair_out = finish(
        core[None],
        mine,
        theirs,
        pair,
        gate,
        jnp.broadcast_to(jnp.roll(tri_gain[1], turn)[:, None], (channels, each)),
        jnp.roll(w_tri_out, turn, axis=0).T,
        local_rows,
    )
    attended_rows = att_rows.transpose(1, 0, 2).reshape(local_rows, -1)
    mixed = jnp.dot(
        attended_rows, full_out.reshape(-1, full_out.shape[-1]), preferred_element_type=jnp.float32
    )
    hidden_out = (hidden_in.astype(jnp.float32) + mixed).astype(jnp.bfloat16)
    return (hidden_out, pair_out)


def solution(mesh):
    placed = (
        P(("groups", "mp"), None),
        P(),
        P(None, None, "mp"),
        P("mp", None),
        P("groups"),
        P(),
        P(),
        P(),
        P(),
        P(),
        P(),
    )
    return jax.shard_map(
        per_device,
        mesh=mesh,
        in_specs=placed,
        out_specs=(P(("groups", "mp"), None), P(("groups", "mp"), None, None)),
        check_vma=False,
    )
```

```python
import functools

import jax
import jax.numpy as jnp
import numpy as np
from jax import lax
from jax.experimental import pallas as pl
from jax.experimental.pallas import tpu as pltpu
from jax.sharding import PartitionSpec as P

HD = 64
BINS = 65
BIN_ROWS = 80
LANES = 128
CHUNKS = 3
VMEM_BYTES = 60 * 1024 * 1024
MESH = pl.DeviceIdType.MESH
EXACT = lax.Precision.HIGHEST


def layer_norm(tensor, gain_vec, norm_axis):
    center = jnp.mean(tensor, axis=norm_axis, keepdims=True)
    centered = tensor - center
    variance = jnp.mean(centered * centered, axis=norm_axis, keepdims=True)
    return centered * lax.rsqrt(variance + 1e-05) * gain_vec


def rotary_tables(length, heads):
    powers = np.arange(0, HD, 2, dtype=np.float32) / np.float32(HD)
    inv_freq = np.float32(1.0) / np.power(np.float32(10000.0), powers)
    angles = np.arange(length, dtype=np.float32)[:, None] * inv_freq[None, :]
    cos, sin = np.cos(angles), np.sin(angles)
    return (
        jnp.asarray(np.tile(np.concatenate([cos, cos], axis=1), (1, heads)), jnp.float32),
        jnp.asarray(np.tile(np.concatenate([-sin, sin], axis=1), (1, heads)), jnp.float32),
    )


def maps_kernel(first, q_ref, k_ref, out_ref, scratch):
    pieces, _, rows, wide = q_ref.shape
    blocks = scratch.shape[0]
    heads = pieces * (wide // HD)

    def one_piece(d, carry):
        queries, keys = q_ref[d, 0], k_ref[d]
        lane = lax.broadcasted_iota(jnp.int32, queries.shape, 1)
        for h in range(wide // HD):
            mine = (lane >= h * HD) & (lane < (h + 1) * HD)
            own = jnp.where(mine, queries.astype(jnp.float32), 0.0).astype(jnp.bfloat16)
            scores = jnp.dot(own, keys, preferred_element_type=jnp.float32)
            top = jnp.max(scores, axis=-1, keepdims=True)
            powers = jnp.exp(scores - top)
            probs = powers * (1.0 / jnp.sum(powers, axis=-1, keepdims=True))
            start = (d * (wide // HD) + h) * (rows + 1)
            for n in range(blocks):
                scratch[n, pl.ds(start, rows), :] = probs[:, n * LANES : (n + 1) * LANES]
        return carry

    lax.fori_loop(0, pieces, one_piece, 0, unroll=4)

    def one_row(j, carry):
        for n in range(blocks):
            rows_of = scratch[n, pl.ds(j, heads, stride=rows + 1), :]
            out_ref[j, :, n * LANES : (n + 1) * LANES] = rows_of.astype(jnp.bfloat16)
        return carry

    lax.fori_loop(0, rows, one_row, 0, unroll=8)


def attention_maps(first, queries, keys, count):
    pieces, _, rows, wide = queries.shape
    length = keys.shape[2]
    heads = pieces * (wide // HD)
    return pl.pallas_call(
        maps_kernel,
        out_shape=jax.ShapeDtypeStruct((count * rows, heads, length), jnp.bfloat16),
        grid_spec=pltpu.PrefetchScalarGridSpec(
            num_scalar_prefetch=1,
            grid=(count,),
            in_specs=[
                pl.BlockSpec((pieces, 1, rows, wide), lambda b, s: (0, s[0] + b, 0, 0)),
                pl.BlockSpec(keys.shape, lambda b, s: (0, 0, 0)),
            ],
            out_specs=pl.BlockSpec((rows, heads, length), lambda b, s: (b, 0, 0)),
            scratch_shapes=[
                pltpu.VMEM((length // LANES, heads * (rows + 1) + 7, LANES), jnp.float32)
            ],
        ),
        compiler_params=pltpu.CompilerParams(vmem_limit_bytes=VMEM_BYTES),
        cost_estimate=pl.CostEstimate(
            flops=2 * heads * count * rows * length * HD * 4,
            bytes_accessed=2 * heads * count * rows * length,
            transcendentals=heads * count * rows * length,
        ),
        name="attention_maps",
    )(first, queries, keys)


class Ring:
    def __init__(self, count, across, arrays, send, recv, local):
        self.arrays, self.send, self.recv, self.local = arrays, send, recv, local
        self.count, self.across, self.chips = count, across, count // 2
        self.ahead = self.chips // 2
        self.back = self.chips - 1 - self.ahead
        self.me = lax.axis_index("mp")
        self.core = lax.rem(self.me, 2)
        self.place = self.position(lax.div(self.me, 2))

    def position(self, chip):
        if self.across == 1:
            return chip
        z, y = lax.div(chip, 2), lax.rem(chip, 2)
        return z + y * (self.chips - 1 - 2 * z)

    def device(self, shift):
        place = lax.rem(self.place + self.chips + shift, self.chips)
        if self.across == 1:
            return 2 * place + self.core
        y = lax.div(place, self.chips // 2)
        z = place + y * (self.chips - 1 - 2 * place)
        return 2 * (2 * z + y) + self.core

    def twin(self):
        return self.me + 1 - 2 * self.core

    def copy(self, a, block, own, slot, target):
        src, out = self.arrays[a]
        return pltpu.make_async_remote_copy(
            src_ref=src if own else out.at[block],
            dst_ref=out.at[block],
            send_sem=self.send.at[a, slot],
            recv_sem=self.recv.at[a, slot],
            device_id={"mp": target},
            device_id_type=MESH,
        )

    def hop(self, a, way, step):
        slot = step if way > 0 else self.ahead + step
        return self.copy(a, self.device(-way * step), step == 0, slot, self.device(way))

    def hand(self, a, way, step):
        if way == 0:
            return self.copy(a, self.me, True, self.chips - 1, self.twin())
        slot = self.chips + (step if way > 0 else self.ahead + step)
        return self.copy(a, self.device(-way * (step + 1)), False, slot, self.twin())

    def keep(self, a):
        src, out = self.arrays[a]
        return pltpu.make_async_copy(src, out.at[self.me], self.local.at[a])

    def start(self):
        for a in range(len(self.arrays)):
            self.hop(a, 1, 0).start()
            if self.back:
                self.hop(a, -1, 0).start()
            self.hand(a, 0, 0).start()
            self.keep(a).start()

    def steps(self):
        return self.ahead

    def step(self, s):
        for a in range(len(self.arrays)):
            for way, most in ((1, self.ahead), (-1, self.back)):
                if s < most:
                    self.hop(a, way, s).wait_recv()
                    if s + 1 < most:
                        self.hop(a, way, s + 1).start()
                    self.hand(a, way, s).start()

    def finish(self):
        for a in range(len(self.arrays)):
            hands = [self.hand(a, 0, 0)]
            for way, most in ((1, self.ahead), (-1, self.back)):
                for s in range(most):
                    self.hop(a, way, s).wait_send()
                    hands.append(self.hand(a, way, s))
            for hand in hands:
                hand.wait_recv()
                hand.wait_send()
            self.keep(a).wait()


def greet_all(count):
    me = lax.axis_index("mp")
    barrier = pltpu.get_barrier_semaphore()

    def greet(d, carry):
        pl.semaphore_signal(
            barrier, inc=1, device_id={"mp": lax.rem(me + d, count)}, device_id_type=MESH
        )
        return carry

    lax.fori_loop(1, count, greet, 0)
    pl.semaphore_wait(barrier, count - 1)


def gather_kernel(
    count,
    across,
    eyes,
    x_ref,
    gain_ref,
    w_out_ref,
    w_side_ref,
    tri_gain_ref,
    tri_ref,
    map_ref,
    bins_ref,
    *rest,
):
    all_ref, side_ref, own_ref, r_fold, r_mix, l_fold, l_mix, low_ref = rest[:8]
    normed, send, recv, local = rest[8:]
    core = lax.rem(lax.axis_index("mp"), 2)
    greet_all(count)
    hidden = x_ref[...].astype(jnp.float32)
    normed[...] = layer_norm(hidden, gain_ref[...], -1).astype(jnp.bfloat16)
    ring = Ring(count, across, [(normed, all_ref)], send, recv, local)
    ring.start()

    channels = tri_ref.shape[1]
    for s in range(2):
        cols = slice(s * channels, (s + 1) * channels)
        own_ref[:, cols] = jnp.dot(
            x_ref[...], w_side_ref[s], preferred_element_type=jnp.float32
        )
        side_ref[:, cols] = jnp.dot(
            w_out_ref[...], w_side_ref[s], preferred_element_type=jnp.float32
        ).astype(jnp.bfloat16)
    ring.step(0)

    row = lax.broadcasted_iota(jnp.int32, (channels, channels), 0)
    column = lax.broadcasted_iota(jnp.int32, (channels, channels), 1)
    identity = jnp.where(row == column, 1.0, 0.0)
    center = identity - 1.0 / channels
    half = channels // 2
    length = x_ref.shape[0] * count
    maps = map_ref[...].astype(jnp.float32) * length
    bins = bins_ref[...]

    def gated(p, turned):
        weights = tri_ref[p].astype(jnp.float32).T * (0.5 * tri_gain_ref[0:1, :])
        if turned:
            other = jnp.concatenate([weights[half:], weights[:half]], axis=0)
            weights = jnp.where(core == 0, weights, other)
        return jnp.dot(weights, center, precision=EXACT, preferred_element_type=jnp.float32)

    def across_terms(fold, parts, eye_rows):
        rows = jnp.concatenate([jnp.zeros((eye_rows, channels), jnp.float32)] + parts, axis=0)
        return lax.dot_general(
            fold,
            rows,
            (((1,), (1,)), ((), ())),
            precision=EXACT,
            preferred_element_type=jnp.float32,
        ).astype(jnp.bfloat16)

    fold = jnp.concatenate([center, gated(2, True), gated(3, True)], axis=0)
    r_fold[...] = fold.astype(jnp.bfloat16)
    r_mix[...] = across_terms(fold, [maps, bins, identity], eyes[0])
    for s in range(1, ring.steps()):
        ring.step(s)
        if s == 1:
            fold = jnp.concatenate(
                [identity, gated(0, True), gated(1, True), gated(4, False)], axis=0
            )
            l_fold[...] = fold.astype(jnp.bfloat16)
            l_mix[...] = across_terms(fold, [maps, bins, identity], eyes[1])
            low = [v - v.astype(jnp.bfloat16).astype(jnp.float32) for v in (maps, bins)]
            low_ref[...] = across_terms(identity, low, eyes[1])
    ring.finish()


def gather_rows(count, across, eyes, *operands):
    block, _, w_out, w_side, _, w_tri, w_map, bins = operands
    channels = w_tri.shape[1]
    sems = pltpu.SemaphoreType.DMA((1, count - 1))
    vmem = pl.BlockSpec(memory_space=pltpu.VMEM)
    terms = [e + w_map.shape[0] + bins.shape[0] for e in eyes]
    outs = [
        ((count,) + block.shape, jnp.bfloat16),
        ((w_out.shape[0], 2 * channels), jnp.bfloat16),
        ((block.shape[0], 2 * channels), jnp.float32),
        ((3 * channels, channels), jnp.bfloat16),
        ((3 * channels, terms[0] + channels), jnp.bfloat16),
        ((4 * channels, channels), jnp.bfloat16),
        ((4 * channels, terms[1] + channels), jnp.bfloat16),
        ((channels, terms[1]), jnp.bfloat16),
    ]
    return pl.pallas_call(
        functools.partial(gather_kernel, count, across, eyes),
        out_shape=[jax.ShapeDtypeStruct(*out) for out in outs],
        in_specs=[vmem] * len(operands),
        out_specs=[pl.BlockSpec(memory_space=pl.ANY)] + [vmem] * 7,
        scratch_shapes=[
            pltpu.VMEM(block.shape, jnp.bfloat16),
            sems,
            sems,
            pltpu.SemaphoreType.DMA((1,)),
        ],
        compiler_params=pltpu.CompilerParams(
            collective_id=0, has_side_effects=True, vmem_limit_bytes=VMEM_BYTES
        ),
        name="gather_rows",
    )(*operands)


def attend_kernel(count, across, x_ref, w_ref, cos_ref, sin_ref, mix_ref, own_ref, *rest):
    q_all, k_all, out_ref, rows_ref = rest[:4]
    q_ref, k_ref, v_ref, att, parts, landed, mine, send, recv, local = rest[4:14]
    send_a, recv_a, send_b, recv_b, send_c, recv_c = rest[14:]
    me = lax.axis_index("mp")
    width, length = k_ref.shape
    rows = length // count
    turn = HD // 2

    def each(step):
        def run(d, carry):
            step(d)
            return carry

        lax.fori_loop(1, count, run, 0)

    def rotated(tensor, where):
        turned = []
        for h in range(0, width, HD):
            turned += [tensor[:, h + turn : h + HD], tensor[:, h : h + turn]]
        turned = jnp.concatenate(turned, axis=1)
        return tensor * cos_ref[where, :] + turned * sin_ref[where, :]

    greet_all(count)
    span = length // 2
    for r in range(2):
        where = slice(r * span, (r + 1) * span)
        both = jnp.dot(
            x_ref[where, :],
            jnp.concatenate([w_ref[0], w_ref[1]], axis=1),
            preferred_element_type=jnp.float32,
        )
        queries = rotated(both[:, :width] * HD**-0.5, where).astype(jnp.bfloat16)
        k_ref[:, where] = rotated(both[:, width:], where).T.astype(jnp.bfloat16)
        for b in range(count // 2):
            q_ref[r * (count // 2) + b] = queries[b * rows : (b + 1) * rows]
    ring = Ring(count, across, [(k_ref, k_all), (q_ref, q_all)], send, recv, local)
    ring.start()
    v_ref[...] = jnp.dot(x_ref[...], w_ref[2], preferred_element_type=jnp.float32).astype(
        jnp.bfloat16
    )
    group = 4

    def one_group(g, carry):
        queries = q_ref[pl.ds(g * group, group)].reshape(group * rows, width)
        found = []
        for h in range(width // HD):
            head = slice(h * HD, (h + 1) * HD)
            scores = jnp.dot(queries[:, head], k_ref[head, :], preferred_element_type=jnp.float32)
            powers = jnp.exp(scores - jnp.max(scores, axis=-1, keepdims=True))
            probs = powers * (1.0 / jnp.sum(powers, axis=-1, keepdims=True))
            found.append(
                jnp.dot(
                    probs.astype(jnp.bfloat16), v_ref[:, head], preferred_element_type=jnp.float32
                )
            )
        found = jnp.concatenate(found, axis=1).astype(jnp.bfloat16)
        part = jnp.dot(found, mix_ref[...], preferred_element_type=jnp.float32)
        part = part.astype(jnp.bfloat16)
        for b in range(group):
            att[g * group + b] = found[b * rows : (b + 1) * rows]
            parts[g * group + b] = part[b * rows : (b + 1) * rows]
        return carry

    lax.fori_loop(0, count // group, one_group, 0)

    def scatter(d):
        target = lax.rem(me + d, count)
        return pltpu.make_async_remote_copy(
            src_ref=parts.at[target],
            dst_ref=landed.at[d],
            send_sem=send_a.at[d],
            recv_sem=recv_a.at[d],
            device_id={"mp": target},
            device_id_type=MESH,
        )

    def carry_rows(d):
        target = lax.rem(me + d, count)
        return pltpu.make_async_remote_copy(
            src_ref=att.at[target],
            dst_ref=rows_ref.at[me],
            send_sem=send_c.at[d],
            recv_sem=recv_c.at[d],
            device_id={"mp": target},
            device_id_type=MESH,
        )

    def spread(d):
        return pltpu.make_async_remote_copy(
            src_ref=mine,
            dst_ref=out_ref.at[me],
            send_sem=send_b.at[d],
            recv_sem=recv_b.at[d],
            device_id={"mp": lax.rem(me + d, count)},
            device_id_type=MESH,
        )

    each(lambda d: scatter(d).start())
    ring.step(0)

    def add(d, total):
        scatter(d).wait_recv()
        return total + landed[d].astype(jnp.float32)

    total = lax.fori_loop(1, count, add, own_ref[...] + parts[me].astype(jnp.float32))
    mine[...] = total.astype(jnp.bfloat16)
    out_ref[me] = total.astype(jnp.bfloat16)
    each(lambda d: spread(d).start())
    for s in range(1, ring.steps()):
        ring.step(s)
    rows_ref[me] = att[me]
    each(lambda d: carry_rows(d).start())
    ring.finish()
    each(lambda d: spread(d).wait_recv())
    each(lambda d: carry_rows(d).wait_recv())
    each(lambda d: scatter(d).wait_send())
    each(lambda d: spread(d).wait_send())
    each(lambda d: carry_rows(d).wait_send())


def attend_and_gather(count, across, rows, weights, cos_table, sin_table, mix, own):
    length, width = cos_table.shape
    ring_sems = pltpu.SemaphoreType.DMA((2, count - 1))
    sems = pltpu.SemaphoreType.DMA((count,))
    vmem = pl.BlockSpec(memory_space=pltpu.VMEM)
    anywhere = pl.BlockSpec(memory_space=pl.ANY)
    queries, keys = (count, length // count, width), (width, length)
    sides = (count,) + own.shape
    shapes = [(count,) + queries, (count,) + keys, sides, queries]
    scratch = [queries, keys, (length, width), queries, sides, sides, own.shape]
    return pl.pallas_call(
        functools.partial(attend_kernel, count, across),
        out_shape=[jax.ShapeDtypeStruct(shape, jnp.bfloat16) for shape in shapes],
        in_specs=[vmem] * 6,
        out_specs=[anywhere, anywhere, vmem, vmem],
        scratch_shapes=[pltpu.VMEM(shape, jnp.bfloat16) for shape in scratch]
        + [ring_sems, ring_sems, pltpu.SemaphoreType.DMA((2,))]
        + [sems] * 6,
        compiler_params=pltpu.CompilerParams(
            collective_id=1, has_side_effects=True, vmem_limit_bytes=VMEM_BYTES
        ),
        name="attend_and_gather",
    )(rows, weights, cos_table, sin_table, mix, own)


def places_of(rows, width):
    places = lax.broadcasted_iota(jnp.int32, (rows, width), 0)
    return places.astype(jnp.float32).astype(jnp.bfloat16)


def hot_rows(places, index):
    index = index.astype(jnp.float32).astype(jnp.bfloat16)
    return jnp.where(places == index, jnp.ones((), jnp.bfloat16), jnp.zeros((), jnp.bfloat16))


def edges_kernel(
    own, row_index, maps_ref, left_ref, fold_ref, mix_ref, low_ref, right_ref, cols_ref, *rest
):
    scratch, full_ref = rest[-2], rest[-1]
    block, heads, length = maps_ref.shape
    channels = right_ref.shape[0]
    eye_rows = mix_ref.shape[1] - channels - heads - BIN_ROWS
    pitch = channels + 1
    width = 2 * LANES
    reach = (BINS - 1) // 2
    first = pl.program_id(0) * block

    lefts = jnp.concatenate(
        [left_ref[...], jnp.zeros((LANES - block, channels), jnp.bfloat16)], axis=0
    )
    folded = lax.dot_general(
        fold_ref[...], lefts, (((1,), (1,)), ((), ())), preferred_element_type=jnp.float32
    )
    full_ref[:, :LANES] = (folded + mix_ref[:, :LANES].astype(jnp.float32)).astype(jnp.bfloat16)
    full_ref[:, LANES:] = mix_ref[:, LANES:]

    def one_row(j, carry):
        here = row_index[first + j]
        eye = hot_rows(places_of(eye_rows, width), jnp.broadcast_to(j, (1, width)))
        for n in range(length // width):
            cols = slice(n * width, (n + 1) * width)
            bins = jnp.clip(cols_ref[:, cols] - here, -reach, reach) + reach
            hot = hot_rows(places_of(BIN_ROWS, width), bins)
            probs = maps_ref[j, :, cols]
            terms = jnp.concatenate([eye, probs, hot, right_ref[:, cols]], axis=0)
            mixed = jnp.dot(
                full_ref[: 3 * channels], terms, preferred_element_type=jnp.float32
            )
            centered = mixed[:channels]
            if own:
                pair = centered + jnp.dot(
                    low_ref[...],
                    jnp.concatenate([eye, probs, hot], axis=0),
                    preferred_element_type=jnp.float32,
                )
                rest[2][j, :, cols] = pair.astype(jnp.bfloat16)
                centered = pair - jnp.sum(pair, axis=0, keepdims=True) * (1.0 / channels)
            variance = jnp.sum(centered * centered, axis=0, keepdims=True) * (1.0 / channels)
            scale = lax.rsqrt(variance + 1e-05)
            value = mixed[channels : 2 * channels] * scale
            edge = value + value * jnp.tanh(mixed[2 * channels : 3 * channels] * scale)
            start = j * pitch
            for m in range(width // LANES):
                scratch[n * (width // LANES) + m, pl.ds(start, channels), :] = edge[
                    :, m * LANES : (m + 1) * LANES
                ]
            if own:
                gated = jnp.dot(
                    full_ref[3 * channels :], terms, preferred_element_type=jnp.float32
                )
                gate = 0.5 + 0.5 * jnp.tanh(gated * scale)
                rest[3][j, :, cols] = gate.astype(jnp.bfloat16)
        return carry

    lax.fori_loop(0, block, one_row, 0, unroll=min(16, block))
    half = channels // 2

    def one_channel(c, carry):
        for n in range(length // LANES):
            for side in range(2):
                rows_of = scratch[n, pl.ds(c + side * half, block, stride=pitch), :]
                rest[side][c, :, n * LANES : (n + 1) * LANES] = rows_of.astype(jnp.bfloat16)
        return carry

    lax.fori_loop(0, half, one_channel, 0, unroll=16)


def edges(own, row_index, maps, left, fold, mix, low, right, cols, block, skip=0, rows=None):
    _, heads, length = maps.shape
    rows = maps.shape[0] if rows is None else rows
    channels = right.shape[0]
    half = channels // 2
    out_shape = [jax.ShapeDtypeStruct((half, rows, length), jnp.bfloat16)] * 2
    out_specs = [pl.BlockSpec((half, block, length), lambda b, s: (0, b, 0))] * 2
    if own:
        out_shape += [jax.ShapeDtypeStruct((rows, channels, length), jnp.bfloat16)] * 2
        out_specs += [pl.BlockSpec((block, channels, length), lambda b, s: (b, 0, 0))] * 2
    first = skip // block
    whole = [pl.BlockSpec(a.shape, lambda b, s: (0, 0)) for a in (fold, mix, low, right, cols)]
    return pl.pallas_call(
        functools.partial(edges_kernel, own),
        out_shape=out_shape,
        grid_spec=pltpu.PrefetchScalarGridSpec(
            num_scalar_prefetch=1,
            grid=(rows // block,),
            in_specs=[
                pl.BlockSpec((block, heads, length), lambda b, s: (b + first, 0, 0)),
                pl.BlockSpec((block, channels), lambda b, s: (b, 0)),
            ]
            + whole,
            out_specs=out_specs,
            scratch_shapes=[
                pltpu.VMEM((length // LANES, block * (channels + 1) + 7, LANES), jnp.float32),
                pltpu.VMEM(mix.shape, jnp.bfloat16),
            ],
        ),
        compiler_params=pltpu.CompilerParams(vmem_limit_bytes=VMEM_BYTES),
        cost_estimate=pl.CostEstimate(
            flops=2 * rows * length * channels * 800,
            bytes_accessed=2 * rows * length * channels,
            transcendentals=rows * length * channels,
        ),
        name="own_edges" if own else "right_edges",
    )(row_index, maps, left, fold, mix, low, right, cols)


def products_kernel(keep_ref, arrive_ref, *refs):
    parts, (mine_ref, theirs_ref) = refs[:-2], refs[-2:]
    count, rows, _ = keep_ref.shape
    for c in range(count):
        lefts = jnp.concatenate([keep_ref[c], arrive_ref[c]], axis=0)
        for p, part in enumerate(parts):
            out = lax.dot_general(
                lefts, part[c], (((1,), (1,)), ((), ())), preferred_element_type=jnp.float32
            ).astype(jnp.bfloat16)
            mine_ref[p, c] = out[:rows]
            theirs_ref[p, c] = out[rows:]


def edge_products(keep, arrive, parts):
    half, rows, length = keep.shape
    each = parts[0].shape[1]
    count = 4 if half % 4 == 0 else 1
    out = jax.ShapeDtypeStruct((len(parts), half, rows, each), jnp.bfloat16)
    return pl.pallas_call(
        products_kernel,
        out_shape=[out] * 2,
        grid=(half // count,),
        in_specs=[pl.BlockSpec((count, rows, length), lambda b: (b, 0, 0))] * 2
        + [pl.BlockSpec((count, each, length), lambda b: (b, 0, 0))] * len(parts),
        out_specs=[pl.BlockSpec((len(parts), count, rows, each), lambda b: (0, b, 0, 0))] * 2,
        compiler_params=pltpu.CompilerParams(vmem_limit_bytes=VMEM_BYTES),
        cost_estimate=pl.CostEstimate(
            flops=4 * half * rows * len(parts) * each * length,
            bytes_accessed=2 * half * len(parts) * each * length,
            transcendentals=0,
        ),
        name="edge_products",
    )(keep, arrive, *parts)


def final_kernel(core, mine_ref, theirs_ref, pair_ref, gate_ref, gain_ref, w_ref, out_ref, scratch):
    half, block, width = mine_ref.shape[1:]
    for n, ref in enumerate((mine_ref, theirs_ref)):

        def one_channel(c, carry):
            scratch[n, pl.ds(c * (block + 1), block), :] = ref[0, c].astype(jnp.float32)
            return carry

        lax.fori_loop(0, half, one_channel, 0, unroll=8)

    def one_row(i, carry):
        products = jnp.concatenate(
            [scratch[n, pl.ds(i, half, stride=block + 1), :] for n in range(2)], axis=0
        )
        center = jnp.mean(products, axis=0, keepdims=True)
        centered = products - center
        variance = jnp.mean(centered * centered, axis=0, keepdims=True)
        normed = (centered * lax.rsqrt(variance + 1e-05) * gain_ref[...]).astype(jnp.bfloat16)
        projected = jnp.dot(w_ref[...], normed, preferred_element_type=jnp.float32)
        total = pair_ref[i].astype(jnp.float32) + gate_ref[i].astype(jnp.float32) * projected
        out_ref[i] = total.T.astype(jnp.bfloat16)
        return carry

    lax.fori_loop(0, block, one_row, 0, unroll=16)


def finish(core, mine, theirs, pair, gate, gain, weights, block):
    pieces, half, rows, width = mine.shape
    _, channels, length = pair.shape
    each = pieces // 2

    def column(u, core):
        side = u // each
        return (side + core[0] - 2 * side * core[0]) * each + u % each

    return pl.pallas_call(
        final_kernel,
        out_shape=jax.ShapeDtypeStruct((rows, length, channels), jnp.bfloat16),
        grid_spec=pltpu.PrefetchScalarGridSpec(
            num_scalar_prefetch=1,
            grid=(rows // block, pieces),
            in_specs=[
                pl.BlockSpec((1, half, block, width), lambda b, u, s: (u, 0, b, 0)),
                pl.BlockSpec(
                    (1, half, block, width), lambda b, u, s: ((u + each) % pieces, 0, b, 0)
                ),
                pl.BlockSpec((block, channels, width), lambda b, u, s: (b, 0, column(u, s))),
                pl.BlockSpec((block, channels, width), lambda b, u, s: (b, 0, column(u, s))),
                pl.BlockSpec(gain.shape, lambda b, u, s: (0, 0)),
                pl.BlockSpec(weights.shape, lambda b, u, s: (0, 0)),
            ],
            out_specs=pl.BlockSpec((block, width, channels), lambda b, u, s: (b, column(u, s), 0)),
            scratch_shapes=[pltpu.VMEM((2, half * (block + 1) + 7, width), jnp.float32)],
        ),
        compiler_params=pltpu.CompilerParams(vmem_limit_bytes=VMEM_BYTES),
        name="finish",
    )(core, mine, theirs, pair, gate, gain, weights)


def per_device(
    across,
    hidden_in,
    ln_gain,
    w_qkv,
    w_out,
    residue_index,
    w_map,
    relpos_table,
    w_side,
    tri_gain,
    w_tri,
    w_tri_out,
):
    local_rows = hidden_in.shape[0]
    devices_mp = lax.axis_size("mp")
    me = lax.axis_index("mp")
    core = lax.rem(me, 2)
    length = local_rows * devices_mp
    local_heads = w_qkv.shape[2] // HD
    heads, channels = w_map.shape
    swap = [(d, d ^ 1) for d in range(devices_mp)]
    half_rows = length // 2
    each = half_rows // CHUNKS
    block = 16 if local_rows % 16 == 0 else local_rows
    r_block = 16 if each % 16 == 0 else each
    turn = -core * (channels // 2)
    gathered, side_mix, own_sides, right_fold, right_mix, left_fold, left_mix, low = gather_rows(
        devices_mp,
        across,
        tuple(-(-b // 16) * 16 for b in (r_block, block)),
        hidden_in,
        ln_gain[None],
        w_out,
        w_side,
        tri_gain,
        w_tri,
        w_map,
        jnp.pad(relpos_table, ((0, BIN_ROWS - relpos_table.shape[0]), (0, 0))),
    )
    cos_table, sin_table = rotary_tables(length, local_heads)
    all_queries, all_keys, all_sides, att_rows = attend_and_gather(
        devices_mp,
        across,
        gathered.reshape(length, -1),
        w_qkv,
        cos_table,
        sin_table,
        side_mix,
        own_sides,
    )
    out_part, all_sides, att_rows, all_queries, all_keys = lax.optimization_barrier(
        (w_out, all_sides, att_rows, all_queries, all_keys)
    )
    full_out = lax.all_gather(out_part, "mp", axis=0)

    row_start = me * local_rows
    half_start = core * half_rows
    own_maps = attention_maps(me[None], all_queries, all_keys, 1)
    half_maps = attention_maps(
        (core * (devices_mp // 2))[None], all_queries, all_keys, devices_mp // 2
    )

    all_sides = all_sides.reshape(length, 2 * channels)
    left_rows = all_sides[:, :channels]
    right = all_sides[:, channels:].T

    cols = residue_index[None, :]

    half_left = lax.dynamic_slice_in_dim(left_rows, half_start, half_rows, 0)
    half_index = lax.dynamic_slice_in_dim(residue_index, half_start, half_rows, 0)
    kept, arriving = [], []
    for n in range(CHUNKS):
        part = slice(n * each, (n + 1) * each)
        keep, send = edges(
            False,
            half_index[part],
            half_maps,
            half_left[part],
            right_fold,
            right_mix,
            low,
            right,
            cols,
            r_block,
            n * each,
            each,
        )
        kept.append(keep)
        arriving.append(lax.ppermute(send, "mp", swap))
    left_keep, left_send, pair, gate = edges(
        True,
        lax.dynamic_slice_in_dim(residue_index, row_start, local_rows, 0),
        own_maps,
        lax.dynamic_slice_in_dim(left_rows, row_start, local_rows, 0),
        left_fold,
        left_mix,
        low,
        right,
        cols,
        block,
    )
    left_arrive = lax.ppermute(left_send, "mp", swap)
    mine, theirs = edge_products(left_keep, left_arrive, kept + arriving)
    theirs = lax.ppermute(theirs, "mp", swap)
    pair_out = finish(
        core[None],
        mine,
        theirs,
        pair,
        gate,
        jnp.broadcast_to(jnp.roll(tri_gain[1], turn)[:, None], (channels, each)),
        jnp.roll(w_tri_out, turn, axis=0).T,
        local_rows,
    )
    attended_rows = att_rows.transpose(1, 0, 2).reshape(local_rows, -1)
    mixed = jnp.dot(
        attended_rows, full_out.reshape(-1, full_out.shape[-1]), preferred_element_type=jnp.float32
    )
    hidden_out = (hidden_in.astype(jnp.float32) + mixed).astype(jnp.bfloat16)
    return (hidden_out, pair_out)


def solution(mesh):
    placed = (
        P(("groups", "mp"), None),
        P(),
        P(None, None, "mp"),
        P("mp", None),
        P("groups"),
        P(),
        P(),
        P(),
        P(),
        P(),
        P(),
    )
    chips = [d.coords for d in mesh.devices.reshape(-1, mesh.shape["mp"])[0][::2] if hasattr(d, "coords")]
    across = 1
    if len(chips) > 3 and sum(abs(p - q) for p, q in zip(chips[0], chips[2])) == 1:
        across = 2
    return jax.shard_map(
        functools.partial(per_device, across),
        mesh=mesh,
        in_specs=placed,
        out_specs=(P(("groups", "mp"), None), P(("groups", "mp"), None, None)),
        check_vma=False,
    )
```

```python
import functools

import jax
import jax.numpy as jnp
import numpy as np
from jax import lax
from jax.experimental import pallas as pl
from jax.experimental.pallas import tpu as pltpu
from jax.sharding import PartitionSpec as P

HD = 64
BINS = 65
BIN_ROWS = 80
LANES = 128
CHUNKS = 3
VMEM_BYTES = 60 * 1024 * 1024
MESH = pl.DeviceIdType.MESH
EXACT = lax.Precision.HIGHEST


def layer_norm(tensor, gain_vec, norm_axis):
    center = jnp.mean(tensor, axis=norm_axis, keepdims=True)
    centered = tensor - center
    variance = jnp.mean(centered * centered, axis=norm_axis, keepdims=True)
    return centered * lax.rsqrt(variance + 1e-05) * gain_vec


def rotary_tables(length, heads):
    powers = np.arange(0, HD, 2, dtype=np.float32) / np.float32(HD)
    inv_freq = np.float32(1.0) / np.power(np.float32(10000.0), powers)
    angles = np.arange(length, dtype=np.float32)[:, None] * inv_freq[None, :]
    cos, sin = np.cos(angles), np.sin(angles)
    return (
        jnp.asarray(np.tile(np.concatenate([cos, cos], axis=1), (1, heads)), jnp.float32),
        jnp.asarray(np.tile(np.concatenate([-sin, sin], axis=1), (1, heads)), jnp.float32),
    )


class Ring:
    def __init__(self, count, across, arrays, send, recv, local):
        self.arrays, self.send, self.recv, self.local = arrays, send, recv, local
        self.count, self.across, self.chips = count, across, count // 2
        self.ahead = self.chips // 2
        self.back = self.chips - 1 - self.ahead
        self.me = lax.axis_index("mp")
        self.core = lax.rem(self.me, 2)
        self.place = self.position(lax.div(self.me, 2))

    def position(self, chip):
        if self.across == 1:
            return chip
        z, y = lax.div(chip, 2), lax.rem(chip, 2)
        return z + y * (self.chips - 1 - 2 * z)

    def device(self, shift):
        place = lax.rem(self.place + self.chips + shift, self.chips)
        if self.across == 1:
            return 2 * place + self.core
        y = lax.div(place, self.chips // 2)
        z = place + y * (self.chips - 1 - 2 * place)
        return 2 * (2 * z + y) + self.core

    def twin(self):
        return self.me + 1 - 2 * self.core

    def copy(self, a, block, own, slot, target):
        src, out = self.arrays[a]
        return pltpu.make_async_remote_copy(
            src_ref=src if own else out.at[block],
            dst_ref=out.at[block],
            send_sem=self.send.at[a, slot],
            recv_sem=self.recv.at[a, slot],
            device_id={"mp": target},
            device_id_type=MESH,
        )

    def hop(self, a, way, step):
        slot = step if way > 0 else self.ahead + step
        return self.copy(a, self.device(-way * step), step == 0, slot, self.device(way))

    def hand(self, a, way, step):
        if way == 0:
            return self.copy(a, self.me, True, self.chips - 1, self.twin())
        slot = self.chips + (step if way > 0 else self.ahead + step)
        return self.copy(a, self.device(-way * (step + 1)), False, slot, self.twin())

    def keep(self, a):
        src, out = self.arrays[a]
        return pltpu.make_async_copy(src, out.at[self.me], self.local.at[a])

    def start(self, store=True):
        for a in range(len(self.arrays)):
            self.hop(a, 1, 0).start()
            if self.back:
                self.hop(a, -1, 0).start()
            self.hand(a, 0, 0).start()
            if store:
                self.keep(a).start()

    def steps(self):
        return self.ahead

    def ways(self, s):
        return [way for way, most in ((1, self.ahead), (-1, self.back)) if s < most]

    def step(self, s):
        for a in range(len(self.arrays)):
            for way in self.ways(s):
                self.hop(a, way, s).wait_recv()
                if way in self.ways(s + 1):
                    self.hop(a, way, s + 1).start()
                self.hand(a, way, s).start()

    def take(self, way, s):
        for a in range(len(self.arrays)):
            self.hand(a, way, s).wait_recv()

    def finish(self):
        for a in range(len(self.arrays)):
            self.hand(a, 0, 0).wait_send()
            for s in range(self.ahead):
                for way in self.ways(s):
                    self.hop(a, way, s).wait_send()
                    self.hand(a, way, s).wait_send()


def greet_all(count):
    me = lax.axis_index("mp")
    barrier = pltpu.get_barrier_semaphore()

    def greet(d, carry):
        pl.semaphore_signal(
            barrier, inc=1, device_id={"mp": lax.rem(me + d, count)}, device_id_type=MESH
        )
        return carry

    lax.fori_loop(1, count, greet, 0)
    pl.semaphore_wait(barrier, count - 1)


def gather_kernel(
    count,
    across,
    eyes,
    x_ref,
    gain_ref,
    w_out_ref,
    w_side_ref,
    tri_gain_ref,
    tri_ref,
    map_ref,
    bins_ref,
    *rest,
):
    all_ref, side_ref, own_ref, r_fold, r_mix, l_fold, l_mix, low_ref = rest[:8]
    normed, send, recv, local = rest[8:]
    core = lax.rem(lax.axis_index("mp"), 2)
    greet_all(count)
    hidden = x_ref[...].astype(jnp.float32)
    normed[...] = layer_norm(hidden, gain_ref[...], -1).astype(jnp.bfloat16)
    ring = Ring(count, across, [(normed, all_ref)], send, recv, local)
    ring.start()

    channels = tri_ref.shape[1]
    for s in range(2):
        cols = slice(s * channels, (s + 1) * channels)
        own_ref[:, cols] = jnp.dot(
            x_ref[...], w_side_ref[s], preferred_element_type=jnp.float32
        )
        side_ref[:, cols] = jnp.dot(
            w_out_ref[...], w_side_ref[s], preferred_element_type=jnp.float32
        ).astype(jnp.bfloat16)
    ring.step(0)

    row = lax.broadcasted_iota(jnp.int32, (channels, channels), 0)
    column = lax.broadcasted_iota(jnp.int32, (channels, channels), 1)
    identity = jnp.where(row == column, 1.0, 0.0)
    center = identity - 1.0 / channels
    half = channels // 2
    length = x_ref.shape[0] * count
    maps = map_ref[...].astype(jnp.float32) * length
    bins = bins_ref[...]

    def gated(p, turned):
        weights = tri_ref[p].astype(jnp.float32).T * (0.5 * tri_gain_ref[0:1, :])
        if turned:
            other = jnp.concatenate([weights[half:], weights[:half]], axis=0)
            weights = jnp.where(core == 0, weights, other)
        return jnp.dot(weights, center, precision=EXACT, preferred_element_type=jnp.float32)

    def across_terms(fold, parts, eye_rows):
        rows = jnp.concatenate([jnp.zeros((eye_rows, channels), jnp.float32)] + parts, axis=0)
        return lax.dot_general(
            fold,
            rows,
            (((1,), (1,)), ((), ())),
            precision=EXACT,
            preferred_element_type=jnp.float32,
        ).astype(jnp.bfloat16)

    fold = jnp.concatenate([center, gated(2, True), gated(3, True)], axis=0)
    r_fold[...] = fold.astype(jnp.bfloat16)
    r_mix[...] = across_terms(fold, [maps, bins, identity], eyes[0])
    for s in range(1, ring.steps()):
        ring.step(s)
        if s == 1:
            fold = jnp.concatenate(
                [identity, gated(0, True), gated(1, True), gated(4, False)], axis=0
            )
            l_fold[...] = fold.astype(jnp.bfloat16)
            l_mix[...] = across_terms(fold, [maps, bins, identity], eyes[1])
            low = [v - v.astype(jnp.bfloat16).astype(jnp.float32) for v in (maps, bins)]
            low_ref[...] = across_terms(identity, low, eyes[1])
    ring.take(0, 0)
    for s in range(ring.steps()):
        for way in ring.ways(s):
            ring.take(way, s)
    ring.finish()
    ring.keep(0).wait()


def gather_rows(count, across, eyes, *operands):
    block, _, w_out, w_side, _, w_tri, w_map, bins = operands
    channels = w_tri.shape[1]
    sems = pltpu.SemaphoreType.DMA((1, count - 1))
    vmem = pl.BlockSpec(memory_space=pltpu.VMEM)
    terms = [e + w_map.shape[0] + bins.shape[0] for e in eyes]
    outs = [
        ((count,) + block.shape, jnp.bfloat16),
        ((w_out.shape[0], 2 * channels), jnp.bfloat16),
        ((block.shape[0], 2 * channels), jnp.float32),
        ((3 * channels, channels), jnp.bfloat16),
        ((3 * channels, terms[0] + channels), jnp.bfloat16),
        ((4 * channels, channels), jnp.bfloat16),
        ((4 * channels, terms[1] + channels), jnp.bfloat16),
        ((channels, terms[1]), jnp.bfloat16),
    ]
    return pl.pallas_call(
        functools.partial(gather_kernel, count, across, eyes),
        out_shape=[jax.ShapeDtypeStruct(*out) for out in outs],
        in_specs=[vmem] * len(operands),
        out_specs=[pl.BlockSpec(memory_space=pl.ANY)] + [vmem] * 7,
        scratch_shapes=[
            pltpu.VMEM(block.shape, jnp.bfloat16),
            sems,
            sems,
            pltpu.SemaphoreType.DMA((1,)),
        ],
        compiler_params=pltpu.CompilerParams(
            collective_id=0, has_side_effects=True, vmem_limit_bytes=VMEM_BYTES
        ),
        name="gather_rows",
    )(*operands)


def attend_kernel(count, across, x_ref, w_ref, cos_ref, sin_ref, mix_ref, own_ref, *rest):
    maps_ref, out_ref, att = rest[:3]
    q_ref, k_ref, v_ref, q_all, k_all, parts, paired, landed, mine, stage = rest[3:13]
    send, recv, pair_sems, send_a, recv_a, send_b, recv_b, send_c, recv_c, stored = rest[13:]
    me = lax.axis_index("mp")
    core, chip, chips = lax.rem(me, 2), lax.div(me, 2), count // 2
    twin = me + 1 - 2 * core
    width, length = k_ref.shape
    rows = length // count
    half = count // 2
    turn = HD // 2
    heads = [slice(h * HD, (h + 1) * HD) for h in range(width // HD)]

    def rotated(tensor, where):
        turned = []
        for h in range(0, width, HD):
            turned += [tensor[:, h + turn : h + HD], tensor[:, h : h + turn]]
        turned = jnp.concatenate(turned, axis=1)
        return tensor * cos_ref[where, :] + turned * sin_ref[where, :]

    def softmax(scores):
        powers = jnp.exp(scores - jnp.max(scores, axis=-1, keepdims=True))
        probs = powers * (1.0 / jnp.sum(powers, axis=-1, keepdims=True))
        return probs.astype(jnp.bfloat16)

    greet_all(count)
    span = length // 2
    for r in range(2):
        where = slice(r * span, (r + 1) * span)
        both = jnp.dot(
            x_ref[where, :],
            jnp.concatenate([w_ref[0], w_ref[1]], axis=1),
            preferred_element_type=jnp.float32,
        )
        queries = rotated(both[:, :width] * HD**-0.5, where).astype(jnp.bfloat16)
        k_ref[:, where] = rotated(both[:, width:], where).T.astype(jnp.bfloat16)
        for b in range(half):
            q_ref[r * half + b] = queries[b * rows : (b + 1) * rows]
    ring = Ring(count, across, [(k_ref, k_all), (q_ref, q_all)], send, recv, None)
    ring.start(store=False)
    v_ref[...] = jnp.dot(x_ref[...], w_ref[2], preferred_element_type=jnp.float32).astype(
        jnp.bfloat16
    )
    group = 4

    def one_group(g, carry):
        queries = q_ref[pl.ds(g * group, group)].reshape(group * rows, width)
        found = []
        for head in heads:
            scores = jnp.dot(queries[:, head], k_ref[head, :], preferred_element_type=jnp.float32)
            found.append(
                jnp.dot(softmax(scores), v_ref[:, head], preferred_element_type=jnp.float32)
            )
        found = jnp.concatenate(found, axis=1).astype(jnp.bfloat16)
        part = jnp.dot(found, mix_ref[...], preferred_element_type=jnp.float32)
        part = part.astype(jnp.bfloat16)
        for b in range(group):
            att[g * group + b] = found[b * rows : (b + 1) * rows]
            parts[b % 2, g * (group // 2) + b // 2] = part[b * rows : (b + 1) * rows]
        return carry

    lax.fori_loop(0, count // group, one_group, 0)

    pair = pltpu.make_async_remote_copy(
        src_ref=parts.at[1 - core],
        dst_ref=paired,
        send_sem=pair_sems.at[0],
        recv_sem=pair_sems.at[1],
        device_id={"mp": twin},
        device_id_type=MESH,
    )
    pair.start()

    def store(i, block):
        return pltpu.make_async_copy(stage.at[i % 2], maps_ref.at[block], stored.at[i % 2])

    def block_maps(i, queries_of, keys_of, block):
        slot = i % 2
        if i >= 2:
            store(i, block).wait()

        def fill(queries, start, size):
            queries = queries.reshape(size, width)
            for h, head in enumerate(heads):
                scores = jnp.dot(
                    queries[:, head], keys_of[head, :], preferred_element_type=jnp.float32
                )
                stage[slot, h, pl.ds(start, size), :] = softmax(scores)

        def one_pair(g, carry):
            start = pl.multiple_of(g * 2 * rows, 16)
            fill(queries_of[pl.ds(core * half + 2 * g, 2)], start, 2 * rows)
            return carry

        lax.fori_loop(0, half // 2, one_pair, 0)
        fill(queries_of[pl.ds(me, 1)], half * rows, rows)
        store(i, block).start()

    block_maps(0, q_ref, k_ref, me)

    def scatter(d):
        target = lax.rem(chip + d, chips)
        return pltpu.make_async_remote_copy(
            src_ref=paired.at[target],
            dst_ref=landed.at[d],
            send_sem=send_a.at[d],
            recv_sem=recv_a.at[d],
            device_id={"mp": 2 * target + core},
            device_id_type=MESH,
        )

    def spread(d):
        return pltpu.make_async_remote_copy(
            src_ref=mine,
            dst_ref=out_ref.at[me],
            send_sem=send_b.at[d],
            recv_sem=recv_b.at[d],
            device_id={"mp": 2 * lax.rem(chip + d, chips) + core},
            device_id_type=MESH,
        )

    def hand_side(d):
        source = 2 * lax.rem(chip + chips - d, chips) + core
        return pltpu.make_async_remote_copy(
            src_ref=out_ref.at[source],
            dst_ref=out_ref.at[source],
            send_sem=send_c.at[d],
            recv_sem=recv_c.at[d],
            device_id={"mp": twin},
            device_id_type=MESH,
        )

    def each(step, first=1):
        def run(d, carry):
            step(d)
            return carry

        lax.fori_loop(first, chips, run, 0)

    pair.wait_recv()

    def join(d):
        both = paired[d].astype(jnp.float32) + parts[core, d].astype(jnp.float32)
        paired[d] = both.astype(jnp.bfloat16)

    each(join, 0)
    each(lambda d: scatter(d).start())
    ring.take(0, 0)
    block_maps(1, q_all.at[twin], k_all.at[twin], twin)
    done = 2
    for s in range(ring.steps()):
        ring.step(s)
        if s == 0:

            def add(d, total):
                scatter(d).wait_recv()
                return total + landed[d].astype(jnp.float32)

            total = own_ref[...] + paired[chip].astype(jnp.float32)
            total = lax.fori_loop(1, chips, add, total).astype(jnp.bfloat16)
            mine[...] = total
            out_ref[me] = total
            each(lambda d: spread(d).start())
            hand_side(0).start()
        if s == min(1, ring.steps() - 1):

            def forward(d):
                spread(d).wait_recv()
                hand_side(d).start()

            each(forward)
        for way in ring.ways(s):
            block = ring.device(-way * (s + 1))
            block_maps(done, q_all.at[block], k_all.at[block], block)
            done += 1
        for way in ring.ways(s):
            block = ring.device(-way * (s + 1)) + 1 - 2 * core
            ring.take(way, s)
            block_maps(done, q_all.at[block], k_all.at[block], block)
            done += 1
    ring.finish()
    store(done - 2, me).wait()
    store(done - 1, me).wait()
    pair.wait_send()
    each(lambda d: hand_side(d).wait_recv(), 0)
    each(lambda d: hand_side(d).wait_send(), 0)
    each(lambda d: scatter(d).wait_send())
    each(lambda d: spread(d).wait_send())


def attend_and_gather(count, across, rows, weights, cos_table, sin_table, mix, own):
    length, width = cos_table.shape
    ring_sems = pltpu.SemaphoreType.DMA((2, count - 1))
    sems = pltpu.SemaphoreType.DMA((count // 2,))
    vmem = pl.BlockSpec(memory_space=pltpu.VMEM)
    queries, keys = (count, length // count, width), (width, length)
    sides = (count // 2,) + own.shape
    piece = (width // HD, length // 2 + length // count, length)
    shapes = [(count,) + piece, (count,) + own.shape, queries]
    scratch = [
        queries,
        keys,
        (length, width),
        (count,) + queries,
        (count,) + keys,
        (2,) + sides,
        sides,
        sides,
        own.shape,
        (2,) + piece,
    ]
    return pl.pallas_call(
        functools.partial(attend_kernel, count, across),
        out_shape=[jax.ShapeDtypeStruct(shape, jnp.bfloat16) for shape in shapes],
        in_specs=[vmem] * 6,
        out_specs=[pl.BlockSpec(memory_space=pl.ANY), vmem, vmem],
        scratch_shapes=[pltpu.VMEM(shape, jnp.bfloat16) for shape in scratch]
        + [ring_sems, ring_sems, pltpu.SemaphoreType.DMA((2,))]
        + [sems] * 6
        + [pltpu.SemaphoreType.DMA((2,))],
        compiler_params=pltpu.CompilerParams(
            collective_id=1, has_side_effects=True, vmem_limit_bytes=VMEM_BYTES
        ),
        name="attend_and_gather",
    )(rows, weights, cos_table, sin_table, mix, own)


def places_of(rows, width):
    places = lax.broadcasted_iota(jnp.int32, (rows, width), 0)
    return places.astype(jnp.float32).astype(jnp.bfloat16)


def hot_rows(places, index):
    index = index.astype(jnp.float32).astype(jnp.bfloat16)
    return jnp.where(places == index, jnp.ones((), jnp.bfloat16), jnp.zeros((), jnp.bfloat16))


def edges_kernel(
    own, row_index, maps_ref, left_ref, fold_ref, mix_ref, low_ref, right_ref, cols_ref, *rest
):
    scratch, full_ref, probs_ref = rest[-3:]
    heads, block, length = maps_ref.shape
    channels = right_ref.shape[0]
    eye_rows = mix_ref.shape[1] - channels - heads - BIN_ROWS
    pitch = channels + 1
    width = 2 * LANES
    reach = (BINS - 1) // 2
    first = pl.program_id(0) * block

    lefts = jnp.concatenate(
        [left_ref[...], jnp.zeros((LANES - block, channels), jnp.bfloat16)], axis=0
    )
    folded = lax.dot_general(
        fold_ref[...], lefts, (((1,), (1,)), ((), ())), preferred_element_type=jnp.float32
    )
    full_ref[:, :LANES] = (folded + mix_ref[:, :LANES].astype(jnp.float32)).astype(jnp.bfloat16)
    full_ref[:, LANES:] = mix_ref[:, LANES:]

    def one_head(h, carry):
        for n in range(length // LANES):
            probs_ref[n, pl.ds(h * (block + 1), block), :] = maps_ref[
                h, :, n * LANES : (n + 1) * LANES
            ].astype(jnp.float32)
        return carry

    lax.fori_loop(0, heads, one_head, 0, unroll=8)

    def one_row(j, carry):
        here = row_index[first + j]
        eye = hot_rows(places_of(eye_rows, width), jnp.broadcast_to(j, (1, width)))
        for n in range(length // width):
            cols = slice(n * width, (n + 1) * width)
            bins = jnp.clip(cols_ref[:, cols] - here, -reach, reach) + reach
            hot = hot_rows(places_of(BIN_ROWS, width), bins)
            probs = [
                probs_ref[m, pl.ds(j, heads, stride=block + 1), :].astype(jnp.bfloat16)
                for m in range(n * width // LANES, (n + 1) * width // LANES)
            ]
            probs = jnp.concatenate(probs, axis=1)
            terms = jnp.concatenate([eye, probs, hot, right_ref[:, cols]], axis=0)
            mixed = jnp.dot(
                full_ref[: 3 * channels], terms, preferred_element_type=jnp.float32
            )
            centered = mixed[:channels]
            if own:
                pair = centered + jnp.dot(
                    low_ref[...],
                    jnp.concatenate([eye, probs, hot], axis=0),
                    preferred_element_type=jnp.float32,
                )
                rest[2][j, :, cols] = pair.astype(jnp.bfloat16)
                centered = pair - jnp.sum(pair, axis=0, keepdims=True) * (1.0 / channels)
            variance = jnp.sum(centered * centered, axis=0, keepdims=True) * (1.0 / channels)
            scale = lax.rsqrt(variance + 1e-05)
            value = mixed[channels : 2 * channels] * scale
            edge = value + value * jnp.tanh(mixed[2 * channels : 3 * channels] * scale)
            start = j * pitch
            for m in range(width // LANES):
                scratch[n * (width // LANES) + m, pl.ds(start, channels), :] = edge[
                    :, m * LANES : (m + 1) * LANES
                ]
            if own:
                gated = jnp.dot(
                    full_ref[3 * channels :], terms, preferred_element_type=jnp.float32
                )
                gate = 0.5 + 0.5 * jnp.tanh(gated * scale)
                rest[3][j, :, cols] = gate.astype(jnp.bfloat16)
        return carry

    lax.fori_loop(0, block, one_row, 0, unroll=min(16, block))
    half = channels // 2

    def one_channel(c, carry):
        for n in range(length // LANES):
            for side in range(2):
                rows_of = scratch[n, pl.ds(c + side * half, block, stride=pitch), :]
                rest[side][c, :, n * LANES : (n + 1) * LANES] = rows_of.astype(jnp.bfloat16)
        return carry

    lax.fori_loop(0, half, one_channel, 0, unroll=16)


def edges(own, row_index, maps, left, fold, mix, low, right, cols, block, skip, rows):
    heads, _, length = maps.shape
    channels = right.shape[0]
    half = channels // 2
    out_shape = [jax.ShapeDtypeStruct((half, rows, length), jnp.bfloat16)] * 2
    out_specs = [pl.BlockSpec((half, block, length), lambda b, s: (0, b, 0))] * 2
    if own:
        out_shape += [jax.ShapeDtypeStruct((rows, channels, length), jnp.bfloat16)] * 2
        out_specs += [pl.BlockSpec((block, channels, length), lambda b, s: (b, 0, 0))] * 2
    first = skip // block
    whole = [pl.BlockSpec(a.shape, lambda b, s: (0, 0)) for a in (fold, mix, low, right, cols)]
    return pl.pallas_call(
        functools.partial(edges_kernel, own),
        out_shape=out_shape,
        grid_spec=pltpu.PrefetchScalarGridSpec(
            num_scalar_prefetch=1,
            grid=(rows // block,),
            in_specs=[
                pl.BlockSpec((heads, block, length), lambda b, s: (0, b + first, 0)),
                pl.BlockSpec((block, channels), lambda b, s: (b, 0)),
            ]
            + whole,
            out_specs=out_specs,
            scratch_shapes=[
                pltpu.VMEM((length // LANES, block * (channels + 1) + 7, LANES), jnp.float32),
                pltpu.VMEM(mix.shape, jnp.bfloat16),
                pltpu.VMEM((length // LANES, heads * (block + 1) + 7, LANES), jnp.float32),
            ],
        ),
        compiler_params=pltpu.CompilerParams(vmem_limit_bytes=VMEM_BYTES),
        cost_estimate=pl.CostEstimate(
            flops=2 * rows * length * channels * 800,
            bytes_accessed=2 * rows * length * channels,
            transcendentals=rows * length * channels,
        ),
        name="own_edges" if own else "right_edges",
    )(row_index, maps, left, fold, mix, low, right, cols)


def products_kernel(keep_ref, arrive_ref, *refs):
    parts, (mine_ref, theirs_ref) = refs[:-2], refs[-2:]
    count, rows, _ = keep_ref.shape
    for c in range(count):
        lefts = jnp.concatenate([keep_ref[c], arrive_ref[c]], axis=0)
        for p, part in enumerate(parts):
            out = lax.dot_general(
                lefts, part[c], (((1,), (1,)), ((), ())), preferred_element_type=jnp.float32
            ).astype(jnp.bfloat16)
            mine_ref[p, c] = out[:rows]
            theirs_ref[p, c] = out[rows:]


def edge_products(keep, arrive, parts):
    half, rows, length = keep.shape
    each = parts[0].shape[1]
    count = 4 if half % 4 == 0 else 1
    out = jax.ShapeDtypeStruct((len(parts), half, rows, each), jnp.bfloat16)
    return pl.pallas_call(
        products_kernel,
        out_shape=[out] * 2,
        grid=(half // count,),
        in_specs=[pl.BlockSpec((count, rows, length), lambda b: (b, 0, 0))] * 2
        + [pl.BlockSpec((count, each, length), lambda b: (b, 0, 0))] * len(parts),
        out_specs=[pl.BlockSpec((len(parts), count, rows, each), lambda b: (0, b, 0, 0))] * 2,
        compiler_params=pltpu.CompilerParams(vmem_limit_bytes=VMEM_BYTES),
        cost_estimate=pl.CostEstimate(
            flops=4 * half * rows * len(parts) * each * length,
            bytes_accessed=2 * half * len(parts) * each * length,
            transcendentals=0,
        ),
        name="edge_products",
    )(keep, arrive, *parts)


def final_kernel(core, mine_ref, theirs_ref, pair_ref, gate_ref, gain_ref, w_ref, out_ref, scratch):
    half, block, width = mine_ref.shape[1:]
    for n, ref in enumerate((mine_ref, theirs_ref)):

        def one_channel(c, carry):
            scratch[n, pl.ds(c * (block + 1), block), :] = ref[0, c].astype(jnp.float32)
            return carry

        lax.fori_loop(0, half, one_channel, 0, unroll=8)

    def one_row(i, carry):
        products = jnp.concatenate(
            [scratch[n, pl.ds(i, half, stride=block + 1), :] for n in range(2)], axis=0
        )
        center = jnp.mean(products, axis=0, keepdims=True)
        centered = products - center
        variance = jnp.mean(centered * centered, axis=0, keepdims=True)
        normed = (centered * lax.rsqrt(variance + 1e-05) * gain_ref[...]).astype(jnp.bfloat16)
        projected = jnp.dot(w_ref[...], normed, preferred_element_type=jnp.float32)
        total = pair_ref[i].astype(jnp.float32) + gate_ref[i].astype(jnp.float32) * projected
        out_ref[i] = total.T.astype(jnp.bfloat16)
        return carry

    lax.fori_loop(0, block, one_row, 0, unroll=16)


def finish(core, mine, theirs, pair, gate, gain, weights, block):
    pieces, half, rows, width = mine.shape
    _, channels, length = pair.shape
    each = pieces // 2

    def column(u, core):
        side = u // each
        return (side + core[0] - 2 * side * core[0]) * each + u % each

    return pl.pallas_call(
        final_kernel,
        out_shape=jax.ShapeDtypeStruct((rows, length, channels), jnp.bfloat16),
        grid_spec=pltpu.PrefetchScalarGridSpec(
            num_scalar_prefetch=1,
            grid=(rows // block, pieces),
            in_specs=[
                pl.BlockSpec((1, half, block, width), lambda b, u, s: (u, 0, b, 0)),
                pl.BlockSpec(
                    (1, half, block, width), lambda b, u, s: ((u + each) % pieces, 0, b, 0)
                ),
                pl.BlockSpec((block, channels, width), lambda b, u, s: (b, 0, column(u, s))),
                pl.BlockSpec((block, channels, width), lambda b, u, s: (b, 0, column(u, s))),
                pl.BlockSpec(gain.shape, lambda b, u, s: (0, 0)),
                pl.BlockSpec(weights.shape, lambda b, u, s: (0, 0)),
            ],
            out_specs=pl.BlockSpec((block, width, channels), lambda b, u, s: (b, column(u, s), 0)),
            scratch_shapes=[pltpu.VMEM((2, half * (block + 1) + 7, width), jnp.float32)],
        ),
        compiler_params=pltpu.CompilerParams(vmem_limit_bytes=VMEM_BYTES),
        name="finish",
    )(core, mine, theirs, pair, gate, gain, weights)


def per_device(
    across,
    hidden_in,
    ln_gain,
    w_qkv,
    w_out,
    residue_index,
    w_map,
    relpos_table,
    w_side,
    tri_gain,
    w_tri,
    w_tri_out,
):
    local_rows = hidden_in.shape[0]
    devices_mp = lax.axis_size("mp")
    me = lax.axis_index("mp")
    core = lax.rem(me, 2)
    length = local_rows * devices_mp
    local_heads = w_qkv.shape[2] // HD
    heads, channels = w_map.shape
    swap = [(d, d ^ 1) for d in range(devices_mp)]
    half_rows = length // 2
    each = half_rows // CHUNKS
    block = 16 if local_rows % 16 == 0 else local_rows
    r_block = 16 if each % 16 == 0 else each
    turn = -core * (channels // 2)
    gathered, side_mix, own_sides, right_fold, right_mix, left_fold, left_mix, low = gather_rows(
        devices_mp,
        across,
        tuple(-(-b // 16) * 16 for b in (r_block, block)),
        hidden_in,
        ln_gain[None],
        w_out,
        w_side,
        tri_gain,
        w_tri,
        w_map,
        jnp.pad(relpos_table, ((0, BIN_ROWS - relpos_table.shape[0]), (0, 0))),
    )
    cos_table, sin_table = rotary_tables(length, local_heads)
    maps, all_sides, attended = attend_and_gather(
        devices_mp,
        across,
        gathered.reshape(length, -1),
        w_qkv,
        cos_table,
        sin_table,
        side_mix,
        own_sides,
    )
    maps = maps.reshape(heads, half_rows + local_rows, length)
    out_part, all_sides, attended = lax.optimization_barrier((w_out, all_sides, attended))
    full_out = lax.all_gather(out_part, "mp", axis=0)
    att_rows = lax.all_to_all(attended, "mp", 0, 0)

    row_start = me * local_rows
    half_start = core * half_rows
    all_sides = all_sides.reshape(length, 2 * channels)
    left_rows = all_sides[:, :channels]
    right = all_sides[:, channels:].T

    cols = residue_index[None, :]

    half_left = lax.dynamic_slice_in_dim(left_rows, half_start, half_rows, 0)
    half_index = lax.dynamic_slice_in_dim(residue_index, half_start, half_rows, 0)
    kept, arriving = [], []
    for n in range(CHUNKS):
        part = slice(n * each, (n + 1) * each)
        keep, send = edges(
            False,
            half_index[part],
            maps,
            half_left[part],
            right_fold,
            right_mix,
            low,
            right,
            cols,
            r_block,
            n * each,
            each,
        )
        kept.append(keep)
        arriving.append(lax.ppermute(send, "mp", swap))
    left_keep, left_send, pair, gate = edges(
        True,
        lax.dynamic_slice_in_dim(residue_index, row_start, local_rows, 0),
        maps,
        lax.dynamic_slice_in_dim(left_rows, row_start, local_rows, 0),
        left_fold,
        left_mix,
        low,
        right,
        cols,
        block,
        half_rows,
        local_rows,
    )
    left_arrive = lax.ppermute(left_send, "mp", swap)
    mine, theirs = edge_products(left_keep, left_arrive, kept + arriving)
    theirs = lax.ppermute(theirs, "mp", swap)
    pair_out = finish(
        core[None],
        mine,
        theirs,
        pair,
        gate,
        jnp.broadcast_to(jnp.roll(tri_gain[1], turn)[:, None], (channels, each)),
        jnp.roll(w_tri_out, turn, axis=0).T,
        local_rows,
    )
    attended_rows = att_rows.transpose(1, 0, 2).reshape(local_rows, -1)
    mixed = jnp.dot(
        attended_rows, full_out.reshape(-1, full_out.shape[-1]), preferred_element_type=jnp.float32
    )
    hidden_out = (hidden_in.astype(jnp.float32) + mixed).astype(jnp.bfloat16)
    return (hidden_out, pair_out)


def solution(mesh):
    placed = (
        P(("groups", "mp"), None),
        P(),
        P(None, None, "mp"),
        P("mp", None),
        P("groups"),
        P(),
        P(),
        P(),
        P(),
        P(),
        P(),
    )
    chips = [d.coords for d in mesh.devices.reshape(-1, mesh.shape["mp"])[0][::2] if hasattr(d, "coords")]
    across = 1
    if len(chips) > 3 and sum(abs(p - q) for p, q in zip(chips[0], chips[2])) == 1:
        across = 2
    return jax.shard_map(
        functools.partial(per_device, across),
        mesh=mesh,
        in_specs=placed,
        out_specs=(P(("groups", "mp"), None), P(("groups", "mp"), None, None)),
        check_vma=False,
    )
```

```python
import functools

import jax
import jax.numpy as jnp
import numpy as np
from jax import lax
from jax.experimental import pallas as pl
from jax.experimental.pallas import tpu as pltpu
from jax.sharding import PartitionSpec as P

HD = 64
BINS = 65
BIN_ROWS = 80
LANES = 128
CHUNKS = 3
VMEM_BYTES = 60 * 1024 * 1024
MESH = pl.DeviceIdType.MESH
EXACT = lax.Precision.HIGHEST


def layer_norm(tensor, gain_vec, norm_axis):
    center = jnp.mean(tensor, axis=norm_axis, keepdims=True)
    centered = tensor - center
    variance = jnp.mean(centered * centered, axis=norm_axis, keepdims=True)
    return centered * lax.rsqrt(variance + 1e-05) * gain_vec


def rotary_tables(length, heads):
    powers = np.arange(0, HD, 2, dtype=np.float32) / np.float32(HD)
    inv_freq = np.float32(1.0) / np.power(np.float32(10000.0), powers)
    angles = np.arange(length, dtype=np.float32)[:, None] * inv_freq[None, :]
    cos, sin = np.cos(angles), np.sin(angles)
    return (
        jnp.asarray(np.tile(np.concatenate([cos, cos], axis=1), (1, heads)), jnp.float32),
        jnp.asarray(np.tile(np.concatenate([-sin, sin], axis=1), (1, heads)), jnp.float32),
    )


class Ring:
    def __init__(self, count, across, arrays, send, recv):
        self.arrays, self.send, self.recv = arrays, send, recv
        self.count, self.across, self.chips = count, across, count // 2
        self.ahead = self.chips // 2
        self.back = self.chips - 1 - self.ahead
        self.me = lax.axis_index("mp")
        self.core = lax.rem(self.me, 2)
        self.place = self.position(lax.div(self.me, 2))

    def position(self, chip):
        if self.across == 1:
            return chip
        z, y = lax.div(chip, 2), lax.rem(chip, 2)
        return z + y * (self.chips - 1 - 2 * z)

    def device(self, shift):
        place = lax.rem(self.place + self.chips + shift, self.chips)
        if self.across == 1:
            return 2 * place + self.core
        y = lax.div(place, self.chips // 2)
        z = place + y * (self.chips - 1 - 2 * place)
        return 2 * (2 * z + y) + self.core

    def twin(self):
        return self.me + 1 - 2 * self.core

    def copy(self, a, block, own, slot, target, part=None):
        src, out, axis = self.arrays[a]
        piece = ()
        if part is not None:
            size = src.shape[axis] // 2
            piece = (slice(None),) * axis + (pl.ds(part * size, size),)
        target_ref = out.at[(block,) + piece]
        source_ref = (src.at[piece] if piece else src) if own else target_ref
        return pltpu.make_async_remote_copy(
            src_ref=source_ref,
            dst_ref=target_ref,
            send_sem=self.send.at[a, slot],
            recv_sem=self.recv.at[a, slot],
            device_id={"mp": target},
            device_id_type=MESH,
        )

    def hop(self, a, way, step):
        slot = step if way > 0 else self.ahead + step
        part = None
        if self.back < self.ahead and step == self.back:
            part = 0 if way > 0 else 1
        block = self.device(-way * step)
        return self.copy(a, block, step == 0, slot, self.device(way), part)

    def hand(self, a, way, step):
        if way == 0:
            return self.copy(a, self.me, True, self.chips, self.twin())
        slot = self.chips + 1 + (step if way > 0 else self.ahead + step)
        return self.copy(a, self.device(-way * (step + 1)), False, slot, self.twin())

    def start(self):
        for a in range(len(self.arrays)):
            for way in (1, -1):
                self.hop(a, way, 0).start()
            self.hand(a, 0, 0).start()

    def steps(self):
        return self.ahead

    def ways(self, s):
        return [way for way, most in ((1, self.ahead), (-1, self.back)) if s < most]

    def step(self, s):
        for a in range(len(self.arrays)):
            for way in (1, -1):
                self.hop(a, way, s).wait_recv()
                if s + 1 < self.ahead:
                    self.hop(a, way, s + 1).start()
                if self.ways(s) == [1, -1]:
                    self.hand(a, way, s).start()
            if self.ways(s) == [1]:
                self.hand(a, 1, s).start()

    def take(self, way, s):
        for a in range(len(self.arrays)):
            self.hand(a, way, s).wait_recv()

    def finish(self):
        for a in range(len(self.arrays)):
            self.hand(a, 0, 0).wait_send()
            for s in range(self.ahead):
                for way in (1, -1):
                    self.hop(a, way, s).wait_send()
                for way in self.ways(s):
                    self.hand(a, way, s).wait_send()


def greet_all(count):
    me = lax.axis_index("mp")
    barrier = pltpu.get_barrier_semaphore()

    def greet(d, carry):
        pl.semaphore_signal(
            barrier, inc=1, device_id={"mp": lax.rem(me + d, count)}, device_id_type=MESH
        )
        return carry

    lax.fori_loop(1, count, greet, 0)
    pl.semaphore_wait(barrier, count - 1)


def gather_part(count, across, eyes, operands, outs, normed, x_all, send, recv):
    x_ref, gain_ref, w_out_ref, w_side_ref, tri_gain_ref, tri_ref, map_ref, bins_ref = operands
    side_ref, own_ref, r_fold, r_mix, l_fold, l_mix, low_ref = outs
    me = lax.axis_index("mp")
    core = lax.rem(me, 2)
    greet_all(count)
    hidden = x_ref[...].astype(jnp.float32)
    normed[...] = layer_norm(hidden, gain_ref[...], -1).astype(jnp.bfloat16)
    x_all[me] = normed[...]
    ring = Ring(count, across, [(normed, x_all, 1)], send, recv)
    ring.start()

    channels = tri_ref.shape[1]
    for s in range(2):
        cols = slice(s * channels, (s + 1) * channels)
        own_ref[:, cols] = jnp.dot(
            x_ref[...], w_side_ref[s], preferred_element_type=jnp.float32
        )
        side_ref[:, cols] = jnp.dot(
            w_out_ref[...], w_side_ref[s], preferred_element_type=jnp.float32
        ).astype(jnp.bfloat16)
    ring.step(0)

    row = lax.broadcasted_iota(jnp.int32, (channels, channels), 0)
    column = lax.broadcasted_iota(jnp.int32, (channels, channels), 1)
    identity = jnp.where(row == column, 1.0, 0.0)
    center = identity - 1.0 / channels
    half = channels // 2
    length = x_ref.shape[0] * count
    maps = map_ref[...].astype(jnp.float32) * length
    bins = bins_ref[...]

    def gated(p, turned):
        weights = tri_ref[p].astype(jnp.float32).T * (0.5 * tri_gain_ref[0:1, :])
        if turned:
            other = jnp.concatenate([weights[half:], weights[:half]], axis=0)
            weights = jnp.where(core == 0, weights, other)
        return jnp.dot(weights, center, precision=EXACT, preferred_element_type=jnp.float32)

    def across_terms(fold, parts, eye_rows):
        rows = jnp.concatenate([jnp.zeros((eye_rows, channels), jnp.float32)] + parts, axis=0)
        return lax.dot_general(
            fold,
            rows,
            (((1,), (1,)), ((), ())),
            precision=EXACT,
            preferred_element_type=jnp.float32,
        ).astype(jnp.bfloat16)

    fold = jnp.concatenate([center, gated(2, True), gated(3, True)], axis=0)
    r_fold[...] = fold.astype(jnp.bfloat16)
    r_mix[...] = across_terms(fold, [maps, bins, identity], eyes[0])
    for s in range(1, ring.steps()):
        ring.step(s)
        if s == 1:
            fold = jnp.concatenate(
                [identity, gated(0, True), gated(1, True), gated(4, False)], axis=0
            )
            l_fold[...] = fold.astype(jnp.bfloat16)
            l_mix[...] = across_terms(fold, [maps, bins, identity], eyes[1])
            low = [v - v.astype(jnp.bfloat16).astype(jnp.float32) for v in (maps, bins)]
            low_ref[...] = across_terms(identity, low, eyes[1])
    ring.take(0, 0)
    for s in range(ring.steps()):
        for way in ring.ways(s):
            ring.take(way, s)
    ring.finish()


def attend_kernel(count, across, eyes, *refs):
    operands, refs = refs[:8], refs[8:]
    w_ref, cos_ref, sin_ref = refs[:3]
    maps_ref, out_ref, rows_ref = refs[3:6]
    outs, rest = refs[6:11], refs[11:]
    mix_ref, own_ref, normed, x_all = rest[:4]
    q_ref, k_ref, v_ref, q_all, k_all, parts, paired, landed, mine, stage = rest[4:14]
    att, first_send, first_recv, send, recv, pair_sems = rest[14:20]
    send_a, recv_a, send_b, recv_b, send_c, recv_c, stored, send_d, recv_d = rest[20:]
    gather_part(
        count,
        across,
        eyes,
        operands,
        (mix_ref, own_ref) + tuple(outs),
        normed,
        x_all,
        first_send,
        first_recv,
    )
    me = lax.axis_index("mp")
    core, chip, chips = lax.rem(me, 2), lax.div(me, 2), count // 2
    twin = me + 1 - 2 * core
    width, length = k_ref.shape
    rows = length // count
    half = count // 2
    turn = HD // 2
    heads = [slice(h * HD, (h + 1) * HD) for h in range(width // HD)]

    def rotated(tensor, where):
        turned = []
        for h in range(0, width, HD):
            turned += [tensor[:, h + turn : h + HD], tensor[:, h : h + turn]]
        turned = jnp.concatenate(turned, axis=1)
        return tensor * cos_ref[where, :] + turned * sin_ref[where, :]

    def softmax(scores):
        powers = jnp.exp(scores - jnp.max(scores, axis=-1, keepdims=True))
        probs = powers * (1.0 / jnp.sum(powers, axis=-1, keepdims=True))
        return probs.astype(jnp.bfloat16)

    span = length // 2
    for r in range(2):
        where = slice(r * span, (r + 1) * span)
        both = jnp.dot(
            x_all[r * half : (r + 1) * half].reshape(span, x_all.shape[2]),
            jnp.concatenate([w_ref[0], w_ref[1]], axis=1),
            preferred_element_type=jnp.float32,
        )
        queries = rotated(both[:, :width] * HD**-0.5, where).astype(jnp.bfloat16)
        k_ref[:, where] = rotated(both[:, width:], where).T.astype(jnp.bfloat16)
        for b in range(half):
            q_ref[r * half + b] = queries[b * rows : (b + 1) * rows]
    ring = Ring(count, across, [(k_ref, k_all, 0), (q_ref, q_all, 0)], send, recv)
    ring.start()
    v_ref[...] = jnp.dot(
        x_all[...].reshape(length, x_all.shape[2]), w_ref[2], preferred_element_type=jnp.float32
    ).astype(jnp.bfloat16)
    group = 4

    def one_group(g, carry):
        queries = q_ref[pl.ds(g * group, group)].reshape(group * rows, width)
        found = []
        for head in heads:
            scores = jnp.dot(queries[:, head], k_ref[head, :], preferred_element_type=jnp.float32)
            found.append(
                jnp.dot(softmax(scores), v_ref[:, head], preferred_element_type=jnp.float32)
            )
        found = jnp.concatenate(found, axis=1).astype(jnp.bfloat16)
        part = jnp.dot(found, mix_ref[...], preferred_element_type=jnp.float32)
        part = part.astype(jnp.bfloat16)
        for b in range(group):
            att[g * group + b] = found[b * rows : (b + 1) * rows]
            parts[b % 2, g * (group // 2) + b // 2] = part[b * rows : (b + 1) * rows]
        return carry

    lax.fori_loop(0, count // group, one_group, 0)

    pair = pltpu.make_async_remote_copy(
        src_ref=parts.at[1 - core],
        dst_ref=paired,
        send_sem=pair_sems.at[0],
        recv_sem=pair_sems.at[1],
        device_id={"mp": twin},
        device_id_type=MESH,
    )
    pair.start()

    def store(i, block):
        return pltpu.make_async_copy(stage.at[i % 2], maps_ref.at[block], stored.at[i % 2])

    def block_maps(i, queries_of, keys_of, block):
        slot = i % 2
        if i >= 2:
            store(i, block).wait()

        def fill(queries, start, size):
            queries = queries.reshape(size, width)
            for h, head in enumerate(heads):
                scores = jnp.dot(
                    queries[:, head], keys_of[head, :], preferred_element_type=jnp.float32
                )
                stage[slot, h, pl.ds(start, size), :] = softmax(scores)

        def one_pair(g, carry):
            start = pl.multiple_of(g * 2 * rows, 16)
            fill(queries_of[pl.ds(core * half + 2 * g, 2)], start, 2 * rows)
            return carry

        lax.fori_loop(0, half // 2, one_pair, 0)
        fill(queries_of[pl.ds(me, 1)], half * rows, rows)
        store(i, block).start()

    block_maps(0, q_ref, k_ref, me)

    def scatter(d):
        target = lax.rem(chip + d, chips)
        return pltpu.make_async_remote_copy(
            src_ref=paired.at[target],
            dst_ref=landed.at[d],
            send_sem=send_a.at[d],
            recv_sem=recv_a.at[d],
            device_id={"mp": 2 * target + core},
            device_id_type=MESH,
        )

    def spread(d):
        return pltpu.make_async_remote_copy(
            src_ref=mine,
            dst_ref=out_ref.at[me],
            send_sem=send_b.at[d],
            recv_sem=recv_b.at[d],
            device_id={"mp": 2 * lax.rem(chip + d, chips) + core},
            device_id_type=MESH,
        )

    def hand_side(d):
        source = 2 * lax.rem(chip + chips - d, chips) + core
        return pltpu.make_async_remote_copy(
            src_ref=out_ref.at[source],
            dst_ref=out_ref.at[source],
            send_sem=send_c.at[d],
            recv_sem=recv_c.at[d],
            device_id={"mp": twin},
            device_id_type=MESH,
        )

    def each(step, first=1, last=chips):
        def run(d, carry):
            step(d)
            return carry

        lax.fori_loop(first, last, run, 0)

    def carry_rows(d):
        target = lax.rem(me + d, count)
        return pltpu.make_async_remote_copy(
            src_ref=att.at[target],
            dst_ref=rows_ref.at[me],
            send_sem=send_d.at[d],
            recv_sem=recv_d.at[d],
            device_id={"mp": target},
            device_id_type=MESH,
        )

    pair.wait_recv()

    def join(d):
        both = paired[d].astype(jnp.float32) + parts[core, d].astype(jnp.float32)
        paired[d] = both.astype(jnp.bfloat16)

    each(join, 0)
    each(lambda d: scatter(d).start())
    ring.take(0, 0)
    block_maps(1, q_all.at[twin], k_all.at[twin], twin)
    done = 2
    for s in range(ring.steps()):
        ring.step(s)
        if s == 0:

            def add(d, total):
                scatter(d).wait_recv()
                return total + landed[d].astype(jnp.float32)

            total = own_ref[...] + paired[chip].astype(jnp.float32)
            total = lax.fori_loop(1, chips, add, total).astype(jnp.bfloat16)
            mine[...] = total
            out_ref[me] = total
            each(lambda d: spread(d).start())
            hand_side(0).start()
        if s == min(1, ring.steps() - 1):

            def forward(d):
                spread(d).wait_recv()
                hand_side(d).start()

            each(forward)
        if s == ring.steps() - 1:
            rows_ref[me] = att[me]
            each(lambda d: carry_rows(d).start(), last=count)
        for way in ring.ways(s):
            block = ring.device(-way * (s + 1))
            block_maps(done, q_all.at[block], k_all.at[block], block)
            done += 1
        for way in ring.ways(s):
            block = ring.device(-way * (s + 1)) + 1 - 2 * core
            ring.take(way, s)
            block_maps(done, q_all.at[block], k_all.at[block], block)
            done += 1
    ring.finish()
    store(done - 2, me).wait()
    store(done - 1, me).wait()
    pair.wait_send()
    each(lambda d: hand_side(d).wait_recv(), 0)
    each(lambda d: hand_side(d).wait_send(), 0)
    each(lambda d: scatter(d).wait_send())
    each(lambda d: spread(d).wait_send())
    each(lambda d: carry_rows(d).wait_recv(), last=count)
    each(lambda d: carry_rows(d).wait_send(), last=count)


def attend_and_gather(count, across, eyes, operands, weights, cos_table, sin_table):
    block, _, w_out, w_side, _, w_tri, w_map, bins = operands
    channels = w_tri.shape[1]
    length, width = cos_table.shape
    rows = block.shape[0]
    terms = [e + w_map.shape[0] + bins.shape[0] for e in eyes]
    vmem = pl.BlockSpec(memory_space=pltpu.VMEM)
    queries, keys, own = (count, rows, width), (width, length), (rows, 2 * channels)
    sides = (count // 2,) + own
    piece = (width // HD, length // 2 + rows, length)
    shapes = [
        (count,) + piece,
        (count,) + own,
        queries,
        (3 * channels, channels),
        (3 * channels, terms[0] + channels),
        (4 * channels, channels),
        (4 * channels, terms[1] + channels),
        (channels, terms[1]),
    ]
    scratch = [
        block.shape,
        (count,) + block.shape,
        queries,
        keys,
        (length, width),
        (count,) + queries,
        (count,) + keys,
        (2,) + sides,
        sides,
        sides,
        own,
        (2,) + piece,
        queries,
    ]
    return pl.pallas_call(
        functools.partial(attend_kernel, count, across, eyes),
        out_shape=[jax.ShapeDtypeStruct(shape, jnp.bfloat16) for shape in shapes],
        in_specs=[vmem] * (len(operands) + 3),
        out_specs=[pl.BlockSpec(memory_space=pl.ANY)] + [vmem] * 7,
        scratch_shapes=[
            pltpu.VMEM((w_out.shape[0], 2 * channels), jnp.bfloat16),
            pltpu.VMEM(own, jnp.float32),
        ]
        + [pltpu.VMEM(shape, jnp.bfloat16) for shape in scratch]
        + [pltpu.SemaphoreType.DMA((1, count))] * 2
        + [pltpu.SemaphoreType.DMA((2, count))] * 2
        + [pltpu.SemaphoreType.DMA((2,))]
        + [pltpu.SemaphoreType.DMA((count // 2,))] * 6
        + [pltpu.SemaphoreType.DMA((2,))]
        + [pltpu.SemaphoreType.DMA((count,))] * 2,
        compiler_params=pltpu.CompilerParams(
            collective_id=0, has_side_effects=True, vmem_limit_bytes=VMEM_BYTES
        ),
        name="attend_and_gather",
    )(*operands, weights, cos_table, sin_table)


def places_of(rows, width):
    places = lax.broadcasted_iota(jnp.int32, (rows, width), 0)
    return places.astype(jnp.float32).astype(jnp.bfloat16)


def hot_rows(places, index):
    index = index.astype(jnp.float32).astype(jnp.bfloat16)
    return jnp.where(places == index, jnp.ones((), jnp.bfloat16), jnp.zeros((), jnp.bfloat16))


def edges_kernel(
    own, row_index, maps_ref, left_ref, fold_ref, mix_ref, low_ref, right_ref, cols_ref, *rest
):
    scratch, full_ref, probs_ref = rest[-3:]
    heads, block, length = maps_ref.shape
    channels = right_ref.shape[0]
    eye_rows = mix_ref.shape[1] - channels - heads - BIN_ROWS
    pitch = channels + 1
    width = 2 * LANES
    reach = (BINS - 1) // 2
    first = pl.program_id(0) * block

    lefts = jnp.concatenate(
        [left_ref[...], jnp.zeros((LANES - block, channels), jnp.bfloat16)], axis=0
    )
    folded = lax.dot_general(
        fold_ref[...], lefts, (((1,), (1,)), ((), ())), preferred_element_type=jnp.float32
    )
    full_ref[:, :LANES] = (folded + mix_ref[:, :LANES].astype(jnp.float32)).astype(jnp.bfloat16)
    full_ref[:, LANES:] = mix_ref[:, LANES:]

    def one_head(h, carry):
        for n in range(length // LANES):
            probs_ref[n, pl.ds(h * (block + 1), block), :] = maps_ref[
                h, :, n * LANES : (n + 1) * LANES
            ].astype(jnp.float32)
        return carry

    lax.fori_loop(0, heads, one_head, 0, unroll=8)

    def one_row(j, carry):
        here = row_index[first + j]
        eye = hot_rows(places_of(eye_rows, width), jnp.broadcast_to(j, (1, width)))
        for n in range(length // width):
            cols = slice(n * width, (n + 1) * width)
            bins = jnp.clip(cols_ref[:, cols] - here, -reach, reach) + reach
            hot = hot_rows(places_of(BIN_ROWS, width), bins)
            probs = [
                probs_ref[m, pl.ds(j, heads, stride=block + 1), :].astype(jnp.bfloat16)
                for m in range(n * width // LANES, (n + 1) * width // LANES)
            ]
            probs = jnp.concatenate(probs, axis=1)
            terms = jnp.concatenate([eye, probs, hot, right_ref[:, cols]], axis=0)
            mixed = jnp.dot(
                full_ref[: 3 * channels], terms, preferred_element_type=jnp.float32
            )
            centered = mixed[:channels]
            if own:
                pair = centered + jnp.dot(
                    low_ref[...],
                    jnp.concatenate([eye, probs, hot], axis=0),
                    preferred_element_type=jnp.float32,
                )
                rest[2][j, :, cols] = pair.astype(jnp.bfloat16)
                centered = pair - jnp.sum(pair, axis=0, keepdims=True) * (1.0 / channels)
            variance = jnp.sum(centered * centered, axis=0, keepdims=True) * (1.0 / channels)
            scale = lax.rsqrt(variance + 1e-05)
            value = mixed[channels : 2 * channels] * scale
            edge = value + value * jnp.tanh(mixed[2 * channels : 3 * channels] * scale)
            start = j * pitch
            for m in range(width // LANES):
                scratch[n * (width // LANES) + m, pl.ds(start, channels), :] = edge[
                    :, m * LANES : (m + 1) * LANES
                ]
            if own:
                gated = jnp.dot(
                    full_ref[3 * channels :], terms, preferred_element_type=jnp.float32
                )
                gate = 0.5 + 0.5 * jnp.tanh(gated * scale)
                rest[3][j, :, cols] = gate.astype(jnp.bfloat16)
        return carry

    lax.fori_loop(0, block, one_row, 0, unroll=min(16, block))
    half = channels // 2

    def one_channel(c, carry):
        for n in range(length // LANES):
            for side in range(2):
                rows_of = scratch[n, pl.ds(c + side * half, block, stride=pitch), :]
                rest[side][c, :, n * LANES : (n + 1) * LANES] = rows_of.astype(jnp.bfloat16)
        return carry

    lax.fori_loop(0, half, one_channel, 0, unroll=16)


def edges(own, row_index, maps, left, fold, mix, low, right, cols, block, skip, rows):
    heads, _, length = maps.shape
    channels = right.shape[0]
    half = channels // 2
    out_shape = [jax.ShapeDtypeStruct((half, rows, length), jnp.bfloat16)] * 2
    out_specs = [pl.BlockSpec((half, block, length), lambda b, s: (0, b, 0))] * 2
    if own:
        out_shape += [jax.ShapeDtypeStruct((rows, channels, length), jnp.bfloat16)] * 2
        out_specs += [pl.BlockSpec((block, channels, length), lambda b, s: (b, 0, 0))] * 2
    first = skip // block
    whole = [pl.BlockSpec(a.shape, lambda b, s: (0, 0)) for a in (fold, mix, low, right, cols)]
    return pl.pallas_call(
        functools.partial(edges_kernel, own),
        out_shape=out_shape,
        grid_spec=pltpu.PrefetchScalarGridSpec(
            num_scalar_prefetch=1,
            grid=(rows // block,),
            in_specs=[
                pl.BlockSpec((heads, block, length), lambda b, s: (0, b + first, 0)),
                pl.BlockSpec((block, channels), lambda b, s: (b, 0)),
            ]
            + whole,
            out_specs=out_specs,
            scratch_shapes=[
                pltpu.VMEM((length // LANES, block * (channels + 1) + 7, LANES), jnp.float32),
                pltpu.VMEM(mix.shape, jnp.bfloat16),
                pltpu.VMEM((length // LANES, heads * (block + 1) + 7, LANES), jnp.float32),
            ],
        ),
        compiler_params=pltpu.CompilerParams(vmem_limit_bytes=VMEM_BYTES),
        cost_estimate=pl.CostEstimate(
            flops=2 * rows * length * channels * 800,
            bytes_accessed=2 * rows * length * channels,
            transcendentals=rows * length * channels,
        ),
        name="own_edges" if own else "right_edges",
    )(row_index, maps, left, fold, mix, low, right, cols)


def products_kernel(keep_ref, arrive_ref, *refs):
    parts, (mine_ref, theirs_ref) = refs[:-2], refs[-2:]
    count, rows, _ = keep_ref.shape
    for c in range(count):
        lefts = jnp.concatenate([keep_ref[c], arrive_ref[c]], axis=0)
        for p, part in enumerate(parts):
            out = lax.dot_general(
                lefts, part[c], (((1,), (1,)), ((), ())), preferred_element_type=jnp.float32
            ).astype(jnp.bfloat16)
            mine_ref[p, c] = out[:rows]
            theirs_ref[p, c] = out[rows:]


def edge_products(keep, arrive, parts):
    half, rows, length = keep.shape
    each = parts[0].shape[1]
    count = 8 if half % 8 == 0 else 1
    out = jax.ShapeDtypeStruct((len(parts), half, rows, each), jnp.bfloat16)
    return pl.pallas_call(
        products_kernel,
        out_shape=[out] * 2,
        grid=(half // count,),
        in_specs=[pl.BlockSpec((count, rows, length), lambda b: (b, 0, 0))] * 2
        + [pl.BlockSpec((count, each, length), lambda b: (b, 0, 0))] * len(parts),
        out_specs=[pl.BlockSpec((len(parts), count, rows, each), lambda b: (0, b, 0, 0))] * 2,
        compiler_params=pltpu.CompilerParams(vmem_limit_bytes=VMEM_BYTES),
        cost_estimate=pl.CostEstimate(
            flops=4 * half * rows * len(parts) * each * length,
            bytes_accessed=2 * half * len(parts) * each * length,
            transcendentals=0,
        ),
        name="edge_products",
    )(keep, arrive, *parts)


def final_kernel(core, *refs):
    sources = refs[:4]
    pair_ref, gate_ref, gain_ref, w_ref, out_ref, scratch = refs[4:]
    half, block, width = sources[0].shape[1:]
    early = pl.program_id(1) < pl.num_programs(1) // 2

    def fill(n, ref):
        def one_channel(c, carry):
            scratch[n, pl.ds(c * (block + 1), block), :] = ref[0, c].astype(jnp.float32)
            return carry

        lax.fori_loop(0, half, one_channel, 0, unroll=8)

    for n in range(2):
        pl.when(early)(functools.partial(fill, n, sources[2 * n]))
        pl.when(jnp.logical_not(early))(functools.partial(fill, n, sources[2 * n + 1]))

    def one_row(i, carry):
        products = jnp.concatenate(
            [scratch[n, pl.ds(i, half, stride=block + 1), :] for n in range(2)], axis=0
        )
        center = jnp.mean(products, axis=0, keepdims=True)
        centered = products - center
        variance = jnp.mean(centered * centered, axis=0, keepdims=True)
        normed = (centered * lax.rsqrt(variance + 1e-05) * gain_ref[...]).astype(jnp.bfloat16)
        projected = jnp.dot(w_ref[...], normed, preferred_element_type=jnp.float32)
        total = pair_ref[i].astype(jnp.float32) + gate_ref[i].astype(jnp.float32) * projected
        out_ref[i] = total.T.astype(jnp.bfloat16)
        return carry

    lax.fori_loop(0, block, one_row, 0, unroll=16)


def finish(core, products, pair, gate, gain, weights, block):
    each, half, rows, width = products[0].shape
    pieces = 2 * each
    _, channels, length = pair.shape

    def column(u, core):
        side = u // each
        return (side + core[0] - 2 * side * core[0]) * each + u % each

    def early(b, u, s):
        return jnp.minimum(u, each - 1), 0, b, 0

    def late(b, u, s):
        return jnp.maximum(u - each, 0), 0, b, 0

    return pl.pallas_call(
        final_kernel,
        out_shape=jax.ShapeDtypeStruct((rows, length, channels), jnp.bfloat16),
        grid_spec=pltpu.PrefetchScalarGridSpec(
            num_scalar_prefetch=1,
            grid=(rows // block, pieces),
            in_specs=[
                pl.BlockSpec((1, half, block, width), early),
                pl.BlockSpec((1, half, block, width), late),
                pl.BlockSpec((1, half, block, width), early),
                pl.BlockSpec((1, half, block, width), late),
                pl.BlockSpec((block, channels, width), lambda b, u, s: (b, 0, column(u, s))),
                pl.BlockSpec((block, channels, width), lambda b, u, s: (b, 0, column(u, s))),
                pl.BlockSpec(gain.shape, lambda b, u, s: (0, 0)),
                pl.BlockSpec(weights.shape, lambda b, u, s: (0, 0)),
            ],
            out_specs=pl.BlockSpec((block, width, channels), lambda b, u, s: (b, column(u, s), 0)),
            scratch_shapes=[pltpu.VMEM((2, half * (block + 1) + 7, width), jnp.float32)],
        ),
        compiler_params=pltpu.CompilerParams(vmem_limit_bytes=VMEM_BYTES),
        name="finish",
    )(core, *products, pair, gate, gain, weights)


def per_device(
    across,
    hidden_in,
    ln_gain,
    w_qkv,
    w_out,
    residue_index,
    w_map,
    relpos_table,
    w_side,
    tri_gain,
    w_tri,
    w_tri_out,
):
    local_rows = hidden_in.shape[0]
    devices_mp = lax.axis_size("mp")
    me = lax.axis_index("mp")
    core = lax.rem(me, 2)
    length = local_rows * devices_mp
    local_heads = w_qkv.shape[2] // HD
    heads, channels = w_map.shape
    swap = [(d, d ^ 1) for d in range(devices_mp)]
    half_rows = length // 2
    each = half_rows // CHUNKS
    block = 16 if local_rows % 16 == 0 else local_rows
    r_block = 16 if each % 16 == 0 else each
    turn = -core * (channels // 2)
    cos_table, sin_table = rotary_tables(length, local_heads)
    operands = (
        hidden_in,
        ln_gain[None],
        w_out,
        w_side,
        tri_gain,
        w_tri,
        w_map,
        jnp.pad(relpos_table, ((0, BIN_ROWS - relpos_table.shape[0]), (0, 0))),
    )
    maps, all_sides, att_rows, right_fold, right_mix, left_fold, left_mix, low = attend_and_gather(
        devices_mp,
        across,
        tuple(-(-b // 16) * 16 for b in (r_block, block)),
        operands,
        w_qkv,
        cos_table,
        sin_table,
    )
    maps = maps.reshape(heads, half_rows + local_rows, length)
    out_part, all_sides, att_rows = lax.optimization_barrier((w_out, all_sides, att_rows))
    full_out = lax.all_gather(out_part, "mp", axis=0)

    row_start = me * local_rows
    half_start = core * half_rows
    all_sides = all_sides.reshape(length, 2 * channels)
    left_rows = all_sides[:, :channels]
    right = all_sides[:, channels:].T

    cols = residue_index[None, :]

    half_left = lax.dynamic_slice_in_dim(left_rows, half_start, half_rows, 0)
    half_index = lax.dynamic_slice_in_dim(residue_index, half_start, half_rows, 0)
    left_keep, left_send, pair, gate = edges(
        True,
        lax.dynamic_slice_in_dim(residue_index, row_start, local_rows, 0),
        maps,
        lax.dynamic_slice_in_dim(left_rows, row_start, local_rows, 0),
        left_fold,
        left_mix,
        low,
        right,
        cols,
        block,
        half_rows,
        local_rows,
    )
    left_send, half_index = lax.optimization_barrier((left_send, half_index))
    left_arrive = lax.ppermute(left_send, "mp", swap)
    kept, arriving = [], []
    for n in range(CHUNKS):
        part = slice(n * each, (n + 1) * each)
        if n == 1:
            left_arrive, half_index = lax.optimization_barrier((left_arrive, half_index))
        keep, send = edges(
            False,
            half_index[part],
            maps,
            half_left[part],
            right_fold,
            right_mix,
            low,
            right,
            cols,
            r_block,
            n * each,
            each,
        )
        kept.append(keep)
        arriving.append(lax.ppermute(send, "mp", swap))
    mine_kept, theirs_kept = edge_products(left_keep, left_arrive, kept)
    theirs_kept = lax.ppermute(theirs_kept, "mp", swap)
    mine_other, theirs_other = edge_products(left_keep, left_arrive, arriving)
    theirs_other = lax.ppermute(theirs_other, "mp", swap)
    pair_out = finish(
        core[None],
        (mine_kept, mine_other, theirs_other, theirs_kept),
        pair,
        gate,
        jnp.broadcast_to(jnp.roll(tri_gain[1], turn)[:, None], (channels, each)),
        jnp.roll(w_tri_out, turn, axis=0).T,
        local_rows,
    )
    attended_rows = att_rows.transpose(1, 0, 2).reshape(local_rows, -1)
    mixed = jnp.dot(
        attended_rows, full_out.reshape(-1, full_out.shape[-1]), preferred_element_type=jnp.float32
    )
    hidden_out = (hidden_in.astype(jnp.float32) + mixed).astype(jnp.bfloat16)
    return (hidden_out, pair_out)


def solution(mesh):
    placed = (
        P(("groups", "mp"), None),
        P(),
        P(None, None, "mp"),
        P("mp", None),
        P("groups"),
        P(),
        P(),
        P(),
        P(),
        P(),
        P(),
    )
    chips = [d.coords for d in mesh.devices.reshape(-1, mesh.shape["mp"])[0][::2] if hasattr(d, "coords")]
    across = 1
    if len(chips) > 3 and sum(abs(p - q) for p, q in zip(chips[0], chips[2])) == 1:
        across = 2
    return jax.shard_map(
        functools.partial(per_device, across),
        mesh=mesh,
        in_specs=placed,
        out_specs=(P(("groups", "mp"), None), P(("groups", "mp"), None, None)),
        check_vma=False,
    )
```

```python
import functools

import jax
import jax.numpy as jnp
import numpy as np
from jax import lax
from jax.experimental import pallas as pl
from jax.experimental.pallas import tpu as pltpu
from jax.sharding import PartitionSpec as P

HD = 64
BINS = 65
BIN_ROWS = 80
LANES = 128
CHUNKS = 3
VMEM_BYTES = 60 * 1024 * 1024
MESH = pl.DeviceIdType.MESH
EXACT = lax.Precision.HIGHEST


def layer_norm(tensor, gain_vec, norm_axis):
    center = jnp.mean(tensor, axis=norm_axis, keepdims=True)
    centered = tensor - center
    variance = jnp.mean(centered * centered, axis=norm_axis, keepdims=True)
    return centered * lax.rsqrt(variance + 1e-05) * gain_vec


def rotary_tables(length, heads):
    powers = np.arange(0, HD, 2, dtype=np.float32) / np.float32(HD)
    inv_freq = np.float32(1.0) / np.power(np.float32(10000.0), powers)
    angles = np.arange(length, dtype=np.float32)[:, None] * inv_freq[None, :]
    cos, sin = np.cos(angles), np.sin(angles)
    return (
        jnp.asarray(np.tile(np.concatenate([cos, cos], axis=1), (1, heads)), jnp.float32),
        jnp.asarray(np.tile(np.concatenate([-sin, sin], axis=1), (1, heads)), jnp.float32),
    )


class Ring:
    def __init__(self, count, across, arrays, send, recv):
        self.arrays, self.send, self.recv = arrays, send, recv
        self.count, self.across, self.chips = count, across, count // 2
        self.ahead = self.chips // 2
        self.back = self.chips - 1 - self.ahead
        self.me = lax.axis_index("mp")
        self.core = lax.rem(self.me, 2)
        self.place = self.position(lax.div(self.me, 2))

    def position(self, chip):
        if self.across == 1:
            return chip
        z, y = lax.div(chip, 2), lax.rem(chip, 2)
        return z + y * (self.chips - 1 - 2 * z)

    def device(self, shift):
        place = lax.rem(self.place + self.chips + shift, self.chips)
        if self.across == 1:
            return 2 * place + self.core
        y = lax.div(place, self.chips // 2)
        z = place + y * (self.chips - 1 - 2 * place)
        return 2 * (2 * z + y) + self.core

    def twin(self):
        return self.me + 1 - 2 * self.core

    def copy(self, a, block, own, slot, target, part=None):
        src, out, axis = self.arrays[a]
        piece = ()
        if part is not None:
            size = src.shape[axis] // 2
            piece = (slice(None),) * axis + (pl.ds(part * size, size),)
        target_ref = out.at[(block,) + piece]
        source_ref = (src.at[piece] if piece else src) if own else target_ref
        return pltpu.make_async_remote_copy(
            src_ref=source_ref,
            dst_ref=target_ref,
            send_sem=self.send.at[a, slot],
            recv_sem=self.recv.at[a, slot],
            device_id={"mp": target},
            device_id_type=MESH,
        )

    def hop(self, a, way, step):
        slot = step if way > 0 else self.ahead + step
        part = None
        if self.back < self.ahead and step == self.back:
            part = 0 if way > 0 else 1
        block = self.device(-way * step)
        return self.copy(a, block, step == 0, slot, self.device(way), part)

    def hand(self, a, way, step):
        if way == 0:
            return self.copy(a, self.me, True, self.chips, self.twin())
        slot = self.chips + 1 + (step if way > 0 else self.ahead + step)
        return self.copy(a, self.device(-way * (step + 1)), False, slot, self.twin())

    def start(self):
        for a in range(len(self.arrays)):
            for way in (1, -1):
                self.hop(a, way, 0).start()
            self.hand(a, 0, 0).start()

    def steps(self):
        return self.ahead

    def ways(self, s):
        return [way for way, most in ((1, self.ahead), (-1, self.back)) if s < most]

    def step(self, s):
        for a in range(len(self.arrays)):
            for way in (1, -1):
                self.hop(a, way, s).wait_recv()
                if s + 1 < self.ahead:
                    self.hop(a, way, s + 1).start()
                if self.ways(s) == [1, -1]:
                    self.hand(a, way, s).start()
            if self.ways(s) == [1]:
                self.hand(a, 1, s).start()

    def take(self, way, s):
        for a in range(len(self.arrays)):
            self.hand(a, way, s).wait_recv()

    def finish(self):
        for a in range(len(self.arrays)):
            self.hand(a, 0, 0).wait_send()
            for s in range(self.ahead):
                for way in (1, -1):
                    self.hop(a, way, s).wait_send()
                for way in self.ways(s):
                    self.hand(a, way, s).wait_send()


def greet_all(count):
    me = lax.axis_index("mp")
    barrier = pltpu.get_barrier_semaphore()

    def greet(d, carry):
        pl.semaphore_signal(
            barrier, inc=1, device_id={"mp": lax.rem(me + d, count)}, device_id_type=MESH
        )
        return carry

    lax.fori_loop(1, count, greet, 0)
    pl.semaphore_wait(barrier, count - 1)


def gather_part(count, across, eyes, operands, outs, bins, normed, x_all, send, recv):
    x_ref, gain_ref, w_out_ref, w_side_ref, tri_gain_ref, tri_ref, map_ref, bins_ref = operands
    side_ref, own_ref, r_fold, r_mix, l_fold, l_mix, low_ref = outs
    me = lax.axis_index("mp")
    core = lax.rem(me, 2)
    greet_all(count)
    hidden = x_ref[...].astype(jnp.float32)
    normed[...] = layer_norm(hidden, gain_ref[...], -1).astype(jnp.bfloat16)
    x_all[me] = normed[...]
    ring = Ring(count, across, [(normed, x_all, 1)], send, recv)
    ring.start()

    channels = tri_ref.shape[1]
    for s in range(2):
        cols = slice(s * channels, (s + 1) * channels)
        own_ref[:, cols] = jnp.dot(
            x_ref[...], w_side_ref[s], preferred_element_type=jnp.float32
        )
        side_ref[:, cols] = jnp.dot(
            w_out_ref[...], w_side_ref[s], preferred_element_type=jnp.float32
        ).astype(jnp.bfloat16)
    ring.step(0)

    row = lax.broadcasted_iota(jnp.int32, (channels, channels), 0)
    column = lax.broadcasted_iota(jnp.int32, (channels, channels), 1)
    identity = jnp.where(row == column, 1.0, 0.0)
    center = identity - 1.0 / channels
    half = channels // 2
    length = x_ref.shape[0] * count
    maps = map_ref[...].astype(jnp.float32) * length
    bins[...] = jnp.zeros_like(bins)
    bins[: bins_ref.shape[0], :] = bins_ref[...]
    bins = bins[...]

    def gated(p, turned):
        weights = tri_ref[p].astype(jnp.float32).T * (0.5 * tri_gain_ref[0:1, :])
        if turned:
            other = jnp.concatenate([weights[half:], weights[:half]], axis=0)
            weights = jnp.where(core == 0, weights, other)
        return jnp.dot(weights, center, precision=EXACT, preferred_element_type=jnp.float32)

    def across_terms(fold, parts, eye_rows):
        rows = jnp.concatenate([jnp.zeros((eye_rows, channels), jnp.float32)] + parts, axis=0)
        return lax.dot_general(
            fold,
            rows,
            (((1,), (1,)), ((), ())),
            precision=EXACT,
            preferred_element_type=jnp.float32,
        ).astype(jnp.bfloat16)

    fold = jnp.concatenate([center, gated(2, True), gated(3, True)], axis=0)
    r_fold[...] = fold.astype(jnp.bfloat16)
    r_mix[...] = across_terms(fold, [maps, bins, identity], eyes[0])
    for s in range(1, ring.steps()):
        ring.step(s)
        if s == 1:
            fold = jnp.concatenate(
                [identity, gated(0, True), gated(1, True), gated(4, False)], axis=0
            )
            l_fold[...] = fold.astype(jnp.bfloat16)
            l_mix[...] = across_terms(fold, [maps, bins, identity], eyes[1])
            low = [v - v.astype(jnp.bfloat16).astype(jnp.float32) for v in (maps, bins)]
            low_ref[...] = across_terms(identity, low, eyes[1])
    ring.take(0, 0)
    for s in range(ring.steps()):
        for way in ring.ways(s):
            ring.take(way, s)
    ring.finish()


def attend_kernel(count, across, eyes, *refs):
    operands, refs = refs[:8], refs[8:]
    w_ref, cos_ref, sin_ref = refs[:3]
    maps_ref, out_ref, rows_ref = refs[3:6]
    outs, rest = refs[6:11], refs[11:]
    mix_ref, own_ref, normed, x_all = rest[:4]
    q_ref, k_ref, v_ref, q_all, k_all, parts, paired, landed, mine, stage = rest[4:14]
    att, first_send, first_recv, send, recv, pair_sems = rest[14:20]
    send_a, recv_a, send_b, recv_b, send_c, recv_c, stored, send_d, recv_d = rest[20:-1]
    gather_part(
        count,
        across,
        eyes,
        operands,
        (mix_ref, own_ref) + tuple(outs),
        rest[-1],
        normed,
        x_all,
        first_send,
        first_recv,
    )
    me = lax.axis_index("mp")
    core, chip, chips = lax.rem(me, 2), lax.div(me, 2), count // 2
    twin = me + 1 - 2 * core
    width, length = k_ref.shape
    rows = length // count
    half = count // 2
    turn = HD // 2
    heads = [slice(h * HD, (h + 1) * HD) for h in range(width // HD)]

    def rotated(tensor, where):
        turned = []
        for h in range(0, width, HD):
            turned += [tensor[:, h + turn : h + HD], tensor[:, h : h + turn]]
        turned = jnp.concatenate(turned, axis=1)
        return tensor * cos_ref[where, :] + turned * sin_ref[where, :]

    def softmax(scores):
        powers = jnp.exp(scores - jnp.max(scores, axis=-1, keepdims=True))
        probs = powers * (1.0 / jnp.sum(powers, axis=-1, keepdims=True))
        return probs.astype(jnp.bfloat16)

    span = length // 2
    for r in range(2):
        where = slice(r * span, (r + 1) * span)
        both = jnp.dot(
            x_all[r * half : (r + 1) * half].reshape(span, x_all.shape[2]),
            jnp.concatenate([w_ref[0], w_ref[1]], axis=1),
            preferred_element_type=jnp.float32,
        )
        queries = rotated(both[:, :width] * HD**-0.5, where).astype(jnp.bfloat16)
        k_ref[:, where] = rotated(both[:, width:], where).T.astype(jnp.bfloat16)
        for b in range(half):
            q_ref[r * half + b] = queries[b * rows : (b + 1) * rows]
    ring = Ring(count, across, [(k_ref, k_all, 0), (q_ref, q_all, 0)], send, recv)
    ring.start()
    v_ref[...] = jnp.dot(
        x_all[...].reshape(length, x_all.shape[2]), w_ref[2], preferred_element_type=jnp.float32
    ).astype(jnp.bfloat16)
    group = 4

    def one_group(g, carry):
        queries = q_ref[pl.ds(g * group, group)].reshape(group * rows, width)
        found = []
        for head in heads:
            scores = jnp.dot(queries[:, head], k_ref[head, :], preferred_element_type=jnp.float32)
            found.append(
                jnp.dot(softmax(scores), v_ref[:, head], preferred_element_type=jnp.float32)
            )
        found = jnp.concatenate(found, axis=1).astype(jnp.bfloat16)
        part = jnp.dot(found, mix_ref[...], preferred_element_type=jnp.float32)
        part = part.astype(jnp.bfloat16)
        for b in range(group):
            att[g * group + b] = found[b * rows : (b + 1) * rows]
            parts[b % 2, g * (group // 2) + b // 2] = part[b * rows : (b + 1) * rows]
        return carry

    lax.fori_loop(0, count // group, one_group, 0)

    pair = pltpu.make_async_remote_copy(
        src_ref=parts.at[1 - core],
        dst_ref=paired,
        send_sem=pair_sems.at[0],
        recv_sem=pair_sems.at[1],
        device_id={"mp": twin},
        device_id_type=MESH,
    )
    pair.start()

    def store(i, block):
        return pltpu.make_async_copy(stage.at[i % 2], maps_ref.at[block], stored.at[i % 2])

    def block_maps(i, queries_of, keys_of, block):
        slot = i % 2
        if i >= 2:
            store(i, block).wait()

        def fill(queries, start, size):
            queries = queries.reshape(size, width)
            for h, head in enumerate(heads):
                scores = jnp.dot(
                    queries[:, head], keys_of[head, :], preferred_element_type=jnp.float32
                )
                stage[slot, h, pl.ds(start, size), :] = softmax(scores)

        def one_pair(g, carry):
            start = pl.multiple_of(g * 2 * rows, 16)
            fill(queries_of[pl.ds(core * half + 2 * g, 2)], start, 2 * rows)
            return carry

        lax.fori_loop(0, half // 2, one_pair, 0)
        fill(queries_of[pl.ds(me, 1)], half * rows, rows)
        store(i, block).start()

    block_maps(0, q_ref, k_ref, me)

    def scatter(d):
        target = lax.rem(chip + d, chips)
        return pltpu.make_async_remote_copy(
            src_ref=paired.at[target],
            dst_ref=landed.at[d],
            send_sem=send_a.at[d],
            recv_sem=recv_a.at[d],
            device_id={"mp": 2 * target + core},
            device_id_type=MESH,
        )

    def spread(d):
        return pltpu.make_async_remote_copy(
            src_ref=mine,
            dst_ref=out_ref.at[me],
            send_sem=send_b.at[d],
            recv_sem=recv_b.at[d],
            device_id={"mp": 2 * lax.rem(chip + d, chips) + core},
            device_id_type=MESH,
        )

    def hand_side(d):
        source = 2 * lax.rem(chip + chips - d, chips) + core
        return pltpu.make_async_remote_copy(
            src_ref=out_ref.at[source],
            dst_ref=out_ref.at[source],
            send_sem=send_c.at[d],
            recv_sem=recv_c.at[d],
            device_id={"mp": twin},
            device_id_type=MESH,
        )

    def each(step, first=1, last=chips):
        def run(d, carry):
            step(d)
            return carry

        lax.fori_loop(first, last, run, 0)

    def carry_rows(d):
        target = lax.rem(me + d, count)
        return pltpu.make_async_remote_copy(
            src_ref=att.at[target],
            dst_ref=rows_ref.at[me],
            send_sem=send_d.at[d],
            recv_sem=recv_d.at[d],
            device_id={"mp": target},
            device_id_type=MESH,
        )

    pair.wait_recv()

    def join(d):
        both = paired[d].astype(jnp.float32) + parts[core, d].astype(jnp.float32)
        paired[d] = both.astype(jnp.bfloat16)

    each(join, 0)
    each(lambda d: scatter(d).start())
    ring.take(0, 0)
    block_maps(1, q_all.at[twin], k_all.at[twin], twin)
    done = 2
    for s in range(ring.steps()):
        ring.step(s)
        if s == 0:

            def add(d, total):
                scatter(d).wait_recv()
                return total + landed[d].astype(jnp.float32)

            total = own_ref[...] + paired[chip].astype(jnp.float32)
            total = lax.fori_loop(1, chips, add, total).astype(jnp.bfloat16)
            mine[...] = total
            out_ref[me] = total
            each(lambda d: spread(d).start())
            hand_side(0).start()
        if s == min(1, ring.steps() - 1):

            def forward(d):
                spread(d).wait_recv()
                hand_side(d).start()

            each(forward)
        if s == ring.steps() - 1:
            rows_ref[me] = att[me]
            each(lambda d: carry_rows(d).start(), last=count)
        for way in ring.ways(s):
            block = ring.device(-way * (s + 1))
            block_maps(done, q_all.at[block], k_all.at[block], block)
            done += 1
        for way in ring.ways(s):
            block = ring.device(-way * (s + 1)) + 1 - 2 * core
            ring.take(way, s)
            block_maps(done, q_all.at[block], k_all.at[block], block)
            done += 1
    ring.finish()
    store(done - 2, me).wait()
    store(done - 1, me).wait()
    pair.wait_send()
    each(lambda d: hand_side(d).wait_recv(), 0)
    each(lambda d: hand_side(d).wait_send(), 0)
    each(lambda d: scatter(d).wait_send())
    each(lambda d: spread(d).wait_send())
    each(lambda d: carry_rows(d).wait_recv(), last=count)
    each(lambda d: carry_rows(d).wait_send(), last=count)


def attend_and_gather(count, across, eyes, operands, weights, cos_table, sin_table):
    block, _, w_out, w_side, _, w_tri, w_map, bins = operands
    channels = w_tri.shape[1]
    length, width = cos_table.shape
    rows = block.shape[0]
    terms = [e + w_map.shape[0] + BIN_ROWS for e in eyes]
    vmem = pl.BlockSpec(memory_space=pltpu.VMEM)
    queries, keys, own = (count, rows, width), (width, length), (rows, 2 * channels)
    sides = (count // 2,) + own
    piece = (width // HD, length // 2 + rows, length)
    shapes = [
        (count,) + piece,
        (count,) + own,
        queries,
        (3 * channels, channels),
        (3 * channels, terms[0] + channels),
        (4 * channels, channels),
        (4 * channels, terms[1] + channels),
        (channels, terms[1]),
    ]
    scratch = [
        block.shape,
        (count,) + block.shape,
        queries,
        keys,
        (length, width),
        (count,) + queries,
        (count,) + keys,
        (2,) + sides,
        sides,
        sides,
        own,
        (2,) + piece,
        queries,
    ]
    return pl.pallas_call(
        functools.partial(attend_kernel, count, across, eyes),
        out_shape=[jax.ShapeDtypeStruct(shape, jnp.bfloat16) for shape in shapes],
        in_specs=[vmem] * (len(operands) + 3),
        out_specs=[pl.BlockSpec(memory_space=pl.ANY)] + [vmem] * 7,
        scratch_shapes=[
            pltpu.VMEM((w_out.shape[0], 2 * channels), jnp.bfloat16),
            pltpu.VMEM(own, jnp.float32),
        ]
        + [pltpu.VMEM(shape, jnp.bfloat16) for shape in scratch]
        + [pltpu.SemaphoreType.DMA((1, count))] * 2
        + [pltpu.SemaphoreType.DMA((2, count))] * 2
        + [pltpu.SemaphoreType.DMA((2,))]
        + [pltpu.SemaphoreType.DMA((count // 2,))] * 6
        + [pltpu.SemaphoreType.DMA((2,))]
        + [pltpu.SemaphoreType.DMA((count,))] * 2
        + [pltpu.VMEM((BIN_ROWS, channels), jnp.float32)],
        compiler_params=pltpu.CompilerParams(
            collective_id=0, has_side_effects=True, vmem_limit_bytes=VMEM_BYTES
        ),
        name="attend_and_gather",
    )(*operands, weights, cos_table, sin_table)


def places_of(rows, width):
    places = lax.broadcasted_iota(jnp.int32, (rows, width), 0)
    return places.astype(jnp.float32).astype(jnp.bfloat16)


def hot_rows(places, index):
    index = index.astype(jnp.float32).astype(jnp.bfloat16)
    return jnp.where(places == index, jnp.ones((), jnp.bfloat16), jnp.zeros((), jnp.bfloat16))


def edges_kernel(
    own, row_index, start_ref, maps_ref, left_ref, fold_ref, mix_ref, low_ref, right_ref, cols_ref, *rest
):
    scratch, full_ref, probs_ref = rest[-3:]
    heads, block, length = maps_ref.shape
    channels = right_ref.shape[0]
    eye_rows = mix_ref.shape[1] - channels - heads - BIN_ROWS
    pitch = channels + 1
    width = 2 * LANES
    reach = (BINS - 1) // 2
    first = start_ref[0] + pl.program_id(0) * block

    lefts = jnp.concatenate(
        [left_ref[...], jnp.zeros((LANES - block, channels), jnp.bfloat16)], axis=0
    )
    folded = lax.dot_general(
        fold_ref[...], lefts, (((1,), (1,)), ((), ())), preferred_element_type=jnp.float32
    )
    full_ref[:, :LANES] = (folded + mix_ref[:, :LANES].astype(jnp.float32)).astype(jnp.bfloat16)
    full_ref[:, LANES:] = mix_ref[:, LANES:]

    def one_head(h, carry):
        for n in range(length // LANES):
            probs_ref[n, pl.ds(h * (block + 1), block), :] = maps_ref[
                h, :, n * LANES : (n + 1) * LANES
            ].astype(jnp.float32)
        return carry

    lax.fori_loop(0, heads, one_head, 0, unroll=8)

    def one_row(j, carry):
        here = row_index[first + j]
        eye = hot_rows(places_of(eye_rows, width), jnp.broadcast_to(j, (1, width)))
        for n in range(length // width):
            cols = slice(n * width, (n + 1) * width)
            bins = jnp.clip(cols_ref[:, cols] - here, -reach, reach) + reach
            hot = hot_rows(places_of(BIN_ROWS, width), bins)
            probs = [
                probs_ref[m, pl.ds(j, heads, stride=block + 1), :].astype(jnp.bfloat16)
                for m in range(n * width // LANES, (n + 1) * width // LANES)
            ]
            probs = jnp.concatenate(probs, axis=1)
            terms = jnp.concatenate([eye, probs, hot, right_ref[:, cols]], axis=0)
            mixed = jnp.dot(
                full_ref[: 3 * channels], terms, preferred_element_type=jnp.float32
            )
            centered = mixed[:channels]
            if own:
                pair = centered + jnp.dot(
                    low_ref[...],
                    jnp.concatenate([eye, probs, hot], axis=0),
                    preferred_element_type=jnp.float32,
                )
                rest[2][j, :, cols] = pair.astype(jnp.bfloat16)
                centered = pair - jnp.sum(pair, axis=0, keepdims=True) * (1.0 / channels)
            variance = jnp.sum(centered * centered, axis=0, keepdims=True) * (1.0 / channels)
            scale = lax.rsqrt(variance + 1e-05)
            value = mixed[channels : 2 * channels] * scale
            edge = value + value * jnp.tanh(mixed[2 * channels : 3 * channels] * scale)
            start = j * pitch
            for m in range(width // LANES):
                scratch[n * (width // LANES) + m, pl.ds(start, channels), :] = edge[
                    :, m * LANES : (m + 1) * LANES
                ]
            if own:
                gated = jnp.dot(
                    full_ref[3 * channels :], terms, preferred_element_type=jnp.float32
                )
                gate = 0.5 + 0.5 * jnp.tanh(gated * scale)
                rest[3][j, :, cols] = gate.astype(jnp.bfloat16)
        return carry

    lax.fori_loop(0, block, one_row, 0, unroll=min(16, block))
    half = channels // 2

    def one_channel(c, carry):
        for n in range(length // LANES):
            for side in range(2):
                rows_of = scratch[n, pl.ds(c + side * half, block, stride=pitch), :]
                rest[side][c, :, n * LANES : (n + 1) * LANES] = rows_of.astype(jnp.bfloat16)
        return carry

    lax.fori_loop(0, half, one_channel, 0, unroll=16)


def edges(own, row_index, start, maps, sides, fold, mix, low, right, cols, block, skip, rows):
    heads, _, length = maps.shape
    channels = right.shape[0]
    half = channels // 2
    out_shape = [jax.ShapeDtypeStruct((half, rows, length), jnp.bfloat16)] * 2
    out_specs = [pl.BlockSpec((half, block, length), lambda b, s, t: (0, b, 0))] * 2
    if own:
        out_shape += [jax.ShapeDtypeStruct((rows, channels, length), jnp.bfloat16)] * 2
        out_specs += [pl.BlockSpec((block, channels, length), lambda b, s, t: (b, 0, 0))] * 2
    first = skip // block
    whole = [pl.BlockSpec(a.shape, lambda b, s, t: (0, 0)) for a in (fold, mix, low, right, cols)]
    return pl.pallas_call(
        functools.partial(edges_kernel, own),
        out_shape=out_shape,
        grid_spec=pltpu.PrefetchScalarGridSpec(
            num_scalar_prefetch=2,
            grid=(rows // block,),
            in_specs=[
                pl.BlockSpec((heads, block, length), lambda b, s, t: (0, b + first, 0)),
                pl.BlockSpec((block, channels), lambda b, s, t: (lax.div(t[0], block) + b, 0)),
            ]
            + whole,
            out_specs=out_specs,
            scratch_shapes=[
                pltpu.VMEM((length // LANES, block * (channels + 1) + 7, LANES), jnp.float32),
                pltpu.VMEM(mix.shape, jnp.bfloat16),
                pltpu.VMEM((length // LANES, heads * (block + 1) + 7, LANES), jnp.float32),
            ],
        ),
        compiler_params=pltpu.CompilerParams(vmem_limit_bytes=VMEM_BYTES),
        cost_estimate=pl.CostEstimate(
            flops=2 * rows * length * channels * 800,
            bytes_accessed=2 * rows * length * channels,
            transcendentals=rows * length * channels,
        ),
        name="own_edges" if own else "right_edges",
    )(row_index, start, maps, sides, fold, mix, low, right, cols)


def products_kernel(keep_ref, arrive_ref, *refs):
    parts, (mine_ref, theirs_ref) = refs[:-2], refs[-2:]
    count, rows, _ = keep_ref.shape
    for c in range(count):
        lefts = jnp.concatenate([keep_ref[c], arrive_ref[c]], axis=0)
        for p, part in enumerate(parts):
            out = lax.dot_general(
                lefts, part[c], (((1,), (1,)), ((), ())), preferred_element_type=jnp.float32
            ).astype(jnp.bfloat16)
            mine_ref[p, c] = out[:rows]
            theirs_ref[p, c] = out[rows:]


def edge_products(keep, arrive, parts):
    half, rows, length = keep.shape
    each = parts[0].shape[1]
    count = 16 if half % 16 == 0 else 1
    out = jax.ShapeDtypeStruct((len(parts), half, rows, each), jnp.bfloat16)
    return pl.pallas_call(
        products_kernel,
        out_shape=[out] * 2,
        grid=(half // count,),
        in_specs=[pl.BlockSpec((count, rows, length), lambda b: (b, 0, 0))] * 2
        + [pl.BlockSpec((count, each, length), lambda b: (b, 0, 0))] * len(parts),
        out_specs=[pl.BlockSpec((len(parts), count, rows, each), lambda b: (0, b, 0, 0))] * 2,
        compiler_params=pltpu.CompilerParams(vmem_limit_bytes=VMEM_BYTES),
        cost_estimate=pl.CostEstimate(
            flops=4 * half * rows * len(parts) * each * length,
            bytes_accessed=2 * half * len(parts) * each * length,
            transcendentals=0,
        ),
        name="edge_products",
    )(keep, arrive, *parts)


def final_kernel(core, *refs):
    sources = refs[:4]
    pair_ref, gate_ref, gain_ref, w_ref, out_ref, scratch = refs[4:]
    half, block, width = sources[0].shape[1:]
    early = pl.program_id(1) < pl.num_programs(1) // 2

    def fill(n, ref):
        def one_channel(c, carry):
            scratch[n, pl.ds(c * (block + 1), block), :] = ref[0, c].astype(jnp.float32)
            return carry

        lax.fori_loop(0, half, one_channel, 0, unroll=8)

    for n in range(2):
        pl.when(early)(functools.partial(fill, n, sources[2 * n]))
        pl.when(jnp.logical_not(early))(functools.partial(fill, n, sources[2 * n + 1]))

    def one_row(i, carry):
        products = jnp.concatenate(
            [scratch[n, pl.ds(i, half, stride=block + 1), :] for n in range(2)], axis=0
        )
        center = jnp.mean(products, axis=0, keepdims=True)
        centered = products - center
        variance = jnp.mean(centered * centered, axis=0, keepdims=True)
        normed = (centered * lax.rsqrt(variance + 1e-05) * gain_ref[...]).astype(jnp.bfloat16)
        projected = jnp.dot(w_ref[...], normed, preferred_element_type=jnp.float32)
        total = pair_ref[i].astype(jnp.float32) + gate_ref[i].astype(jnp.float32) * projected
        out_ref[i] = total.T.astype(jnp.bfloat16)
        return carry

    lax.fori_loop(0, block, one_row, 0, unroll=16)


def finish(core, products, pair, gate, gain, weights, block):
    each, half, rows, width = products[0].shape
    pieces = 2 * each
    _, channels, length = pair.shape

    def column(u, core):
        side = u // each
        return (side + core[0] - 2 * side * core[0]) * each + u % each

    def early(b, u, s):
        return jnp.minimum(u, each - 1), 0, b, 0

    def late(b, u, s):
        return jnp.maximum(u - each, 0), 0, b, 0

    return pl.pallas_call(
        final_kernel,
        out_shape=jax.ShapeDtypeStruct((rows, length, channels), jnp.bfloat16),
        grid_spec=pltpu.PrefetchScalarGridSpec(
            num_scalar_prefetch=1,
            grid=(rows // block, pieces),
            in_specs=[
                pl.BlockSpec((1, half, block, width), early),
                pl.BlockSpec((1, half, block, width), late),
                pl.BlockSpec((1, half, block, width), early),
                pl.BlockSpec((1, half, block, width), late),
                pl.BlockSpec((block, channels, width), lambda b, u, s: (b, 0, column(u, s))),
                pl.BlockSpec((block, channels, width), lambda b, u, s: (b, 0, column(u, s))),
                pl.BlockSpec(gain.shape, lambda b, u, s: (0, 0)),
                pl.BlockSpec(weights.shape, lambda b, u, s: (0, 0)),
            ],
            out_specs=pl.BlockSpec((block, width, channels), lambda b, u, s: (b, column(u, s), 0)),
            scratch_shapes=[pltpu.VMEM((2, half * (block + 1) + 7, width), jnp.float32)],
        ),
        compiler_params=pltpu.CompilerParams(vmem_limit_bytes=VMEM_BYTES),
        name="finish",
    )(core, *products, pair, gate, gain, weights)


def per_device(
    across,
    hidden_in,
    ln_gain,
    w_qkv,
    w_out,
    residue_index,
    w_map,
    relpos_table,
    w_side,
    tri_gain,
    w_tri,
    w_tri_out,
):
    local_rows = hidden_in.shape[0]
    devices_mp = lax.axis_size("mp")
    me = lax.axis_index("mp")
    core = lax.rem(me, 2)
    length = local_rows * devices_mp
    local_heads = w_qkv.shape[2] // HD
    heads, channels = w_map.shape
    swap = [(d, d ^ 1) for d in range(devices_mp)]
    half_rows = length // 2
    each = half_rows // CHUNKS
    block = 16 if local_rows % 16 == 0 else local_rows
    r_block = 16 if each % 16 == 0 else each
    turn = -core * (channels // 2)
    cos_table, sin_table = rotary_tables(length, local_heads)
    operands = (
        hidden_in,
        ln_gain[None],
        w_out,
        w_side,
        tri_gain,
        w_tri,
        w_map,
        relpos_table,
    )
    maps, all_sides, att_rows, right_fold, right_mix, left_fold, left_mix, low = attend_and_gather(
        devices_mp,
        across,
        tuple(-(-b // 16) * 16 for b in (r_block, block)),
        operands,
        w_qkv,
        cos_table,
        sin_table,
    )
    maps = maps.reshape(heads, half_rows + local_rows, length)
    out_part, all_sides, att_rows = lax.optimization_barrier((w_out, all_sides, att_rows))
    full_out = lax.all_gather(out_part, "mp", axis=0)

    row_start = me * local_rows
    half_start = core * half_rows
    all_sides = all_sides.reshape(length, 2 * channels)
    right = all_sides[:, channels:].T

    cols = residue_index[None, :]

    first_row = half_start[None]
    left_keep, left_send, pair, gate = edges(
        True,
        residue_index,
        row_start[None],
        maps,
        all_sides,
        left_fold,
        left_mix,
        low,
        right,
        cols,
        block,
        half_rows,
        local_rows,
    )
    left_send, first_row = lax.optimization_barrier((left_send, first_row))
    left_arrive = lax.ppermute(left_send, "mp", swap)
    kept, arriving = [], []
    for n in range(CHUNKS):
        if n == 1:
            left_arrive, first_row = lax.optimization_barrier((left_arrive, first_row))
        keep, send = edges(
            False,
            residue_index,
            first_row + n * each,
            maps,
            all_sides,
            right_fold,
            right_mix,
            low,
            right,
            cols,
            r_block,
            n * each,
            each,
        )
        kept.append(keep)
        arriving.append(lax.ppermute(send, "mp", swap))
    mine_kept, theirs_kept = edge_products(left_keep, left_arrive, kept)
    theirs_kept = lax.ppermute(theirs_kept, "mp", swap)
    mine_other, theirs_other = edge_products(left_keep, left_arrive, arriving)
    theirs_other = lax.ppermute(theirs_other, "mp", swap)
    pair_out = finish(
        core[None],
        (mine_kept, mine_other, theirs_other, theirs_kept),
        pair,
        gate,
        jnp.broadcast_to(jnp.roll(tri_gain[1], turn)[:, None], (channels, each)),
        jnp.roll(w_tri_out, turn, axis=0).T,
        local_rows,
    )
    attended_rows = att_rows.transpose(1, 0, 2).reshape(local_rows, -1)
    mixed = jnp.dot(
        attended_rows, full_out.reshape(-1, full_out.shape[-1]), preferred_element_type=jnp.float32
    )
    hidden_out = (hidden_in.astype(jnp.float32) + mixed).astype(jnp.bfloat16)
    return (hidden_out, pair_out)


def solution(mesh):
    placed = (
        P(("groups", "mp"), None),
        P(),
        P(None, None, "mp"),
        P("mp", None),
        P("groups"),
        P(),
        P(),
        P(),
        P(),
        P(),
        P(),
    )
    chips = [d.coords for d in mesh.devices.reshape(-1, mesh.shape["mp"])[0][::2] if hasattr(d, "coords")]
    across = 1
    if len(chips) > 3 and sum(abs(p - q) for p, q in zip(chips[0], chips[2])) == 1:
        across = 2
    return jax.shard_map(
        functools.partial(per_device, across),
        mesh=mesh,
        in_specs=placed,
        out_specs=(P(("groups", "mp"), None), P(("groups", "mp"), None, None)),
        check_vma=False,
    )
```

```python
import functools

import jax
import jax.numpy as jnp
import numpy as np
from jax import lax
from jax.experimental import pallas as pl
from jax.experimental.pallas import tpu as pltpu
from jax.sharding import PartitionSpec as P

HD = 64
BINS = 65
BIN_ROWS = 80
LANES = 128
CHUNKS = 3
VMEM_BYTES = 60 * 1024 * 1024
MESH = pl.DeviceIdType.MESH
EXACT = lax.Precision.HIGHEST


def layer_norm(tensor, gain_vec, norm_axis):
    center = jnp.mean(tensor, axis=norm_axis, keepdims=True)
    centered = tensor - center
    variance = jnp.mean(centered * centered, axis=norm_axis, keepdims=True)
    return centered * lax.rsqrt(variance + 1e-05) * gain_vec


def rotary_tables(length, heads):
    powers = np.arange(0, HD, 2, dtype=np.float32) / np.float32(HD)
    inv_freq = np.float32(1.0) / np.power(np.float32(10000.0), powers)
    angles = np.arange(length, dtype=np.float32)[:, None] * inv_freq[None, :]
    cos, sin = np.cos(angles), np.sin(angles)
    return (
        jnp.asarray(np.tile(np.concatenate([cos, cos], axis=1), (1, heads)), jnp.float32),
        jnp.asarray(np.tile(np.concatenate([-sin, sin], axis=1), (1, heads)), jnp.float32),
    )


class Ring:
    def __init__(self, count, across, arrays, send, recv):
        self.arrays, self.send, self.recv = arrays, send, recv
        self.count, self.across, self.chips = count, across, count // 2
        self.ahead = self.chips // 2
        self.back = self.chips - 1 - self.ahead
        self.me = lax.axis_index("mp")
        self.core = lax.rem(self.me, 2)
        self.place = self.position(lax.div(self.me, 2))

    def position(self, chip):
        if self.across == 1:
            return chip
        z, y = lax.div(chip, 2), lax.rem(chip, 2)
        return z + y * (self.chips - 1 - 2 * z)

    def device(self, shift):
        place = lax.rem(self.place + self.chips + shift, self.chips)
        if self.across == 1:
            return 2 * place + self.core
        y = lax.div(place, self.chips // 2)
        z = place + y * (self.chips - 1 - 2 * place)
        return 2 * (2 * z + y) + self.core

    def twin(self):
        return self.me + 1 - 2 * self.core

    def copy(self, a, block, own, slot, target, part=None):
        src, out, axis = self.arrays[a]
        piece = ()
        if part is not None:
            size = src.shape[axis] // 2
            piece = (slice(None),) * axis + (pl.ds(part * size, size),)
        target_ref = out.at[(block,) + piece]
        source_ref = (src.at[piece] if piece else src) if own else target_ref
        return pltpu.make_async_remote_copy(
            src_ref=source_ref,
            dst_ref=target_ref,
            send_sem=self.send.at[a, slot],
            recv_sem=self.recv.at[a, slot],
            device_id={"mp": target},
            device_id_type=MESH,
        )

    def hop(self, a, way, step):
        slot = step if way > 0 else self.ahead + step
        part = None
        if self.back < self.ahead and step == self.back:
            part = 0 if way > 0 else 1
        block = self.device(-way * step)
        return self.copy(a, block, step == 0, slot, self.device(way), part)

    def hand(self, a, way, step):
        if way == 0:
            return self.copy(a, self.me, True, self.chips, self.twin())
        slot = self.chips + 1 + (step if way > 0 else self.ahead + step)
        return self.copy(a, self.device(-way * (step + 1)), False, slot, self.twin())

    def start(self):
        for a in range(len(self.arrays)):
            for way in (1, -1):
                self.hop(a, way, 0).start()
            self.hand(a, 0, 0).start()

    def steps(self):
        return self.ahead

    def ways(self, s):
        return [way for way, most in ((1, self.ahead), (-1, self.back)) if s < most]

    def step(self, s):
        for a in range(len(self.arrays)):
            for way in (1, -1):
                self.hop(a, way, s).wait_recv()
                if s + 1 < self.ahead:
                    self.hop(a, way, s + 1).start()
                if self.ways(s) == [1, -1]:
                    self.hand(a, way, s).start()
            if self.ways(s) == [1]:
                self.hand(a, 1, s).start()

    def take(self, way, s):
        for a in range(len(self.arrays)):
            self.hand(a, way, s).wait_recv()

    def finish(self):
        for a in range(len(self.arrays)):
            self.hand(a, 0, 0).wait_send()
            for s in range(self.ahead):
                for way in (1, -1):
                    self.hop(a, way, s).wait_send()
                for way in self.ways(s):
                    self.hand(a, way, s).wait_send()


def greet_all(count):
    me = lax.axis_index("mp")
    barrier = pltpu.get_barrier_semaphore()

    def greet(d, carry):
        pl.semaphore_signal(
            barrier, inc=1, device_id={"mp": lax.rem(me + d, count)}, device_id_type=MESH
        )
        return carry

    lax.fori_loop(1, count, greet, 0)
    pl.semaphore_wait(barrier, count - 1)


def gather_part(count, across, eyes, operands, outs, bins, normed, x_all, send, recv):
    x_ref, gain_ref, w_out_ref, w_side_ref, tri_gain_ref, tri_ref, map_ref, bins_ref = operands
    side_ref, own_ref, r_fold, r_mix, l_fold, l_mix, low_ref = outs
    me = lax.axis_index("mp")
    core = lax.rem(me, 2)
    greet_all(count)
    hidden = x_ref[...].astype(jnp.float32)
    normed[...] = layer_norm(hidden, gain_ref[...], -1).astype(jnp.bfloat16)
    x_all[me] = normed[...]
    ring = Ring(count, across, [(normed, x_all, 1)], send, recv)
    ring.start()

    channels = tri_ref.shape[1]
    for s in range(2):
        cols = slice(s * channels, (s + 1) * channels)
        own_ref[:, cols] = jnp.dot(
            x_ref[...], w_side_ref[s], preferred_element_type=jnp.float32
        )
        side_ref[:, cols] = jnp.dot(
            w_out_ref[...], w_side_ref[s], preferred_element_type=jnp.float32
        ).astype(jnp.bfloat16)
    ring.step(0)

    row = lax.broadcasted_iota(jnp.int32, (channels, channels), 0)
    column = lax.broadcasted_iota(jnp.int32, (channels, channels), 1)
    identity = jnp.where(row == column, 1.0, 0.0)
    center = identity - 1.0 / channels
    half = channels // 2
    length = x_ref.shape[0] * count
    maps = map_ref[...].astype(jnp.float32) * length
    bins[...] = jnp.zeros_like(bins)
    bins[: bins_ref.shape[0], :] = bins_ref[...]
    bins = bins[...]

    def gated(p, turned):
        weights = tri_ref[p].astype(jnp.float32).T * (0.5 * tri_gain_ref[0:1, :])
        if turned:
            other = jnp.concatenate([weights[half:], weights[:half]], axis=0)
            weights = jnp.where(core == 0, weights, other)
        return jnp.dot(weights, center, precision=EXACT, preferred_element_type=jnp.float32)

    def across_terms(fold, parts, eye_rows):
        rows = jnp.concatenate([jnp.zeros((eye_rows, channels), jnp.float32)] + parts, axis=0)
        return lax.dot_general(
            fold,
            rows,
            (((1,), (1,)), ((), ())),
            precision=EXACT,
            preferred_element_type=jnp.float32,
        ).astype(jnp.bfloat16)

    fold = jnp.concatenate([center, gated(2, True), gated(3, True)], axis=0)
    r_fold[...] = fold.astype(jnp.bfloat16)
    r_mix[...] = across_terms(fold, [maps, bins, identity], eyes[0])
    for s in range(1, ring.steps()):
        ring.step(s)
        if s == 1:
            fold = jnp.concatenate(
                [identity, gated(0, True), gated(1, True), gated(4, False)], axis=0
            )
            l_fold[...] = fold.astype(jnp.bfloat16)
            l_mix[...] = across_terms(fold, [maps, bins, identity], eyes[1])
            low = [v - v.astype(jnp.bfloat16).astype(jnp.float32) for v in (maps, bins)]
            low_ref[...] = across_terms(identity, low, eyes[1])
    ring.take(0, 0)
    for s in range(ring.steps()):
        for way in ring.ways(s):
            ring.take(way, s)
    ring.finish()


def attend_kernel(count, across, eyes, *refs):
    operands, refs = refs[:8], refs[8:]
    w_ref, cos_ref, sin_ref = refs[:3]
    maps_ref, out_ref, rows_ref = refs[3:6]
    outs, rest = refs[6:11], refs[11:]
    mix_ref, own_ref, normed, x_all = rest[:4]
    q_ref, k_ref, v_ref, q_all, k_all, parts, paired, landed, mine, stage = rest[4:14]
    att, first_send, first_recv, send, recv, pair_sems = rest[14:20]
    send_a, recv_a, send_b, recv_b, send_c, recv_c, stored, send_d, recv_d = rest[20:-1]
    gather_part(
        count,
        across,
        eyes,
        operands,
        (mix_ref, own_ref) + tuple(outs),
        rest[-1],
        normed,
        x_all,
        first_send,
        first_recv,
    )
    me = lax.axis_index("mp")
    core, chip, chips = lax.rem(me, 2), lax.div(me, 2), count // 2
    twin = me + 1 - 2 * core
    width, length = k_ref.shape
    rows = length // count
    half = count // 2
    turn = HD // 2
    heads = [slice(h * HD, (h + 1) * HD) for h in range(width // HD)]

    def rotated(tensor, where):
        turned = []
        for h in range(0, width, HD):
            turned += [tensor[:, h + turn : h + HD], tensor[:, h : h + turn]]
        turned = jnp.concatenate(turned, axis=1)
        return tensor * cos_ref[where, :] + turned * sin_ref[where, :]

    def softmax(scores):
        powers = jnp.exp(scores - jnp.max(scores, axis=-1, keepdims=True))
        probs = powers * (1.0 / jnp.sum(powers, axis=-1, keepdims=True))
        return probs.astype(jnp.bfloat16)

    span = length // 2
    for r in range(2):
        where = slice(r * span, (r + 1) * span)
        both = jnp.dot(
            x_all[r * half : (r + 1) * half].reshape(span, x_all.shape[2]),
            jnp.concatenate([w_ref[0], w_ref[1]], axis=1),
            preferred_element_type=jnp.float32,
        )
        queries = rotated(both[:, :width] * HD**-0.5, where).astype(jnp.bfloat16)
        k_ref[:, where] = rotated(both[:, width:], where).T.astype(jnp.bfloat16)
        for b in range(half):
            q_ref[r * half + b] = queries[b * rows : (b + 1) * rows]
    ring = Ring(count, across, [(k_ref, k_all, 0), (q_ref, q_all, 0)], send, recv)
    ring.start()
    v_ref[...] = jnp.dot(
        x_all[...].reshape(length, x_all.shape[2]), w_ref[2], preferred_element_type=jnp.float32
    ).astype(jnp.bfloat16)
    group = 4

    def one_group(g, carry):
        queries = q_ref[pl.ds(g * group, group)].reshape(group * rows, width)
        found = []
        for head in heads:
            scores = jnp.dot(queries[:, head], k_ref[head, :], preferred_element_type=jnp.float32)
            found.append(
                jnp.dot(softmax(scores), v_ref[:, head], preferred_element_type=jnp.float32)
            )
        found = jnp.concatenate(found, axis=1).astype(jnp.bfloat16)
        part = jnp.dot(found, mix_ref[...], preferred_element_type=jnp.float32)
        part = part.astype(jnp.bfloat16)
        for b in range(group):
            att[g * group + b] = found[b * rows : (b + 1) * rows]
            parts[b % 2, g * (group // 2) + b // 2] = part[b * rows : (b + 1) * rows]
        return carry

    lax.fori_loop(0, count // group, one_group, 0)

    pair = pltpu.make_async_remote_copy(
        src_ref=parts.at[1 - core],
        dst_ref=paired,
        send_sem=pair_sems.at[0],
        recv_sem=pair_sems.at[1],
        device_id={"mp": twin},
        device_id_type=MESH,
    )
    pair.start()

    def store(i, block):
        return pltpu.make_async_copy(stage.at[i % 2], maps_ref.at[block], stored.at[i % 2])

    def block_maps(i, queries_of, keys_of, block):
        slot = i % 2
        if i >= 2:
            store(i, block).wait()

        def fill(queries, start, size):
            queries = queries.reshape(size, width)
            for h, head in enumerate(heads):
                scores = jnp.dot(
                    queries[:, head], keys_of[head, :], preferred_element_type=jnp.float32
                )
                stage[slot, h, pl.ds(start, size), :] = softmax(scores)

        def one_pair(g, carry):
            start = pl.multiple_of(g * 2 * rows, 16)
            fill(queries_of[pl.ds(core * half + 2 * g, 2)], start, 2 * rows)
            return carry

        lax.fori_loop(0, half // 2, one_pair, 0)
        fill(queries_of[pl.ds(me, 1)], half * rows, rows)
        store(i, block).start()

    block_maps(0, q_ref, k_ref, me)

    def scatter(d):
        target = lax.rem(chip + d, chips)
        return pltpu.make_async_remote_copy(
            src_ref=paired.at[target],
            dst_ref=landed.at[d],
            send_sem=send_a.at[d],
            recv_sem=recv_a.at[d],
            device_id={"mp": 2 * target + core},
            device_id_type=MESH,
        )

    def spread(d):
        return pltpu.make_async_remote_copy(
            src_ref=mine,
            dst_ref=out_ref.at[me],
            send_sem=send_b.at[d],
            recv_sem=recv_b.at[d],
            device_id={"mp": 2 * lax.rem(chip + d, chips) + core},
            device_id_type=MESH,
        )

    def hand_side(d):
        source = 2 * lax.rem(chip + chips - d, chips) + core
        return pltpu.make_async_remote_copy(
            src_ref=out_ref.at[source],
            dst_ref=out_ref.at[source],
            send_sem=send_c.at[d],
            recv_sem=recv_c.at[d],
            device_id={"mp": twin},
            device_id_type=MESH,
        )

    def each(step, first=1, last=chips):
        def run(d, carry):
            step(d)
            return carry

        lax.fori_loop(first, last, run, 0)

    def carry_rows(d):
        target = lax.rem(me + d, count)
        return pltpu.make_async_remote_copy(
            src_ref=att.at[target],
            dst_ref=rows_ref.at[me],
            send_sem=send_d.at[d],
            recv_sem=recv_d.at[d],
            device_id={"mp": target},
            device_id_type=MESH,
        )

    pair.wait_recv()

    def join(d):
        both = paired[d].astype(jnp.float32) + parts[core, d].astype(jnp.float32)
        paired[d] = both.astype(jnp.bfloat16)

    each(join, 0)
    each(lambda d: scatter(d).start())
    ring.take(0, 0)
    block_maps(1, q_all.at[twin], k_all.at[twin], twin)
    done = 2
    for s in range(ring.steps()):
        ring.step(s)
        if s == 0:

            def add(d, total):
                scatter(d).wait_recv()
                return total + landed[d].astype(jnp.float32)

            total = own_ref[...] + paired[chip].astype(jnp.float32)
            total = lax.fori_loop(1, chips, add, total).astype(jnp.bfloat16)
            mine[...] = total
            out_ref[me] = total
            each(lambda d: spread(d).start())
            hand_side(0).start()
        if s == min(1, ring.steps() - 1):

            def forward(d):
                spread(d).wait_recv()
                hand_side(d).start()

            each(forward)
        if s == ring.steps() - 1:
            rows_ref[me] = att[me]
            each(lambda d: carry_rows(d).start(), last=count)
        for way in ring.ways(s):
            block = ring.device(-way * (s + 1))
            block_maps(done, q_all.at[block], k_all.at[block], block)
            done += 1
        for way in ring.ways(s):
            block = ring.device(-way * (s + 1)) + 1 - 2 * core
            ring.take(way, s)
            block_maps(done, q_all.at[block], k_all.at[block], block)
            done += 1
    ring.finish()
    store(done - 2, me).wait()
    store(done - 1, me).wait()
    pair.wait_send()
    each(lambda d: hand_side(d).wait_recv(), 0)
    each(lambda d: hand_side(d).wait_send(), 0)
    each(lambda d: scatter(d).wait_send())
    each(lambda d: spread(d).wait_send())
    each(lambda d: carry_rows(d).wait_recv(), last=count)
    each(lambda d: carry_rows(d).wait_send(), last=count)


def attend_and_gather(count, across, eyes, operands, weights, cos_table, sin_table):
    block, _, w_out, w_side, _, w_tri, w_map, bins = operands
    channels = w_tri.shape[1]
    length, width = cos_table.shape
    rows = block.shape[0]
    terms = [e + w_map.shape[0] + BIN_ROWS for e in eyes]
    vmem = pl.BlockSpec(memory_space=pltpu.VMEM)
    queries, keys, own = (count, rows, width), (width, length), (rows, 2 * channels)
    sides = (count // 2,) + own
    piece = (width // HD, length // 2 + rows, length)
    shapes = [
        (count,) + piece,
        (count,) + own,
        queries,
        (3 * channels, channels),
        (3 * channels, terms[0] + channels),
        (4 * channels, channels),
        (4 * channels, terms[1] + channels),
        (channels, terms[1]),
    ]
    scratch = [
        block.shape,
        (count,) + block.shape,
        queries,
        keys,
        (length, width),
        (count,) + queries,
        (count,) + keys,
        (2,) + sides,
        sides,
        sides,
        own,
        (2,) + piece,
        queries,
    ]
    return pl.pallas_call(
        functools.partial(attend_kernel, count, across, eyes),
        out_shape=[jax.ShapeDtypeStruct(shape, jnp.bfloat16) for shape in shapes],
        in_specs=[vmem] * (len(operands) + 3),
        out_specs=[pl.BlockSpec(memory_space=pl.ANY)] + [vmem] * 7,
        scratch_shapes=[
            pltpu.VMEM((w_out.shape[0], 2 * channels), jnp.bfloat16),
            pltpu.VMEM(own, jnp.float32),
        ]
        + [pltpu.VMEM(shape, jnp.bfloat16) for shape in scratch]
        + [pltpu.SemaphoreType.DMA((1, count))] * 2
        + [pltpu.SemaphoreType.DMA((2, count))] * 2
        + [pltpu.SemaphoreType.DMA((2,))]
        + [pltpu.SemaphoreType.DMA((count // 2,))] * 6
        + [pltpu.SemaphoreType.DMA((2,))]
        + [pltpu.SemaphoreType.DMA((count,))] * 2
        + [pltpu.VMEM((BIN_ROWS, channels), jnp.float32)],
        compiler_params=pltpu.CompilerParams(
            collective_id=0, has_side_effects=True, vmem_limit_bytes=VMEM_BYTES
        ),
        name="attend_and_gather",
    )(*operands, weights, cos_table, sin_table)


def places_of(rows, width):
    places = lax.broadcasted_iota(jnp.int32, (rows, width), 0)
    return places.astype(jnp.float32).astype(jnp.bfloat16)


def hot_rows(places, index):
    index = index.astype(jnp.float32).astype(jnp.bfloat16)
    return jnp.where(places == index, jnp.ones((), jnp.bfloat16), jnp.zeros((), jnp.bfloat16))


def edges_kernel(
    own, row_index, start_ref, maps_ref, left_ref, fold_ref, mix_ref, low_ref, right_ref, cols_ref, *rest
):
    scratch, full_ref, probs_ref = rest[-3:]
    heads, block, length = maps_ref.shape
    channels = right_ref.shape[0]
    eye_rows = mix_ref.shape[1] - channels - heads - BIN_ROWS
    pitch = channels + 1
    width = 2 * LANES
    reach = (BINS - 1) // 2
    first = start_ref[0] + pl.program_id(0) * block

    lefts = jnp.concatenate(
        [left_ref[...], jnp.zeros((LANES - block, channels), jnp.bfloat16)], axis=0
    )
    folded = lax.dot_general(
        fold_ref[...], lefts, (((1,), (1,)), ((), ())), preferred_element_type=jnp.float32
    )
    full_ref[:, :LANES] = (folded + mix_ref[:, :LANES].astype(jnp.float32)).astype(jnp.bfloat16)
    full_ref[:, LANES:] = mix_ref[:, LANES:]

    def one_head(h, carry):
        for n in range(length // LANES):
            probs_ref[n, pl.ds(h * (block + 1), block), :] = maps_ref[
                h, :, n * LANES : (n + 1) * LANES
            ].astype(jnp.float32)
        return carry

    lax.fori_loop(0, heads, one_head, 0, unroll=8)

    def one_row(j, carry):
        here = row_index[first + j]
        eye = hot_rows(places_of(eye_rows, width), jnp.broadcast_to(j, (1, width)))
        for n in range(length // width):
            cols = slice(n * width, (n + 1) * width)
            bins = jnp.clip(cols_ref[:, cols] - here, -reach, reach) + reach
            hot = hot_rows(places_of(BIN_ROWS, width), bins)
            probs = [
                probs_ref[m, pl.ds(j, heads, stride=block + 1), :].astype(jnp.bfloat16)
                for m in range(n * width // LANES, (n + 1) * width // LANES)
            ]
            probs = jnp.concatenate(probs, axis=1)
            terms = jnp.concatenate([eye, probs, hot, right_ref[:, cols]], axis=0)
            mixed = jnp.dot(
                full_ref[: 3 * channels], terms, preferred_element_type=jnp.float32
            )
            centered = mixed[:channels]
            if own:
                pair = centered + jnp.dot(
                    low_ref[...],
                    jnp.concatenate([eye, probs, hot], axis=0),
                    preferred_element_type=jnp.float32,
                )
                rest[2][j, :, cols] = pair.astype(jnp.bfloat16)
                centered = pair - jnp.sum(pair, axis=0, keepdims=True) * (1.0 / channels)
            variance = jnp.sum(centered * centered, axis=0, keepdims=True) * (1.0 / channels)
            scale = lax.rsqrt(variance + 1e-05)
            value = mixed[channels : 2 * channels] * scale
            edge = value + value * jnp.tanh(mixed[2 * channels : 3 * channels] * scale)
            start = j * pitch
            for m in range(width // LANES):
                scratch[n * (width // LANES) + m, pl.ds(start, channels), :] = edge[
                    :, m * LANES : (m + 1) * LANES
                ]
            if own:
                gated = jnp.dot(
                    full_ref[3 * channels :], terms, preferred_element_type=jnp.float32
                )
                gate = 0.5 + 0.5 * jnp.tanh(gated * scale)
                rest[3][j, :, cols] = gate.astype(jnp.bfloat16)
        return carry

    lax.fori_loop(0, block, one_row, 0, unroll=min(16, block))
    half = channels // 2

    def one_channel(c, carry):
        for n in range(length // LANES):
            for side in range(2):
                rows_of = scratch[n, pl.ds(c + side * half, block, stride=pitch), :]
                rest[side][c, :, n * LANES : (n + 1) * LANES] = rows_of.astype(jnp.bfloat16)
        return carry

    lax.fori_loop(0, half, one_channel, 0, unroll=16)


def edges(own, row_index, start, maps, sides, fold, mix, low, right, cols, block, skip, rows):
    heads, _, length = maps.shape
    channels = right.shape[0]
    half = channels // 2
    out_shape = [jax.ShapeDtypeStruct((half, rows, length), jnp.bfloat16)] * 2
    out_specs = [pl.BlockSpec((half, block, length), lambda b, s, t: (0, b, 0))] * 2
    if own:
        out_shape += [jax.ShapeDtypeStruct((rows, channels, length), jnp.bfloat16)] * 2
        out_specs += [pl.BlockSpec((block, channels, length), lambda b, s, t: (b, 0, 0))] * 2
    first = skip // block
    whole = [pl.BlockSpec(a.shape, lambda b, s, t: (0, 0)) for a in (fold, mix, low, right, cols)]
    return pl.pallas_call(
        functools.partial(edges_kernel, own),
        out_shape=out_shape,
        grid_spec=pltpu.PrefetchScalarGridSpec(
            num_scalar_prefetch=2,
            grid=(rows // block,),
            in_specs=[
                pl.BlockSpec((heads, block, length), lambda b, s, t: (0, b + first, 0)),
                pl.BlockSpec((block, channels), lambda b, s, t: (lax.div(t[0], block) + b, 0)),
            ]
            + whole,
            out_specs=out_specs,
            scratch_shapes=[
                pltpu.VMEM((length // LANES, block * (channels + 1) + 7, LANES), jnp.float32),
                pltpu.VMEM(mix.shape, jnp.bfloat16),
                pltpu.VMEM((length // LANES, heads * (block + 1) + 7, LANES), jnp.float32),
            ],
        ),
        compiler_params=pltpu.CompilerParams(vmem_limit_bytes=VMEM_BYTES),
        cost_estimate=pl.CostEstimate(
            flops=2 * rows * length * channels * 800,
            bytes_accessed=2 * rows * length * channels,
            transcendentals=rows * length * channels,
        ),
        name="own_edges" if own else "right_edges",
    )(row_index, start, maps, sides, fold, mix, low, right, cols)


def products_kernel(keep_ref, arrive_ref, *refs):
    parts, (mine_ref, theirs_ref) = refs[:-2], refs[-2:]
    count, rows, _ = keep_ref.shape
    for c in range(count):
        lefts = jnp.concatenate([keep_ref[c], arrive_ref[c]], axis=0)
        for p, part in enumerate(parts):
            out = lax.dot_general(
                lefts, part[c], (((1,), (1,)), ((), ())), preferred_element_type=jnp.float32
            ).astype(jnp.bfloat16)
            mine_ref[p, c] = out[:rows]
            theirs_ref[p, c] = out[rows:]


def edge_products(keep, arrive, parts):
    half, rows, length = keep.shape
    each = parts[0].shape[1]
    count = 16 if half % 16 == 0 else 1
    out = jax.ShapeDtypeStruct((len(parts), half, rows, each), jnp.bfloat16)
    return pl.pallas_call(
        products_kernel,
        out_shape=[out] * 2,
        grid=(half // count,),
        in_specs=[pl.BlockSpec((count, rows, length), lambda b: (b, 0, 0))] * 2
        + [pl.BlockSpec((count, each, length), lambda b: (b, 0, 0))] * len(parts),
        out_specs=[pl.BlockSpec((len(parts), count, rows, each), lambda b: (0, b, 0, 0))] * 2,
        compiler_params=pltpu.CompilerParams(vmem_limit_bytes=VMEM_BYTES),
        cost_estimate=pl.CostEstimate(
            flops=4 * half * rows * len(parts) * each * length,
            bytes_accessed=2 * half * len(parts) * each * length,
            transcendentals=0,
        ),
        name="edge_products",
    )(keep, arrive, *parts)


def final_kernel(core, *refs):
    sources = refs[:4]
    pair_ref, gate_ref, w_ref, out_ref, scratch = refs[4:]
    half, block, width = sources[0].shape[1:]
    early = pl.program_id(1) < pl.num_programs(1) // 2

    def fill(n, ref):
        def one_channel(c, carry):
            scratch[n, pl.ds(c * (block + 1), block), :] = ref[0, c].astype(jnp.float32)
            return carry

        lax.fori_loop(0, half, one_channel, 0, unroll=8)

    for n in range(2):
        pl.when(early)(functools.partial(fill, n, sources[2 * n]))
        pl.when(jnp.logical_not(early))(functools.partial(fill, n, sources[2 * n + 1]))

    def one_row(i, carry):
        products = jnp.concatenate(
            [scratch[n, pl.ds(i, half, stride=block + 1), :] for n in range(2)], axis=0
        )
        center = jnp.mean(products, axis=0, keepdims=True)
        centered = products - center
        variance = jnp.mean(centered * centered, axis=0, keepdims=True)
        projected = jnp.dot(
            w_ref[...], centered.astype(jnp.bfloat16), preferred_element_type=jnp.float32
        ) * lax.rsqrt(variance + 1e-05)
        total = pair_ref[i].astype(jnp.float32) + gate_ref[i].astype(jnp.float32) * projected
        out_ref[i] = total.T.astype(jnp.bfloat16)
        return carry

    lax.fori_loop(0, block, one_row, 0, unroll=16)


def finish(core, products, pair, gate, weights, block):
    each, half, rows, width = products[0].shape
    pieces = 2 * each
    _, channels, length = pair.shape

    def column(u, core):
        side = u // each
        return (side + core[0] - 2 * side * core[0]) * each + u % each

    def early(b, u, s):
        return jnp.minimum(u, each - 1), 0, b, 0

    def late(b, u, s):
        return jnp.maximum(u - each, 0), 0, b, 0

    return pl.pallas_call(
        final_kernel,
        out_shape=jax.ShapeDtypeStruct((rows, length, channels), jnp.bfloat16),
        grid_spec=pltpu.PrefetchScalarGridSpec(
            num_scalar_prefetch=1,
            grid=(rows // block, pieces),
            in_specs=[
                pl.BlockSpec((1, half, block, width), early),
                pl.BlockSpec((1, half, block, width), late),
                pl.BlockSpec((1, half, block, width), early),
                pl.BlockSpec((1, half, block, width), late),
                pl.BlockSpec((block, channels, width), lambda b, u, s: (b, 0, column(u, s))),
                pl.BlockSpec((block, channels, width), lambda b, u, s: (b, 0, column(u, s))),
                pl.BlockSpec(weights.shape, lambda b, u, s: (0, 0)),
            ],
            out_specs=pl.BlockSpec((block, width, channels), lambda b, u, s: (b, column(u, s), 0)),
            scratch_shapes=[pltpu.VMEM((2, half * (block + 1) + 7, width), jnp.float32)],
        ),
        compiler_params=pltpu.CompilerParams(vmem_limit_bytes=VMEM_BYTES),
        name="finish",
    )(core, *products, pair, gate, weights)


def per_device(
    across,
    hidden_in,
    ln_gain,
    w_qkv,
    w_out,
    residue_index,
    w_map,
    relpos_table,
    w_side,
    tri_gain,
    w_tri,
    w_tri_out,
):
    local_rows = hidden_in.shape[0]
    devices_mp = lax.axis_size("mp")
    me = lax.axis_index("mp")
    core = lax.rem(me, 2)
    length = local_rows * devices_mp
    local_heads = w_qkv.shape[2] // HD
    heads, channels = w_map.shape
    swap = [(d, d ^ 1) for d in range(devices_mp)]
    half_rows = length // 2
    each = half_rows // CHUNKS
    block = 16 if local_rows % 16 == 0 else local_rows
    r_block = 16 if each % 16 == 0 else each
    turn = -core * (channels // 2)
    cos_table, sin_table = rotary_tables(length, local_heads)
    operands = (
        hidden_in,
        ln_gain[None],
        w_out,
        w_side,
        tri_gain,
        w_tri,
        w_map,
        relpos_table,
    )
    maps, all_sides, att_rows, right_fold, right_mix, left_fold, left_mix, low = attend_and_gather(
        devices_mp,
        across,
        tuple(-(-b // 16) * 16 for b in (r_block, block)),
        operands,
        w_qkv,
        cos_table,
        sin_table,
    )
    maps = maps.reshape(heads, half_rows + local_rows, length)
    out_part, all_sides, att_rows = lax.optimization_barrier((w_out, all_sides, att_rows))
    full_out = lax.all_gather(out_part, "mp", axis=0)

    row_start = me * local_rows
    half_start = core * half_rows
    all_sides = all_sides.reshape(length, 2 * channels)
    right = all_sides[:, channels:].T

    cols = residue_index[None, :]

    first_row = half_start[None]
    left_keep, left_send, pair, gate = edges(
        True,
        residue_index,
        row_start[None],
        maps,
        all_sides,
        left_fold,
        left_mix,
        low,
        right,
        cols,
        block,
        half_rows,
        local_rows,
    )
    left_send, first_row = lax.optimization_barrier((left_send, first_row))
    left_arrive = lax.ppermute(left_send, "mp", swap)
    kept, arriving = [], []
    for n in range(CHUNKS):
        if n == 1:
            left_arrive, first_row = lax.optimization_barrier((left_arrive, first_row))
        keep, send = edges(
            False,
            residue_index,
            first_row + n * each,
            maps,
            all_sides,
            right_fold,
            right_mix,
            low,
            right,
            cols,
            r_block,
            n * each,
            each,
        )
        kept.append(keep)
        arriving.append(lax.ppermute(send, "mp", swap))
    mine_kept, theirs_kept = edge_products(left_keep, left_arrive, kept)
    theirs_kept = lax.ppermute(theirs_kept, "mp", swap)
    mine_other, theirs_other = edge_products(left_keep, left_arrive, arriving)
    theirs_other = lax.ppermute(theirs_other, "mp", swap)
    pair_out = finish(
        core[None],
        (mine_kept, mine_other, theirs_other, theirs_kept),
        pair,
        gate,
        jnp.roll(w_tri_out.astype(jnp.float32) * tri_gain[1][:, None], turn, axis=0)
        .T.astype(jnp.bfloat16),
        local_rows,
    )
    attended_rows = att_rows.transpose(1, 0, 2).reshape(local_rows, -1)
    mixed = jnp.dot(
        attended_rows, full_out.reshape(-1, full_out.shape[-1]), preferred_element_type=jnp.float32
    )
    hidden_out = (hidden_in.astype(jnp.float32) + mixed).astype(jnp.bfloat16)
    return (hidden_out, pair_out)


def solution(mesh):
    placed = (
        P(("groups", "mp"), None),
        P(),
        P(None, None, "mp"),
        P("mp", None),
        P("groups"),
        P(),
        P(),
        P(),
        P(),
        P(),
        P(),
    )
    chips = [d.coords for d in mesh.devices.reshape(-1, mesh.shape["mp"])[0][::2] if hasattr(d, "coords")]
    across = 1
    if len(chips) > 3 and sum(abs(p - q) for p, q in zip(chips[0], chips[2])) == 1:
        across = 2
    return jax.shard_map(
        functools.partial(per_device, across),
        mesh=mesh,
        in_specs=placed,
        out_specs=(P(("groups", "mp"), None), P(("groups", "mp"), None, None)),
        check_vma=False,
    )
```
